32 devices in a mesh: grp: 16 (over z, y, x), row: 2 (over core).
Axes of the slice: x: 2, y: 2, z: 4, core: 2. Of those that a mesh axis runs over, the one named last changes fastest.
Arguments:
- image_rows: bfloat16 [64, 16, 16, 512], P('grp', 'row'), may hold values from -6 to 6
- grad_out: bfloat16 [64, 16, 16, 512], P(('grp', 'row')), may hold values from -6 to 6
- code_ids: int32 [16384], P(('grp', 'row')), may hold values from 0 to 1023
- dead_flags: int32 [1024], replicated, may hold values from 0 to 1, as said below
- replace_ids: int32 [1024], replicated, may hold values from 0 to 16383
- latents: bfloat16 [16384, 256], P(('grp', 'row')), may hold values from -6 to 6
- codebook: float32 [1024, 256], P(('grp', 'row')), may hold values from -6 to 6
- norm1_gain: bfloat16 [512], replicated, may hold values from 0.5 to 1.5
- norm1_bias: bfloat16 [512], replicated, may hold values from -3 to 3
- conv1_kernel: bfloat16 [3, 3, 512, 512], replicated, may hold values from -0.09375 to 0.09375
- conv1_bias: bfloat16 [512], replicated, may hold values from -3 to 3
- norm2_gain: bfloat16 [512], replicated, may hold values from 0.5 to 1.5
- norm2_bias: bfloat16 [512], replicated, may hold values from -3 to 3
- conv2_kernel: bfloat16 [3, 3, 512, 512], replicated, may hold values from -0.09375 to 0.09375
- conv2_bias: bfloat16 [512], replicated, may hold values from -3 to 3
- norm3_gain: bfloat16 [512], replicated, may hold values from 0.5 to 1.5
- norm3_bias: bfloat16 [512], replicated, may hold values from -3 to 3
- query_weight: bfloat16 [512, 512], replicated, may hold values from -0.25 to 0.25
- query_bias: bfloat16 [512], replicated, may hold values from -3 to 3
- key_weight: bfloat16 [512, 512], replicated, may hold values from -0.25 to 0.25
- value_weight: bfloat16 [512, 512], replicated, may hold values from -0.25 to 0.25
- value_bias: bfloat16 [512], replicated, may hold values from -3 to 3
- out_weight: bfloat16 [512, 512], replicated, may hold values from -2 to 2
- out_bias: bfloat16 [512], replicated, may hold values from -3 to 3
Outputs:
- block_out: bfloat16 [64, 16, 16, 512], P(('grp', 'row'))
- input_grad: bfloat16 [64, 16, 16, 512], P('grp', 'row')
- norm1_gain_grad: float32 [512], replicated
- norm1_bias_grad: float32 [512], replicated
- conv1_kernel_grad: float32 [3, 3, 512, 512], replicated
- conv1_bias_grad: float32 [512], replicated
- norm2_gain_grad: float32 [512], replicated
- norm2_bias_grad: float32 [512], replicated
- conv2_kernel_grad: float32 [3, 3, 512, 512], replicated
- conv2_bias_grad: float32 [512], replicated
- norm3_gain_grad: float32 [512], replicated
- norm3_bias_grad: float32 [512], replicated
- query_weight_grad: float32 [512, 512], replicated
- query_bias_grad: float32 [512], replicated
- key_weight_grad: float32 [512, 512], replicated
- value_weight_grad: float32 [512, 512], replicated
- value_bias_grad: float32 [512], replicated
- out_weight_grad: float32 [512, 512], replicated
- out_bias_grad: float32 [512], replicated
- new_codebook: float32 [1024, 256], P(('grp', 'row'))
- usage: int32 [1024], replicated
- perplexity: float32 [], replicated
The draws below stay inside these ranges and needn't reach their ends.
Inputs may be any that keep to these rules, and one draw needn't show every extreme that they name: `code_ids`: a code index. `dead_flags`: exactly 256 entries are 1, the others 0. `replace_ids`: a row of latents.
All inputs are finite; a program needn't handle non-finite values.
Results may differ from the reference program's by a relative error of at most 0.014.
The reference program's roundings to bfloat16 on the way count: a program that leaves them out, or rounds other values in their place, can miss the bound.
Values may be sent and summed in bfloat16 or wider, within the bound.
No kernel may reach another device: no remote copies, remote signals or barrier semaphores. Data moves between devices by JAX's collectives and lax.ppermute only.
A program may use at most 128 MiB of HBM per device.

```python
import math
import jax
import jax.numpy as jnp
import numpy as np
from jax import lax

C = 512
G = 32
CODES = 1024
ZD = 256
SIDE = 16
DEAD = 256
IMAGES = 64
PIXELS = 16384


def draw_dead_flags(key, part):
    order = jax.random.permutation(jax.random.fold_in(key, 17), CODES)
    return (order < DEAD).astype(jnp.int32)


def place_ends(drawn, stream_key, low, top_value):
    place = [jax.random.randint(jax.random.fold_in(stream_key, axis), (), 0, length) for axis, length in enumerate(drawn.shape)]
    main_axis = drawn.shape.index(max(drawn.shape))
    beside = place[:main_axis] + [(place[main_axis] + 1) % drawn.shape[main_axis]] + place[main_axis + 1:]
    return drawn.at[tuple(place)].set(low).at[tuple(beside)].set(top_value)


def steps_of(own_key, extent, pieces, smallest, high):
    level, own = 1.0, jax.random.fold_in(own_key, 6)
    for position, blocks in pieces:
        heights = jnp.exp(jax.random.uniform(jax.random.fold_in(own, position), (blocks,), jnp.float32, smallest / len(pieces), high / len(pieces)))
        level = level * jnp.repeat(heights, extent[position] // blocks).reshape([-1 if axis == position else 1 for axis in range(len(extent))])
    return level


def cumulative_ranks(count, lean):
    weights = [(1 << 20) // math.isqrt(grade ** lean) + 1 for grade in range(1, count + 1)]
    scale = 1 + sum(weights) // (1 << 30)
    return np.cumsum(np.array([max(1, weight // scale) for weight in weights]))


def skewed_ids(stream_key, extent, number_of, lean):
    grid = cumulative_ranks(number_of, lean)
    ticket = jax.random.randint(jax.random.fold_in(stream_key, 1), extent, 0, int(grid[number_of - 1]))
    standing = jnp.searchsorted(jnp.asarray(grid, jnp.int32), ticket, side="right")
    return jax.random.permutation(jax.random.fold_in(stream_key, 2), number_of)[standing].astype(jnp.int32)


def scatter_about(key, extent, deviation, limit, shards=(), dtype=jnp.bfloat16):
    entries = jax.random.normal(key, extent, jnp.float32) * deviation
    if len(shards) > 0:
        entries = steps_of(key, extent, shards, -0.22, 0.18) * entries
    return jnp.clip(entries, min=-limit, max=limit).astype(dtype)


def setup_inputs(seed: int = 0) -> dict:
    streams_of = jax.random.split(jax.random.key(seed), 25)
    image_rows = scatter_about(streams_of[0], (IMAGES, SIDE, SIDE, C), 1.0, 6.0, ((0, 16), (1, 2)))
    grad_out = scatter_about(streams_of[1], (IMAGES, SIDE, SIDE, C), 1.0, 6.0, ((0, 32),))
    code_ids = place_ends(skewed_ids(streams_of[2], (PIXELS,), CODES, 2), jax.random.fold_in(streams_of[2], 3), 0, CODES - 1).astype(jnp.int32)
    dead_flags = draw_dead_flags(jax.random.fold_in(streams_of[24], 71), 0)
    replace_ids = place_ends(jax.random.randint(streams_of[4], (CODES,), 0, PIXELS), jax.random.fold_in(streams_of[4], 1), 0, PIXELS - 1).astype(jnp.int32)
    latents = scatter_about(streams_of[5], (PIXELS, ZD), 1.0, 6.0, ((0, 32),))
    codebook = scatter_about(streams_of[6], (CODES, ZD), 1.0, 6.0, ((0, 32),), jnp.float32)
    norm1_gain = jnp.clip(1.0 + 0.1 * jax.random.normal(streams_of[7], (C,), jnp.float32), 0.5, 1.5).astype(jnp.bfloat16)
    norm1_bias = scatter_about(streams_of[8], (C,), 0.5, 3.0)
    conv1_kernel = scatter_about(streams_of[9], (3, 3, C, C), (9 * C) ** -0.5, 0.09375)
    conv1_bias = scatter_about(streams_of[10], (C,), 0.5, 3.0)
    norm2_gain = jnp.clip(1.0 + 0.1 * jax.random.normal(streams_of[11], (C,), jnp.float32), 0.5, 1.5).astype(jnp.bfloat16)
    norm2_bias = scatter_about(streams_of[12], (C,), 0.5, 3.0)
    conv2_kernel = scatter_about(streams_of[13], (3, 3, C, C), (9 * C) ** -0.5, 0.09375)
    conv2_bias = scatter_about(streams_of[14], (C,), 0.5, 3.0)
    norm3_gain = jnp.clip(1.0 + 0.1 * jax.random.normal(streams_of[15], (C,), jnp.float32), 0.5, 1.5).astype(jnp.bfloat16)
    norm3_bias = scatter_about(streams_of[16], (C,), 0.5, 3.0)
    query_weight = scatter_about(streams_of[17], (C, C), C ** -0.5, 0.25)
    query_bias = scatter_about(streams_of[18], (C,), 0.5, 3.0)
    key_weight = scatter_about(streams_of[19], (C, C), C ** -0.5, 0.25)
    value_weight = scatter_about(streams_of[20], (C, C), C ** -0.5, 0.25)
    value_bias = scatter_about(streams_of[21], (C,), 0.5, 3.0)
    out_weight = scatter_about(streams_of[22], (C, C), (C // 64) ** -0.5, 2.0)
    out_bias = scatter_about(streams_of[23], (C,), 0.5, 3.0)
    return {"image_rows": image_rows, "grad_out": grad_out, "code_ids": code_ids, "dead_flags": dead_flags, "replace_ids": replace_ids, "latents": latents, "codebook": codebook, "norm1_gain": norm1_gain, "norm1_bias": norm1_bias, "conv1_kernel": conv1_kernel, "conv1_bias": conv1_bias, "norm2_gain": norm2_gain, "norm2_bias": norm2_bias, "conv2_kernel": conv2_kernel, "conv2_bias": conv2_bias, "norm3_gain": norm3_gain, "norm3_bias": norm3_bias, "query_weight": query_weight, "query_bias": query_bias, "key_weight": key_weight, "value_weight": value_weight, "value_bias": value_bias, "out_weight": out_weight, "out_bias": out_bias}


@jax.custom_vjp
def low(v):
    return lax.optimization_barrier(v.astype(jnp.bfloat16)).astype(jnp.float32)

@jax.custom_vjp
def low_back(v):
    return v

def low_keep(v):
    return (low(v), None)

def low_pass(kept, grad):
    return (grad,)

def back_keep(v):
    return (v, None)

def back_low(kept, grad):
    return (low(grad),)
low.defvjp(low_keep, low_pass)
low_back.defvjp(back_keep, back_low)
highest = lax.Precision.HIGHEST
epsilon = 1e-06

def group_norm(source, scaling, offsets):
    images, height, across, channels = source.shape
    grouped = source.reshape(images, height * across, G, channels // G)
    middle = lax.optimization_barrier(jnp.mean(grouped, axis=(1, 3), keepdims=True))
    centered = grouped - middle
    spread = lax.optimization_barrier(jnp.mean(centered * centered, axis=(1, 3), keepdims=True))
    normed = (centered * lax.rsqrt(spread + epsilon)).reshape(images, height, across, channels)
    return normed * scaling + offsets

def convolve(source, kernel):
    return lax.conv_general_dilated(source, kernel, (1, 1), 'SAME', dimension_numbers=('NHWC', 'HWIO', 'NHWC'), precision=highest)

def forward(source, norm1_gain, norm1_bias, conv1_kernel, conv1_bias, norm2_gain, norm2_bias, conv2_kernel, conv2_bias, norm3_gain, norm3_bias, query_weight, query_bias, key_weight, value_weight, value_bias, out_weight, out_bias):
    first_active = low(jax.nn.silu(group_norm(source, norm1_gain, norm1_bias)))
    first_filtered = low_back(convolve(first_active, conv1_kernel) + conv1_bias)
    second_active = low(jax.nn.silu(group_norm(first_filtered, norm2_gain, norm2_bias)))
    second_filtered = low_back(convolve(second_active, conv2_kernel) + conv2_bias)
    residual = source + second_filtered
    images, height, across, channels = residual.shape
    normed = low(group_norm(residual, norm3_gain, norm3_bias)).reshape(images, height * across, channels)
    queries = low(low_back(jnp.einsum('bnc,cd->bnd', normed, query_weight, precision=highest) + query_bias))
    key_rows = low(low_back(jnp.einsum('bnc,cd->bnd', normed, key_weight, precision=highest)))
    values = low(low_back(jnp.einsum('bnc,cd->bnd', normed, value_weight, precision=highest) + value_bias))
    scores = low_back(jnp.einsum('bnd,bmd->bnm', queries, key_rows, precision=highest) * channels ** (-0.5))
    attention = low(jax.nn.softmax(scores, axis=-1))
    blended = low(low_back(jnp.einsum('bnm,bmd->bnd', attention, values, precision=highest)))
    projected = jnp.einsum('bnd,de->bne', blended, out_weight, precision=highest) + out_bias
    return residual + projected.reshape(images, height, across, channels)

def reference(image_rows, grad_out, code_ids, dead_flags, replace_ids, latents, codebook, norm1_gain, norm1_bias, conv1_kernel, conv1_bias, norm2_gain, norm2_bias, conv2_kernel, conv2_bias, norm3_gain, norm3_bias, query_weight, query_bias, key_weight, value_weight, value_bias, out_weight, out_bias):
    params = tuple((weight.astype(jnp.float32) for weight in (norm1_gain, norm1_bias, conv1_kernel, conv1_bias, norm2_gain, norm2_bias, conv2_kernel, conv2_bias, norm3_gain, norm3_bias, query_weight, query_bias, key_weight, value_weight, value_bias, out_weight, out_bias)))
    per_block = 16
    blocks = IMAGES // per_block
    images_in = image_rows.astype(jnp.float32).reshape(blocks, per_block, SIDE, SIDE, C)
    cotangents = grad_out.astype(jnp.float32).reshape(blocks, per_block, SIDE, SIDE, C)

    def scan_step(running, inputs):
        source, cotangent = inputs
        output, pullback = jax.vjp(forward, source, *params)
        gradients = pullback(cotangent)
        running = tuple((kept + addend for kept, addend in zip(running, gradients[1:])))
        return (running, (output.astype(jnp.bfloat16), gradients[0].astype(jnp.bfloat16)))
    zeroes = tuple((jnp.zeros_like(weight) for weight in params))
    summed, (outputs, input_grads) = lax.scan(scan_step, zeroes, (images_in, cotangents))
    block_out = outputs.reshape(IMAGES, SIDE, SIDE, C)
    input_grad = input_grads.reshape(IMAGES, SIDE, SIDE, C)
    counts = jax.ops.segment_sum(jnp.ones((PIXELS,), jnp.float32), code_ids, num_segments=CODES)
    shares = counts / PIXELS
    perplexity = jnp.exp(-jnp.sum(shares * jnp.log(shares + 1e-10)))
    chosen = latents[replace_ids].astype(jnp.float32)
    new_codebook = jnp.where(dead_flags[:, None] == 1, chosen, codebook)
    return (block_out, input_grad, summed[0], summed[1], summed[2], summed[3], summed[4], summed[5], summed[6], summed[7], summed[8], summed[9], summed[10], summed[11], summed[12], summed[13], summed[14], summed[15], summed[16], new_codebook, counts.astype(jnp.int32), perplexity)
```

```python
import functools

import jax
import jax.numpy as jnp
from jax import lax
from jax.experimental import pallas as pl
from jax.experimental.pallas import tpu as pltpu
from jax.sharding import PartitionSpec as P

EPS = 1e-06
GROUP = 16
DEAD = 256
AXES = ("grp", "row")
F32 = jnp.float32
BF = jnp.bfloat16
NN = (((1,), (0,)), ((), ()))
NT = (((1,), (1,)), ((), ()))
TN = (((0,), (0,)), ((), ()))
VMEM = pl.BlockSpec(memory_space=pltpu.VMEM)
SMEM = pl.BlockSpec(memory_space=pltpu.SMEM)
HBM = pl.BlockSpec(memory_space=pl.ANY)
shape_of = jax.ShapeDtypeStruct


def mm(a, b, dims=NN):
    return lax.dot_general(a, b, dims, preferred_element_type=F32)


def colsum(v):
    return jnp.sum(v, axis=0, keepdims=True)


def group_sum(v):
    lanes = v.shape[1]
    lane = lax.broadcasted_iota(jnp.int32, v.shape, 1)
    step = 1
    while step < GROUP:
        below = pltpu.roll(v, step, 1)
        above = pltpu.roll(v, lanes - step, 1)
        v = v + jnp.where((lane & step) != 0, below, above)
        step *= 2
    return v


def normalized(v):
    count = v.shape[0] * GROUP
    middle = group_sum(colsum(v)) / count
    centered = v - middle
    spread = group_sum(colsum(centered * centered)) / count
    scale = lax.rsqrt(spread + EPS)
    return centered * scale, scale


def norm_back(n, scale, gain, dy):
    count = n.shape[0] * GROUP
    bias_grad = colsum(dy)
    gain_grad = colsum(dy * n)
    mean_d = group_sum(bias_grad * gain) / count
    mean_dn = group_sum(gain_grad * gain) / count
    return scale * (dy * gain - mean_d - n * mean_dn), gain_grad, bias_grad


def sigmoid(y):
    return 1.0 / (1.0 + jnp.exp(-y))


def shifted(v, side):
    px = v.shape[0]
    col = lax.broadcasted_iota(jnp.int32, v.shape, 0) % side
    left = jnp.where(col == 0, 0.0, pltpu.roll(v, 1, 0))
    right = jnp.where(col == side - 1, 0.0, pltpu.roll(v, px - 1, 0))
    return left, v, right


def put_shifts(s_ref, image, v, side):
    px, ch = v.shape
    for j, t in enumerate(shifted(v, side)):
        s_ref[image, side : px + side, j * ch : (j + 1) * ch] = t.astype(BF)


def clear_edges(s_ref, side):
    images, rows, width = s_ref.shape
    zero = jnp.zeros((side, width), BF)
    for i in range(images):
        s_ref[i, 0:side, :] = zero
        s_ref[i, rows - side : rows, :] = zero


def conv(s_ref, w_ref, image, px, side, ch):
    acc = None
    for dh in range(3):
        part = mm(
            s_ref[image, dh * side : dh * side + px, :],
            w_ref[dh * 3 * ch : (dh + 1) * 3 * ch, :],
        )
        acc = part if acc is None else acc + part
    return acc


def conv_back(s_ref, w_ref, image, px, side, ch):
    acc = None
    for dh in range(3):
        for dw in range(3):
            tap = dh * 3 + dw
            first = (2 - dh) * side
            part = mm(
                s_ref[image, first : first + px, (2 - dw) * ch : (3 - dw) * ch],
                w_ref[tap * ch : (tap + 1) * ch, :],
                NT,
            )
            acc = part if acc is None else acc + part
    return acc


def gather_rows(dst_ref, mine_ref, other_ref, core):
    images, part, ch = other_ref.shape
    for i in range(images):
        dst_ref[i, pl.ds(pl.multiple_of(core * part, part), part), :] = mine_ref[core * images + i]
        dst_ref[i, pl.ds(pl.multiple_of((1 - core) * part, part), part), :] = other_ref[i]


def split_cols(v, core):
    half = v.shape[1] // 2
    low, high = v[:, :half], v[:, half:]
    return jnp.where(core == 0, low, high), jnp.where(core == 0, high, low)


def forward_body(
    place_ref, mine_ref, other_ref, gy_ref, vec_ref, w1_hbm, w2_hbm, wq_hbm, wk_hbm, wv_hbm, wo_hbm,
    out_ref, act1_ref, act2_ref, conv1_ref, dres_ref, dkeep_ref, dsend_ref, stat_ref, gkeep_ref, gsend_ref,
    s_ref, x_ref, w1, w2, wq, wk, wv, wo, normed, q, k, v, mixed, sems, *, side,
):
    images, px, ch = x_ref.shape
    core = place_ref[0]
    me = place_ref[1]
    pairs = ((w1_hbm, w1), (w2_hbm, w2), (wq_hbm, wq), (wk_hbm, wk), (wv_hbm, wv), (wo_hbm, wo))
    copies = [pltpu.make_async_copy(a, b, sems.at[i]) for i, (a, b) in enumerate(pairs)]
    for c in copies:
        c.start()

    def row(i):
        return vec_ref[i : i + 1, :]

    clear_edges(s_ref, side)
    gather_rows(x_ref, mine_ref, other_ref, core)

    def first(i, carry):
        n, _ = normalized(x_ref[i].astype(F32))
        y = n * row(0) + row(1)
        a = y * sigmoid(y)
        act1_ref[i] = a.astype(BF)
        put_shifts(s_ref, i, a, side)
        return carry

    lax.fori_loop(0, images, first, 0)
    copies[0].wait()

    def second(i, carry):
        conv1_ref[i] = conv(s_ref, w1, i, px, side, ch) + row(2)
        return carry

    lax.fori_loop(0, images, second, 0)

    def third(i, carry):
        n, _ = normalized(conv1_ref[i])
        y = n * row(3) + row(4)
        a = y * sigmoid(y)
        act2_ref[i] = a.astype(BF)
        put_shifts(s_ref, i, a, side)
        return carry

    lax.fori_loop(0, images, third, 0)
    copies[1].wait()

    def fourth(i, carry):
        res = x_ref[i].astype(F32) + (conv(s_ref, w2, i, px, side, ch) + row(5))
        dres_ref[i] = res
        n, _ = normalized(res)
        normed[i] = (n * row(6) + row(7)).astype(BF)
        return carry

    lax.fori_loop(0, images, fourth, 0)
    for c in copies[2:]:
        c.wait()
    scale = ch ** -0.5
    stat_ref[...] = jnp.zeros(stat_ref.shape, F32)

    def attend(i, carry):
        nb = normed[i]
        qi = (mm(nb, wq[...]) + row(8)).astype(BF)
        ki = mm(nb, wk[...]).astype(BF)
        vi = (mm(nb, wv[...]) + row(9)).astype(BF)
        scores = mm(qi, ki, NT) * scale
        peak = jnp.max(scores, axis=1, keepdims=True)
        lifted = jnp.exp(scores - peak)
        probs = lifted / jnp.sum(lifted, axis=1, keepdims=True)
        pb = probs.astype(BF)
        mi = mm(pb, vi).astype(BF)
        mixed[i] = mi
        res = dres_ref[i]
        out_ref[i] = (res + (mm(mi, wo[...]) + row(10))).astype(BF)
        gy = gy_ref[i]
        gyf = gy.astype(F32)
        dm = mm(gy, wo[...], NT).astype(BF)
        dv = mm(pb, dm, TN).astype(BF)
        dp = mm(dm, vi, NT)
        ds = (probs * (dp - jnp.sum(probs * dp, axis=1, keepdims=True))).astype(BF)
        dq = (mm(ds, ki) * scale).astype(BF)
        dk = (mm(ds, qi, TN) * scale).astype(BF)
        q[i] = dq
        k[i] = dk
        v[i] = dv
        dn = mm(dq, wq[...], NT) + mm(dk, wk[...], NT) + mm(dv, wv[...], NT)
        n, r = normalized(res)
        dx, gain_grad, bias_grad = norm_back(n, r, row(6), dn)
        dres = gyf + dx
        dres_ref[i] = dres
        db = dres.astype(BF)
        dkeep_ref[i], dsend_ref[i] = split_cols(db, core)
        stat_ref[0:1, :] += colsum(db.astype(F32))
        stat_ref[1:2, :] += gain_grad
        stat_ref[2:3, :] += bias_grad
        stat_ref[3:4, :] += colsum(dq.astype(F32))
        stat_ref[4:5, :] += colsum(dv.astype(F32))
        stat_ref[5:6, :] += colsum(gyf)
        return carry

    lax.fori_loop(0, images, attend, 0)
    owners, _, rows, _ = gkeep_ref.shape

    def flat(ref):
        return ref[...].reshape(images * px, ch)

    for j, (lhs, rhs) in enumerate(((normed, q), (normed, k), (normed, v), (mixed, gy_ref))):
        keep, send = split_cols(mm(flat(lhs), flat(rhs), TN).astype(BF), core)
        for o in range(owners):
            gkeep_ref[o ^ me, j] = keep[o * rows : (o + 1) * rows]
            gsend_ref[o ^ me, j] = send[o * rows : (o + 1) * rows]


def run_forward(place, mine, other, gy, vec, w1, w2, wq, wk, wv, wo, owners, side):
    images, px, ch = gy.shape
    half = ch // 2
    rows = ch // owners
    whole = (images, px, ch)
    return pl.pallas_call(
        functools.partial(forward_body, side=side),
        name="forward_attention",
        in_specs=[SMEM] + [VMEM] * 4 + [HBM] * 6,
        out_specs=[VMEM] * 10,
        out_shape=[
            shape_of(whole, BF), shape_of(whole, BF), shape_of(whole, BF),
            shape_of(whole, F32), shape_of(whole, F32),
            shape_of((images, px, half), BF), shape_of((images, px, half), BF),
            shape_of((8, ch), F32),
            shape_of((owners, 4, rows, half), BF), shape_of((owners, 4, rows, half), BF),
        ],
        scratch_shapes=[
            pltpu.VMEM((images, px + 2 * side, 3 * ch), BF),
            pltpu.VMEM(whole, BF),
            pltpu.VMEM((9 * ch, ch), BF), pltpu.VMEM((9 * ch, ch), BF),
        ]
        + [pltpu.VMEM((ch, ch), BF)] * 4
        + [pltpu.VMEM(whole, BF)] * 5
        + [pltpu.SemaphoreType.DMA((6,))],
        compiler_params=pltpu.CompilerParams(vmem_limit_bytes=52 << 20),
    )(place, mine, other, gy, vec, w1, w2, wq, wk, wv, wo)


def back2_body(
    place_ref, dres_ref, conv1_ref, vec_ref, w2_hbm,
    dkeep_ref, dsend_ref, dfull_ref, stat_ref, s_ref, w2, sem, *, side,
):
    images, px, ch = dres_ref.shape
    core = place_ref[0]
    copy = pltpu.make_async_copy(w2_hbm, w2, sem)
    copy.start()
    clear_edges(s_ref, side)
    stat_ref[...] = jnp.zeros(stat_ref.shape, F32)

    def row(i):
        return vec_ref[i : i + 1, :]

    def shifts(i, carry):
        put_shifts(s_ref, i, dres_ref[i], side)
        return carry

    lax.fori_loop(0, images, shifts, 0)
    copy.wait()

    def body(i, carry):
        da = conv_back(s_ref, w2, i, px, side, ch)
        n, r = normalized(conv1_ref[i])
        y = n * row(3) + row(4)
        sig = sigmoid(y)
        dy = da * (sig * (1.0 + y * (1.0 - sig)))
        dx, gain_grad, bias_grad = norm_back(n, r, row(3), dy)
        db = dx.astype(BF)
        dfull_ref[i] = db
        dkeep_ref[i], dsend_ref[i] = split_cols(db, core)
        stat_ref[0:1, :] += gain_grad
        stat_ref[1:2, :] += bias_grad
        stat_ref[2:3, :] += colsum(db.astype(F32))
        return carry

    lax.fori_loop(0, images, body, 0)


def run_back2(place, dres, conv1, vec, w2, side):
    images, px, ch = dres.shape
    half = (images, px, ch // 2)
    return pl.pallas_call(
        functools.partial(back2_body, side=side),
        name="conv2_back",
        in_specs=[SMEM, VMEM, VMEM, VMEM, HBM],
        out_specs=[VMEM] * 4,
        out_shape=[shape_of(half, BF), shape_of(half, BF), shape_of((images, px, ch), BF), shape_of((8, ch), F32)],
        scratch_shapes=[
            pltpu.VMEM((images, px + 2 * side, 3 * ch), BF),
            pltpu.VMEM((9 * ch, ch), BF),
            pltpu.SemaphoreType.DMA(()),
        ],
        compiler_params=pltpu.CompilerParams(vmem_limit_bytes=40 << 20),
    )(place, dres, conv1, vec, w2)


def back1_body(
    place_ref, dfull_ref, mine_ref, other_ref, dres_ref, vec_ref, w1_hbm,
    keep_ref, send_ref, stat_ref, s_ref, x_ref, w1, sem, *, side,
):
    images, px, ch = dres_ref.shape
    part = px // 2
    core = place_ref[0]
    copy = pltpu.make_async_copy(w1_hbm, w1, sem)
    copy.start()
    clear_edges(s_ref, side)
    stat_ref[...] = jnp.zeros(stat_ref.shape, F32)
    gather_rows(x_ref, mine_ref, other_ref, core)

    def row(i):
        return vec_ref[i : i + 1, :]

    def shifts(i, carry):
        put_shifts(s_ref, i, dfull_ref[i].astype(F32), side)
        return carry

    lax.fori_loop(0, images, shifts, 0)
    copy.wait()

    def body(i, carry):
        da = conv_back(s_ref, w1, i, px, side, ch)
        n, r = normalized(x_ref[i].astype(F32))
        y = n * row(0) + row(1)
        sig = sigmoid(y)
        dy = da * (sig * (1.0 + y * (1.0 - sig)))
        dx, gain_grad, bias_grad = norm_back(n, r, row(0), dy)
        stat_ref[0:1, :] += gain_grad
        stat_ref[1:2, :] += bias_grad
        total = (dres_ref[i] + dx).astype(BF)
        low, high = total[:part], total[part:]
        keep_ref[i] = jnp.where(core == 0, low, high)
        send_ref[i] = jnp.where(core == 0, high, low)
        return carry

    lax.fori_loop(0, images, body, 0)


def run_back1(place, dfull, mine, other, dres, vec, w1, side):
    images, px, ch = dres.shape
    part = (images, px // 2, ch)
    return pl.pallas_call(
        functools.partial(back1_body, side=side),
        name="conv1_back",
        in_specs=[SMEM] + [VMEM] * 5 + [HBM],
        out_specs=[VMEM] * 3,
        out_shape=[shape_of(part, BF), shape_of(part, BF), shape_of((8, ch), F32)],
        scratch_shapes=[
            pltpu.VMEM((images, px + 2 * side, 3 * ch), BF),
            pltpu.VMEM((images, px, ch), BF),
            pltpu.VMEM((9 * ch, ch), BF),
            pltpu.SemaphoreType.DMA(()),
        ],
        compiler_params=pltpu.CompilerParams(vmem_limit_bytes=40 << 20),
    )(place, dfull, mine, other, dres, vec, w1)


def kernel_grad_body(place_ref, a0_ref, a1_ref, d0_ref, d1_ref, low_ref, high_ref, s_ref, d_ref, *, side):
    images, px, ch = a0_ref.shape
    half = d0_ref.shape[2]
    quarter = half // 2
    me = place_ref[1]
    owners, _, rows, _ = low_ref.shape
    zero = jnp.zeros((side, half), BF)
    for n in range(2 * images):
        d_ref[n, 0:side, :] = zero
        d_ref[n, px + side :, :] = zero
    for n, (a, d) in enumerate(((a0_ref, d0_ref), (a1_ref, d1_ref))):

        def fill(i, carry, a=a, d=d, n=n):
            at = n * images + i
            d_ref[at, side : px + side, :] = d[i]
            for j, t in enumerate(shifted(a[i].astype(F32), side)):
                s_ref[j * ch : (j + 1) * ch, pl.ds(pl.multiple_of(at * px, px), px)] = t.astype(BF).T
            return carry

        lax.fori_loop(0, images, fill, 0)
    for dh in range(3):
        start = (2 - dh) * side
        d = jnp.concatenate([d_ref[n, start : start + px, :] for n in range(2 * images)], axis=0)
        g = mm(s_ref[...], d).astype(BF)
        for o in range(owners):
            low_ref[o ^ me, dh] = g[o * rows : (o + 1) * rows, :quarter]
            high_ref[o ^ me, dh] = g[o * rows : (o + 1) * rows, quarter:]


def run_kernel_grad(place, a0, a1, d0, d1, owners, side, name):
    images, px, ch = a0.shape
    half = d0.shape[2]
    out = shape_of((owners, 3, 3 * ch // owners, half // 2), BF)
    return pl.pallas_call(
        functools.partial(kernel_grad_body, side=side),
        name=name,
        in_specs=[SMEM] + [VMEM] * 4,
        out_specs=[VMEM] * 2,
        out_shape=[out, out],
        scratch_shapes=[
            pltpu.VMEM((3 * ch, 2 * images * px), BF),
            pltpu.VMEM((2 * images, px + 2 * side, half), BF),
        ],
        compiler_params=pltpu.CompilerParams(vmem_limit_bytes=40 << 20),
    )(place, a0, a1, d0, d1)


def codes_body(place_ref, ids_ref, dead_ref, replace_ref, latents_ref, counts_ref, slots_ref, keep_ref, send_ref):
    core = place_ref[0]
    me = place_ref[1]
    offset = place_ref[2]
    codes = dead_ref.shape[1]
    pixels, width = latents_ref.shape
    one = jnp.ones((), BF)
    none = jnp.zeros((), BF)
    code = lax.broadcasted_iota(jnp.int32, (codes, pixels), 0)
    hit = jnp.where(code == ids_ref[...], one, none)
    counts_ref[...] = mm(jnp.ones((8, pixels), BF), hit, NT)
    dead = dead_ref[...]
    ahead = lax.broadcasted_iota(jnp.int32, (codes, codes), 0) <= lax.broadcasted_iota(jnp.int32, (codes, codes), 1)
    rank = mm(jnp.broadcast_to(dead.astype(F32), (8, codes)).astype(BF), jnp.where(ahead, one, none))[0:1]
    rank = jnp.where(dead == 1, rank.astype(jnp.int32) - 1, -1)
    owners, count, _ = keep_ref.shape
    at = lax.broadcasted_iota(jnp.int32, (DEAD, codes), 0)
    chip_at = (at % (owners * count)) // count
    at = ((at // (owners * count)) ^ core) * (owners * count) + (chip_at ^ me) * count + at % count
    slot = at == rank
    slots_ref[...] = jnp.where(slot, one, none)
    wanted = jnp.sum(jnp.where(slot, replace_ref[...], 0), axis=1, keepdims=True) - offset
    pixel = lax.broadcasted_iota(jnp.int32, (DEAD, pixels), 1)
    rows = mm(jnp.where(pixel == wanted, one, none), latents_ref[...]).astype(BF)
    for j in range(owners):
        keep_ref[j] = rows[j * count : (j + 1) * count]
        send_ref[j] = rows[DEAD // 2 + j * count : DEAD // 2 + (j + 1) * count]


def run_codes(place, ids, dead, replace, latents, owners):
    codes = dead.shape[1]
    width = latents.shape[1]
    rows = shape_of((owners, DEAD // (2 * owners), width), BF)
    return pl.pallas_call(
        codes_body,
        name="codes",
        in_specs=[SMEM] + [VMEM] * 4,
        out_specs=[VMEM] * 4,
        out_shape=[shape_of((8, codes), F32), shape_of((DEAD, codes), BF), rows, rows],
        compiler_params=pltpu.CompilerParams(vmem_limit_bytes=40 << 20),
    )(place, ids, dead, replace, latents)


def codebook_body(place_ref, mine_low, mine_high, other_low, other_high, slots_ref, book_ref, out_ref, rows_ref):
    device = place_ref[3]
    owners, count, quarter = mine_low.shape
    entries, width = book_ref.shape
    rows_ref[:, width:] = jnp.ones((DEAD, 128), F32)
    for side, (low, high) in enumerate(((mine_low, mine_high), (other_low, other_high))):
        for j in range(owners):
            start = (side * owners + j) * count
            at = slice(start, start + count)
            rows_ref[at, :quarter] = low[j].astype(F32)
            rows_ref[at, quarter:width] = high[j].astype(F32)
    whole = mm(slots_ref[...], rows_ref[...].astype(BF), TN)
    rows_out = whole.shape[0]
    pick = lax.broadcasted_iota(jnp.int32, (entries, rows_out), 1) - device * entries
    pick = jnp.where(pick == lax.broadcasted_iota(jnp.int32, (entries, rows_out), 0), 1.0, 0.0).astype(BF)
    own = mm(pick, whole.astype(BF))
    out_ref[...] = jnp.where(own[:, width : width + 1] > 0.5, own[:, :width], book_ref[...])


def run_codebook(place, mine, other, slots, book):
    entries, width = book.shape
    return pl.pallas_call(
        codebook_body,
        name="codebook",
        in_specs=[SMEM] + [VMEM] * 6,
        out_specs=VMEM,
        out_shape=shape_of(book.shape, F32),
        scratch_shapes=[pltpu.VMEM((DEAD, width + 128), F32)],
        compiler_params=pltpu.CompilerParams(vmem_limit_bytes=40 << 20),
    )(place, *mine, *other, slots, book)


def spread_body(place_ref, mine_low, mine_high, other_low, other_high, *outs):
    core = place_ref[0]
    count = len(outs)
    mine = jnp.concatenate([mine_low[0], mine_high[0]], axis=1).astype(F32)
    other = jnp.concatenate([other_low[0], other_high[0]], axis=1).astype(F32)
    both = jnp.concatenate([jnp.where(core == 0, mine, other), jnp.where(core == 0, other, mine)], axis=1)
    if count == 1:
        outs[0][...] = both.reshape(outs[0].shape)
    else:
        rows = both.shape[0] // count
        for i, out in enumerate(outs):
            out[0] = both[i * rows : (i + 1) * rows]


def run_spread(place, mine, other, outs, name):
    owners, rows, quarter = mine[0].shape
    block = pl.BlockSpec((1, rows, quarter), lambda j, p: (j, 0, 0))
    if len(outs[0]) == 4:
        pieces, _, each, ch = outs[0]
        specs = [pl.BlockSpec((pieces, 1, each, ch), lambda j, p: (0, j ^ p[1], 0, 0))]
    else:
        specs = [pl.BlockSpec((1,) + s[1:], lambda j, p: (j ^ p[1], 0, 0)) for s in outs]
    return pl.pallas_call(
        spread_body,
        name=name,
        grid_spec=pltpu.PrefetchScalarGridSpec(
            num_scalar_prefetch=1, grid=(owners,), in_specs=[block] * 4, out_specs=specs
        ),
        out_shape=[shape_of(s, F32) for s in outs],
        compiler_params=pltpu.CompilerParams(vmem_limit_bytes=32 << 20),
    )(place, *mine, *other)


def vectors_body(sums_ref, *outs):
    *vectors, usage_ref, perplexity_ref = outs
    for i, out in enumerate(vectors):
        out[...] = sums_ref[i : i + 1, :]
    codes = usage_ref.shape[1]
    width = sums_ref.shape[1]
    first = len(vectors)
    counts = jnp.concatenate([sums_ref[first + i : first + i + 1, :] for i in range(codes // width)], axis=1)
    usage_ref[...] = counts.astype(jnp.int32)
    share = counts / jnp.sum(counts, axis=1, keepdims=True)
    entropy = jnp.sum(share * jnp.log(share + 1e-10), axis=1, keepdims=True)
    perplexity_ref[...] = jnp.exp(-entropy)


def run_vectors(sums, vectors, codes):
    ch = sums.shape[1]
    return pl.pallas_call(
        vectors_body,
        name="vectors",
        in_specs=[VMEM],
        out_specs=[VMEM] * (vectors + 2),
        out_shape=[shape_of((1, ch), F32)] * vectors + [shape_of((1, codes), jnp.int32), shape_of((1, 1), F32)],
    )(sums)


class Links:
    def __init__(self, chips):
        self.chips = chips
        bits = chips.bit_length() - 1
        low = max(1, bits // 2 - 1) if bits > 1 else bits
        if bits % 3 == 0:
            sizes = [bits // 3] * 3
        elif bits == 4:
            sizes = [1, 1, 2]
        else:
            sizes = [low, bits - 2 * low, low]
        self.dims = []
        shift = 0
        for size in sizes:
            self.dims.append((shift, 1 << size))
            shift += size
        self.lead = tuple(n for _, n in reversed(self.dims))

    def axis(self, dim):
        return len(self.dims) - 1 - dim

    def send(self, value, key):
        pairs = [(g * 2 + c, (g ^ key) * 2 + c) for g in range(self.chips) for c in range(2)]
        return lax.ppermute(value, AXES, pairs)

    def partner(self, value):
        pairs = [(g * 2 + c, g * 2 + 1 - c) for g in range(self.chips) for c in range(2)]
        return lax.ppermute(value, AXES, pairs)

    def reduce(self, value, dim):
        shift, n = self.dims[dim]
        ax = self.axis(dim)
        got = [self.send(lax.index_in_dim(value, k, ax), k << shift) for k in range(1, n)]
        total = lax.index_in_dim(value, 0, ax).astype(F32)
        for g in got:
            total = total + g.astype(F32)
        return total.astype(BF)

    def gather(self, value, dim):
        shift, n = self.dims[dim]
        return jnp.concatenate([value] + [self.send(value, k << shift) for k in range(1, n)], axis=self.axis(dim))

    def all_reduce(self, low, high):
        shape = low.shape
        rows = shape[1]
        last = range(2, len(self.dims))
        low = low.reshape(self.lead + shape[1:])
        high = high.reshape(self.lead + shape[1:])
        low = self.reduce(low, 0)
        high = self.reduce(high, 1)
        low = self.reduce(low, 1)
        high = self.reduce(high, 0)
        both = jnp.concatenate([low, high], axis=-2)
        for dim in last:
            both = self.reduce(both, dim)
        for dim in reversed(last):
            both = self.gather(both, dim)
        low, high = both[..., :rows, :], both[..., rows:, :]
        low = self.gather(low, 1)
        high = self.gather(high, 0)
        low = self.gather(low, 0)
        high = self.gather(high, 1)
        return low.reshape(shape), high.reshape(shape)

    def small_all_reduce(self, value):
        value = value + self.partner(value)
        key = 1
        while key < self.chips:
            value = value + self.send(value, key)
            key *= 2
        return value


def local(
    image_rows, grad_out, code_ids, dead_flags, replace_ids, latents, codebook,
    norm1_gain, norm1_bias, conv1_kernel, conv1_bias, norm2_gain, norm2_bias, conv2_kernel, conv2_bias,
    norm3_gain, norm3_bias, query_weight, query_bias, key_weight, value_weight, value_bias, out_weight, out_bias,
    *, chips,
):
    links = Links(chips)
    owners = chips
    all_images, part_rows, side, ch = image_rows.shape
    images = all_images // 2
    px = grad_out.shape[1] * side
    part = part_rows * side
    core = lax.axis_index("row").astype(jnp.int32)
    chip = lax.axis_index("grp").astype(jnp.int32)
    device = chip * 2 + core
    place = jnp.stack([core, chip, device * latents.shape[0], device])
    mine = image_rows.reshape(all_images, part, ch)
    other = links.partner(lax.dynamic_slice_in_dim(mine, (1 - core) * images, images))
    vec = jnp.stack([
        norm1_gain, norm1_bias, conv1_bias, norm2_gain, norm2_bias, conv2_bias,
        norm3_gain, norm3_bias, query_bias, value_bias, out_bias,
    ]).astype(F32)
    w1 = conv1_kernel.reshape(9 * ch, ch)
    w2 = conv2_kernel.reshape(9 * ch, ch)
    codes = dead_flags.shape[0]
    counts, slots, ckeep, csend = run_codes(
        place, code_ids.reshape(1, -1), dead_flags.reshape(1, -1), replace_ids.reshape(1, -1), latents, owners
    )
    gy = grad_out.reshape(images, px, ch)
    out, act1, act2, filtered, dres, dkeep2, dsend2, stat_a, gkeep, gsend = run_forward(
        place, mine, other, gy, vec, w1, w2, query_weight, key_weight, value_weight, out_weight, owners, side
    )
    dother2 = links.partner(dsend2)
    act2_other = links.partner(act2)
    act1_other = links.partner(act1)
    got = links.partner(jnp.concatenate([gsend.reshape(owners, -1, ch // 2), csend], axis=1))
    kept = jnp.concatenate([gkeep.reshape(owners, -1, ch // 2), ckeep], axis=1)
    attn = (kept.astype(F32) + got.astype(F32)).astype(BF)
    quarter = ch // 4
    attn_rows = 4 * (ch // owners)
    dkeep1, dsend1, dfull1, stat_b = run_back2(place, dres, filtered, vec, w2, side)
    dother1 = links.partner(dsend1)
    low2, high2 = run_kernel_grad(place, act2, act2_other, dkeep2, dother2, owners, side, "conv2_grad")
    conv_rows = low2.shape[1] * low2.shape[2]
    low2 = low2.reshape(owners, conv_rows, quarter)
    high2 = high2.reshape(owners, conv_rows, quarter)
    low_a, high_a = links.all_reduce(
        jnp.concatenate([attn[:, :, :quarter], low2], axis=1), jnp.concatenate([attn[:, :, quarter:], high2], axis=1)
    )
    low1, high1 = run_kernel_grad(place, act1, act1_other, dkeep1, dother1, owners, side, "conv1_grad")
    low_b, high_b = links.all_reduce(
        low1.reshape(owners, conv_rows, quarter), high1.reshape(owners, conv_rows, quarter)
    )
    in_keep, in_send, stat_c = run_back1(place, dfull1, mine, other, dres, vec, w1, side)
    in_got = links.partner(in_send)
    ordered = jnp.where(core == 0, jnp.concatenate([in_keep, in_got]), jnp.concatenate([in_got, in_keep]))
    input_grad = ordered.reshape(image_rows.shape)
    vectors = jnp.concatenate([stat_c[:2], stat_b[2:3], stat_b[:2], stat_a[:6], counts[:1].reshape(-1, ch)])
    vectors = links.small_all_reduce(vectors)
    *vec_grads, usage, perplexity = run_vectors(vectors, 11, codes)
    (g1, b1, cb1, g2, b2, cb2, g3, b3, qb, vb, ob) = [v.reshape(ch) for v in vec_grads]
    low_ao, high_ao = links.partner(low_a), links.partner(high_a)
    each = ch // owners
    ends = (attn_rows, attn_rows + DEAD // (2 * owners))
    groups = (low_a, high_a, low_ao, high_ao)
    a_parts = [t[:, : ends[0]] for t in groups]
    c_parts = [t[:, ends[0] : ends[1]] for t in groups]
    w_parts = [t[:, ends[1] :] for t in groups]
    qg, kg, vg, og = run_spread(place, a_parts[:2], a_parts[2:], [(owners, each, ch)] * 4, "attention_spread")
    conv_shape = (3, owners, 3 * each, ch)
    (grad2,) = run_spread(place, w_parts[:2], w_parts[2:], [conv_shape], "conv2_spread")
    new_codebook = run_codebook(place, c_parts[:2], c_parts[2:], slots, codebook)
    (grad1,) = run_spread(
        place, (low_b, high_b), (links.partner(low_b), links.partner(high_b)), [conv_shape], "conv1_spread"
    )
    kernel_shape = (3, 3, ch, ch)
    qg, kg, vg, og = [t.reshape(ch, ch) for t in (qg, kg, vg, og)]
    return (
        out.reshape(grad_out.shape), input_grad,
        g1, b1, grad1.reshape(kernel_shape), cb1, g2, b2, grad2.reshape(kernel_shape), cb2, g3, b3,
        qg, qb, kg, vg, vb, og, ob,
        new_codebook, usage.reshape(codes), perplexity.reshape(()),
    )


def solution(mesh):
    both = ("grp", "row")
    in_specs = (
        P("grp", "row", None, None), P(both, None, None, None), P(both), P(), P(), P(both, None), P(both, None),
    ) + (P(),) * 17
    out_specs = (P(both, None, None, None), P("grp", "row", None, None)) + (P(),) * 17 + (P(both, None), P(), P())
    body = functools.partial(local, chips=mesh.shape["grp"])
    return jax.shard_map(body, mesh=mesh, in_specs=in_specs, out_specs=out_specs, check_vma=False)
```

```python
import functools

import jax
import jax.numpy as jnp
from jax import lax
from jax.experimental import pallas as pl
from jax.experimental.pallas import tpu as pltpu
from jax.sharding import PartitionSpec as P

EPS = 1e-06
GROUP = 16
LANES = 128
DEAD = 256
AXES = ("grp", "row")
F32 = jnp.float32
BF = jnp.bfloat16
NN = (((1,), (0,)), ((), ()))
NT = (((1,), (1,)), ((), ()))
TN = (((0,), (0,)), ((), ()))
VMEM = pl.BlockSpec(memory_space=pltpu.VMEM)
SMEM = pl.BlockSpec(memory_space=pltpu.SMEM)
HBM = pl.BlockSpec(memory_space=pltpu.HBM)
shape_of = jax.ShapeDtypeStruct


def took(us):
    return pl.CostEstimate(flops=int(us * 1.15e9), bytes_accessed=1 << 20, transcendentals=0)


def hbm(value):
    return pltpu.with_memory_space_constraint(value, pltpu.HBM)


def mm(a, b, dims=NN):
    return lax.dot_general(a, b, dims, preferred_element_type=F32)


def colsum(v):
    return jnp.sum(v, axis=0, keepdims=True)


def group_sums(rows):
    chunks = rows[0].shape[1] // LANES
    v = jnp.concatenate([r[:, c * LANES : (c + 1) * LANES] for r in rows for c in range(chunks)], axis=0)
    lane = lax.broadcasted_iota(jnp.int32, v.shape, 1)
    step = 1
    while step < GROUP:
        below = pltpu.roll(v, step, 1)
        above = pltpu.roll(v, LANES - step, 1)
        v = v + jnp.where((lane & step) != 0, below, above)
        step *= 2
    return [
        jnp.concatenate([v[k * chunks + c : k * chunks + c + 1] for c in range(chunks)], axis=1)
        for k in range(len(rows))
    ]


def normalized(images):
    count = images[0].shape[0] * GROUP
    middles = group_sums([colsum(v) for v in images])
    centered = [v - m / count for v, m in zip(images, middles)]
    spreads = group_sums([colsum(c * c) for c in centered])
    scales = [lax.rsqrt(v / count + EPS) for v in spreads]
    return [(c * r, r) for c, r in zip(centered, scales)]


def norm_back(images, gain):
    count = images[0][0].shape[0] * GROUP
    bias_grads = [colsum(dy) for _, _, dy in images]
    gain_grads = [colsum(dy * n) for n, _, dy in images]
    sums = group_sums([g * gain for g in bias_grads] + [g * gain for g in gain_grads])
    total = len(images)
    dxs = [
        r * (dy * gain - sums[i] / count - n * (sums[total + i] / count)) for i, (n, r, dy) in enumerate(images)
    ]
    return dxs, sum(gain_grads), sum(bias_grads)


def sigmoid(y):
    return 1.0 / (1.0 + jnp.exp(-y))


def shifted(v, side):
    px = v.shape[0]
    col = lax.broadcasted_iota(jnp.int32, v.shape, 0) % side
    left = jnp.where(col == 0, 0.0, pltpu.roll(v, 1, 0))
    right = jnp.where(col == side - 1, 0.0, pltpu.roll(v, px - 1, 0))
    return left, v, right


def put_shifts(s_ref, image, v, side):
    px, ch = v.shape
    for j, t in enumerate(shifted(v, side)):
        s_ref[image, side : px + side, j * ch : (j + 1) * ch] = t.astype(BF)


def clear_edges(s_ref, side):
    images, rows, width = s_ref.shape
    zero = jnp.zeros((side, width), BF)
    for i in range(images):
        s_ref[i, 0:side, :] = zero
        s_ref[i, rows - side : rows, :] = zero


def window(s_ref, first, px, cols):
    return jnp.concatenate([s_ref[i, first : first + px, cols] for i in range(s_ref.shape[0])], axis=0)


def conv(s_ref, w_ref, px, side, ch):
    acc = None
    for dh in range(3):
        part = mm(window(s_ref, dh * side, px, slice(None)), w_ref[dh * 3 * ch : (dh + 1) * 3 * ch, :])
        acc = part if acc is None else acc + part
    return acc


def conv_back(s_ref, w_ref, px, side, ch):
    acc = None
    for dh in range(3):
        for dw in range(3):
            tap = dh * 3 + dw
            cols = slice((2 - dw) * ch, (3 - dw) * ch)
            part = mm(window(s_ref, (2 - dh) * side, px, cols), w_ref[tap * ch : (tap + 1) * ch, :], NT)
            acc = part if acc is None else acc + part
    return acc


def split_cols(v, bit):
    half = v.shape[1] // 2
    low, high = v[:, :half], v[:, half:]
    return jnp.where(bit == 0, low, high), jnp.where(bit == 0, high, low)


def start_copies(pairs, sems):
    copies = [pltpu.make_async_copy(a, b, sems.at[i]) for i, (a, b) in enumerate(pairs)]
    for c in copies:
        c.start()
    return copies


def entry_body(
    place_ref, mine_hbm, other_ref, vec_ref, w1, gy_hbm, w2_hbm, wq_hbm, wk_hbm, wv_hbm, wo_hbm,
    own_ref, chip_ref, near_ref, far_ref, norm2_ref, scale2_ref, x_ref, gy_ref, w2, wq, wk, wv, wo, s_ref, sems, *, side,
):
    images, px, ch = x_ref.shape
    part = px // 2
    core = place_ref[0]
    bit, other_bit = place_ref[6], place_ref[7]
    here = pl.multiple_of(core * part, part)
    there = pl.multiple_of((1 - core) * part, part)
    copies = start_copies(
        [(mine_hbm.at[core * images + i], x_ref.at[i, pl.ds(here, part)]) for i in range(images)]
        + [(w2_hbm, w2), (gy_hbm, gy_ref), (wq_hbm, wq), (wk_hbm, wk), (wv_hbm, wv), (wo_hbm, wo)],
        sems,
    )

    def row(i):
        return vec_ref[i : i + 1, :]

    def give(which, a):
        for i in range(images):
            low = a[i].astype(BF)
            own_ref[which, i], near_ref[which, i] = split_cols(low, bit)
            chip_ref[which, i], far_ref[which, i] = split_cols(low, other_bit)

    clear_edges(s_ref, side)
    for i in range(images):
        x_ref[i, pl.ds(there, part), :] = other_ref[i]
    for c in copies[:images]:
        c.wait()
    active = []
    for i, (n, _) in enumerate(normalized([x_ref[i].astype(F32) for i in range(images)])):
        y = n * row(0) + row(1)
        active.append(y * sigmoid(y))
        put_shifts(s_ref, i, active[i], side)
    give(0, active)
    filtered = conv(s_ref, w1, px, side, ch) + row(2)
    active = []
    for i, (n, r) in enumerate(normalized([filtered[i * px : (i + 1) * px] for i in range(images)])):
        norm2_ref[i] = n
        scale2_ref[i : i + 1, :] = r
        y = n * row(3) + row(4)
        active.append(y * sigmoid(y))
    give(1, active)
    for c in copies[images:]:
        c.wait()


def run_entry(place, mine, other, vec, w1, gy, w2, weights, side):
    images, part, ch = other.shape
    px = 2 * part
    acts = shape_of((2, images, px, ch // 2), BF)
    whole = (images, px, ch)
    return pl.pallas_call(
        functools.partial(entry_body, side=side),
        name="entry",
        in_specs=[SMEM, HBM] + [VMEM] * 3 + [HBM] * 6,
        out_specs=[VMEM] * 13,
        out_shape=[acts] * 4
        + [shape_of(whole, F32), shape_of((images, ch), F32), shape_of(whole, BF), shape_of(whole, BF), shape_of(w2.shape, BF)]
        + [shape_of((ch, ch), BF)] * 4,
        scratch_shapes=[
            pltpu.VMEM((images, px + 2 * side, 3 * ch), BF),
            pltpu.SemaphoreType.DMA((images + 6,)),
        ],
        cost_estimate=took(8.5),
        compiler_params=pltpu.CompilerParams(vmem_limit_bytes=12 << 20),
    )(place, hbm(mine), other, vec, w1, *[hbm(v) for v in (gy, w2, *weights)])


def attention_body(
    place_ref, x_ref, own_ref, near_ref, gy_ref, ckeep_ref, csend_ref, vec_ref, w2, wq, wk, wv, wo,
    out_ref, dres_ref, dkeep_ref, dsend_ref, stat_ref, gkeep_ref, gsend_ref,
    s_ref, norm_ref, normed, q, k, v, mixed, *, side,
):
    images, px, ch = x_ref.shape
    core = place_ref[0]
    bit = place_ref[6]

    def row(i):
        return vec_ref[i : i + 1, :]

    every = range(images)
    clear_edges(s_ref, side)
    for i in every:
        mine, other = own_ref[1, i], near_ref[1, i]
        a = jnp.concatenate([jnp.where(bit == 0, mine, other), jnp.where(bit == 0, other, mine)], axis=1)
        put_shifts(s_ref, i, a.astype(F32), side)

    def flat(ref):
        return ref[...].reshape(images * px, ch)

    def spans(v):
        return [v[i * px : (i + 1) * px] for i in every]

    dm = mm(flat(gy_ref), wo[...], NT).astype(BF)
    branch = conv(s_ref, w2, px, side, ch) + row(5)
    res = [x_ref[i].astype(F32) + b for i, b in zip(every, spans(branch))]
    scales = []
    for i, (n, r) in enumerate(normalized(res)):
        dres_ref[i] = res[i]
        norm_ref[i] = n
        scales.append(r)
        normed[i] = (n * row(6) + row(7)).astype(BF)
    nb = flat(normed)
    queries = (mm(nb, wq[...]) + row(8)).astype(BF)
    keys = mm(nb, wk[...]).astype(BF)
    values = (mm(nb, wv[...]) + row(9)).astype(BF)
    scale = ch ** -0.5
    for i, qi, ki, vi, di in zip(every, spans(queries), spans(keys), spans(values), spans(dm)):
        scores = mm(qi, ki, NT) * scale
        dp = mm(di, vi, NT)
        peak = jnp.max(scores, axis=1, keepdims=True)
        lifted = jnp.exp(scores - peak)
        probs = lifted / jnp.sum(lifted, axis=1, keepdims=True)
        pb = probs.astype(BF)
        mixed[i] = mm(pb, vi).astype(BF)
        v[i] = mm(pb, di, TN).astype(BF)
        ds = (probs * (dp - jnp.sum(probs * dp, axis=1, keepdims=True))).astype(BF)
        q[i] = (mm(ds, ki) * scale).astype(BF)
        k[i] = (mm(ds, qi, TN) * scale).astype(BF)
    dn = mm(flat(q), wq[...], NT) + mm(flat(k), wk[...], NT) + mm(flat(v), wv[...], NT)
    projected = mm(flat(mixed), wo[...]) + row(10)
    for i, p in zip(every, spans(projected)):
        out_ref[i] = (dres_ref[i] + p).astype(BF)
    dxs, gain_grad, bias_grad = norm_back(
        [(norm_ref[i], r, d) for i, r, d in zip(every, scales, spans(dn))], row(6)
    )
    total = jnp.zeros((1, ch), F32)
    for i, dx in zip(every, dxs):
        dres = gy_ref[i].astype(F32) + dx
        dres_ref[i] = dres
        db = dres.astype(BF)
        dkeep_ref[i], dsend_ref[i] = split_cols(db, core)
        total = total + colsum(db.astype(F32))
    stat_ref[...] = jnp.zeros(stat_ref.shape, F32)
    stat_ref[0:1, :] = total
    stat_ref[1:2, :] = gain_grad
    stat_ref[2:3, :] = bias_grad
    stat_ref[3:4, :] = colsum(flat(q).astype(F32))
    stat_ref[4:5, :] = colsum(flat(v).astype(F32))
    stat_ref[5:6, :] = colsum(flat(gy_ref).astype(F32))
    owners = gkeep_ref.shape[0]
    rows = ch // owners
    mine_at, other_at = place_ref[4], place_ref[5]
    for j, (lhs, rhs) in enumerate(((normed, q), (normed, k), (normed, v), (mixed, gy_ref))):
        keep, send = split_cols(mm(flat(lhs), flat(rhs), TN).astype(BF), core)
        for o in range(owners):
            gkeep_ref[o ^ mine_at, j * rows : (j + 1) * rows] = keep[o * rows : (o + 1) * rows]
            gsend_ref[o ^ other_at, j * rows : (j + 1) * rows] = send[o * rows : (o + 1) * rows]
    for o in range(owners):
        gkeep_ref[o, 4 * rows :] = ckeep_ref[o]
        gsend_ref[o, 4 * rows :] = csend_ref[o]


def run_attention(place, x, own, near, gy, ckeep, csend, vec, weights, side):
    images, px, ch = gy.shape
    half = ch // 2
    owners, count, _ = ckeep.shape
    rows = 4 * (ch // owners) + count
    whole = (images, px, ch)
    return pl.pallas_call(
        functools.partial(attention_body, side=side),
        name="attention",
        in_specs=[SMEM] + [VMEM] * 12,
        out_specs=[VMEM] * 7,
        out_shape=[
            shape_of(whole, BF), shape_of(whole, F32),
            shape_of((images, px, half), BF), shape_of((images, px, half), BF),
            shape_of((8, ch), F32),
            shape_of((owners, rows, half), BF), shape_of((owners, rows, half), BF),
        ],
        scratch_shapes=[pltpu.VMEM((images, px + 2 * side, 3 * ch), BF), pltpu.VMEM(whole, F32)]
        + [pltpu.VMEM(whole, BF)] * 5,
        cost_estimate=took(13.5),
        compiler_params=pltpu.CompilerParams(vmem_limit_bytes=20 << 20),
    )(place, x, own, near, gy, ckeep, csend, vec, *weights)


def swish_back(da, ns, gain, bias):
    dys = []
    for d, n in zip(da, ns):
        y = n * gain + bias
        sig = sigmoid(y)
        dys.append(d * (sig * (1.0 + y * (1.0 - sig))))
    return dys


def back2_body(
    place_ref, dres_ref, norm2_ref, scale2_ref, vec_ref, w2,
    dkeep_ref, dsend_ref, dfull_ref, stat_ref, s_ref, *, side,
):
    images, px, ch = dres_ref.shape
    every = range(images)
    core = place_ref[0]
    clear_edges(s_ref, side)

    def row(i):
        return vec_ref[i : i + 1, :]

    for i in every:
        put_shifts(s_ref, i, dres_ref[i], side)
    da = conv_back(s_ref, w2, px, side, ch)
    ns = [norm2_ref[i] for i in every]
    dys = swish_back([da[i * px : (i + 1) * px] for i in every], ns, row(3), row(4))
    dxs, gain_grad, bias_grad = norm_back(
        [(n, scale2_ref[i : i + 1, :], dy) for i, n, dy in zip(every, ns, dys)], row(3)
    )
    total = jnp.zeros((1, ch), F32)
    for i, dx in zip(every, dxs):
        db = dx.astype(BF)
        dfull_ref[i] = db
        dkeep_ref[i], dsend_ref[i] = split_cols(db, core)
        total = total + colsum(db.astype(F32))
    stat_ref[...] = jnp.zeros(stat_ref.shape, F32)
    stat_ref[0:1, :] = gain_grad
    stat_ref[1:2, :] = bias_grad
    stat_ref[2:3, :] = total


def run_back2(place, dres, norm2, scale2, vec, w2, side):
    images, px, ch = dres.shape
    half = (images, px, ch // 2)
    return pl.pallas_call(
        functools.partial(back2_body, side=side),
        name="conv2_back",
        in_specs=[SMEM] + [VMEM] * 5,
        out_specs=[VMEM] * 4,
        out_shape=[shape_of(half, BF), shape_of(half, BF), shape_of((images, px, ch), BF), shape_of((8, ch), F32)],
        scratch_shapes=[pltpu.VMEM((images, px + 2 * side, 3 * ch), BF)],
        cost_estimate=took(5),
        compiler_params=pltpu.CompilerParams(vmem_limit_bytes=12 << 20),
    )(place, dres, norm2, scale2, vec, w2)


def back1_body(
    place_ref, dfull_ref, x_ref, dres_ref, vec_ref, w1,
    out_hbm, send_ref, stat_ref, s_ref, keep_ref, sem, *, side,
):
    images, px, ch = dres_ref.shape
    part = px // 2
    core = place_ref[0]
    every = range(images)
    clear_edges(s_ref, side)

    def row(i):
        return vec_ref[i : i + 1, :]

    for i in every:
        put_shifts(s_ref, i, dfull_ref[i].astype(F32), side)
    da = conv_back(s_ref, w1, px, side, ch)
    norms = normalized([x_ref[i].astype(F32) for i in every])
    ns = [n for n, _ in norms]
    dys = swish_back([da[i * px : (i + 1) * px] for i in every], ns, row(0), row(1))
    dxs, gain_grad, bias_grad = norm_back([(n, r, dy) for (n, r), dy in zip(norms, dys)], row(0))
    for i, dx in zip(every, dxs):
        total = (dres_ref[i] + dx).astype(BF)
        low, high = total[:part], total[part:]
        keep_ref[i] = jnp.where(core == 0, low, high)
        send_ref[i] = jnp.where(core == 0, high, low)
    stat_ref[...] = jnp.zeros(stat_ref.shape, F32)
    stat_ref[0:1, :] = gain_grad
    stat_ref[1:2, :] = bias_grad
    copy = pltpu.make_async_copy(keep_ref, out_hbm.at[pl.ds(core * images, images)], sem)
    copy.start()
    copy.wait()


def run_back1(place, dfull, x, dres, vec, w1, side):
    images, px, ch = dres.shape
    part = (images, px // 2, ch)
    return pl.pallas_call(
        functools.partial(back1_body, side=side),
        name="conv1_back",
        in_specs=[SMEM] + [VMEM] * 5,
        out_specs=[HBM, VMEM, VMEM],
        out_shape=[shape_of((2 * images, px // 2, ch), BF), shape_of(part, BF), shape_of((8, ch), F32)],
        scratch_shapes=[
            pltpu.VMEM((images, px + 2 * side, 3 * ch), BF),
            pltpu.VMEM(part, BF),
            pltpu.SemaphoreType.DMA(()),
        ],
        cost_estimate=took(5.4),
        compiler_params=pltpu.CompilerParams(vmem_limit_bytes=12 << 20),
    )(place, dfull, x, dres, vec, w1)


def place_rows_body(place_ref, got_ref, into_hbm, out_hbm, token_ref, sem):
    images = got_ref.shape[0]
    token_ref[...] = jnp.zeros(token_ref.shape, F32)
    copy = pltpu.make_async_copy(got_ref, out_hbm.at[pl.ds((1 - place_ref[0]) * images, images)], sem)
    copy.start()
    copy.wait()


def run_place_rows(place, got, into):
    return pl.pallas_call(
        place_rows_body,
        name="place_rows",
        in_specs=[SMEM, VMEM, HBM],
        out_specs=[HBM, VMEM],
        out_shape=[shape_of(into.shape, BF), shape_of((8, 128), F32)],
        scratch_shapes=[pltpu.SemaphoreType.DMA(())],
        input_output_aliases={2: 0},
        cost_estimate=took(1),
        compiler_params=pltpu.CompilerParams(vmem_limit_bytes=4 << 20),
    )(place, got, into)


def kernel_grad_body(place_ref, *refs, side, which):
    acts, grads = refs[:4], refs[4:8]
    out_ref, s_ref, d_ref = refs[-3:]
    _, images, px, part = acts[0].shape
    half = grads[0].shape[2]
    bits = place_ref[8]
    first, second, _, _ = out_ref.shape
    owners = first * second
    rows = part // owners
    zero = jnp.zeros((side, half), BF)
    for n in range(4 * images):
        d_ref[n, 0:side, :] = zero
        d_ref[n, px + side :, :] = zero
    for n, (a, d) in enumerate(zip(acts, grads)):

        def fill(i, carry, a=a, d=d, n=n):
            at = n * images + i
            d_ref[at, side : px + side, :] = d[i]
            for j, t in enumerate(shifted(a[which, i].astype(F32), side)):
                s_ref[j * part : (j + 1) * part, pl.ds(pl.multiple_of(at * px, px), px)] = t.astype(BF).T
            return carry

        lax.fori_loop(0, images, fill, 0)
    for dh in range(3):
        start = (2 - dh) * side
        d = jnp.concatenate([d_ref[n, start : start + px, :] for n in range(4 * images)], axis=0)
        g = mm(s_ref[...], d).astype(BF)
        for o in range(owners):
            at = o ^ bits
            for dw in range(3):
                tap = dh * 3 + dw
                begin = dw * part + o * rows
                out_ref[at // second, at % second, tap * rows : (tap + 1) * rows, :] = g[begin : begin + rows]


def run_kernel_grad(place, which, acts, grads, lead, side, name):
    _, images, px, part = acts[0].shape
    half = grads[0].shape[2]
    rows = 9 * (part // (lead[0] * lead[1]))
    return pl.pallas_call(
        functools.partial(kernel_grad_body, side=side, which=which),
        name=name,
        in_specs=[SMEM] + [VMEM] * 8,
        out_specs=VMEM,
        out_shape=shape_of((lead[0], lead[1], rows, half), BF),
        scratch_shapes=[
            pltpu.VMEM((3 * part, 4 * images * px), BF),
            pltpu.VMEM((4 * images, px + 2 * side, half), BF),
        ],
        cost_estimate=took(4.8),
        compiler_params=pltpu.CompilerParams(vmem_limit_bytes=14 << 20),
    )(place, *acts, *grads)


def prepare_body(place_ref, ids_hbm, dead_hbm, replace_hbm, latents_hbm, w1_hbm, *refs):
    count_vectors = (len(refs) - 12) // 2
    vectors = refs[:count_vectors]
    counts_ref, slots_ref, keep_ref, send_ref, vec_ref, w1_ref = refs[count_vectors : count_vectors + 6]
    lines = refs[count_vectors + 6 : 2 * count_vectors + 6]
    ids_ref, dead_ref, replace_ref, latents_ref, sems, _ = refs[2 * count_vectors + 6 :]
    copies = start_copies(
        (
            (ids_hbm, ids_ref), (dead_hbm, dead_ref), (replace_hbm, replace_ref), (latents_hbm, latents_ref),
            *zip(vectors, lines), (w1_hbm, w1_ref),
        ),
        sems,
    )
    core = place_ref[0]
    offset = place_ref[2]
    for c in copies[:2]:
        c.wait()
    codes = dead_ref.shape[1]
    pixels, width = latents_ref.shape
    one = jnp.ones((), BF)
    none = jnp.zeros((), BF)
    code = lax.broadcasted_iota(jnp.int32, (codes, pixels), 0)
    hit = jnp.where(code == ids_ref[...], one, none)
    counts_ref[...] = mm(jnp.ones((8, pixels), BF), hit, NT)
    dead = dead_ref[...]
    ahead = lax.broadcasted_iota(jnp.int32, (codes, codes), 0) <= lax.broadcasted_iota(jnp.int32, (codes, codes), 1)
    rank = mm(jnp.broadcast_to(dead.astype(F32), (8, codes)).astype(BF), jnp.where(ahead, one, none))[0:1]
    rank = jnp.where(dead == 1, rank.astype(jnp.int32) - 1, -1)
    owners, count, _ = keep_ref.shape
    at = lax.broadcasted_iota(jnp.int32, (DEAD, codes), 0)
    beyond = at // (owners * count)
    owner = ((at % (owners * count)) // count) ^ jnp.where(beyond == 0, place_ref[4], place_ref[5])
    at = (beyond ^ core) * (owners * count) + owner * count + at % count
    slot = at == rank
    slots_ref[...] = jnp.where(slot, one, none)
    for c in copies[2:4]:
        c.wait()
    wanted = jnp.sum(jnp.where(slot, replace_ref[...], 0), axis=1, keepdims=True) - offset
    pixel = lax.broadcasted_iota(jnp.int32, (DEAD, pixels), 1)
    rows = mm(jnp.where(pixel == wanted, one, none), latents_ref[...]).astype(BF)
    for j in range(owners):
        keep_ref[j] = rows[j * count : (j + 1) * count]
        send_ref[j] = rows[DEAD // 2 + j * count : DEAD // 2 + (j + 1) * count]
    for c in copies[4:]:
        c.wait()
    for i, line in enumerate(lines):
        vec_ref[i : i + 1, :] = line[...].astype(F32).reshape(1, -1)


def run_prepare(place, ids, dead, replace, latents, w1, vectors, owners):
    codes = dead.shape[1]
    pixels, width = latents.shape
    ch = w1.shape[1]
    rows = shape_of((owners, DEAD // (2 * owners), width), BF)
    return pl.pallas_call(
        prepare_body,
        name="prepare",
        in_specs=[SMEM] + [HBM] * (5 + len(vectors)),
        out_specs=[VMEM] * 6,
        out_shape=[
            shape_of((8, codes), F32), shape_of((DEAD, codes), BF), rows, rows,
            shape_of((16, ch), F32), shape_of(w1.shape, BF),
        ],
        scratch_shapes=[pltpu.VMEM((ch,), BF)] * len(vectors)
        + [
            pltpu.VMEM((1, pixels), jnp.int32), pltpu.VMEM((1, codes), jnp.int32), pltpu.VMEM((1, codes), jnp.int32),
            pltpu.VMEM((pixels, width), BF), pltpu.SemaphoreType.DMA((5 + len(vectors),)), pltpu.SMEM((1,), jnp.int32),
        ],
        cost_estimate=took(2.2),
        compiler_params=pltpu.CompilerParams(vmem_limit_bytes=16 << 20),
    )(place, *[hbm(v) for v in (ids, dead, replace, latents, w1, *vectors)])


def spread_all(place_ref, pieces, buf, sem, taps_out, outs, start=0):
    core = place_ref[0]
    ats = (place_ref[4], place_ref[5])
    copies = []
    step = 0
    for piece, beyond, far in pieces:
        owners = piece.shape[0]
        _, groups, rows, cols = buf.shape
        high = core ^ beyond
        for j in range(owners):
            buf[step] = piece[j, start : start + groups * rows, :].astype(F32).reshape(groups, rows, cols)
            at = pl.ds(pl.multiple_of(((j + far * owners) ^ ats[beyond]) * rows, rows), rows)
            to = pl.ds(pl.multiple_of(high * cols, cols), cols)
            if taps_out is None:
                new = [pltpu.make_async_copy(buf.at[step, g], out.at[at, to], sem) for g, out in enumerate(outs)]
            else:
                new = [pltpu.make_async_copy(buf.at[step], taps_out.at[:, at, to], sem)]
            for c in new:
                c.start()
            copies += new
            step += 1
    for c in copies:
        c.wait()


def attention_finish_body(place_ref, mine0, other0, mine1, other1, slots_ref, book_ref, *refs):
    *outs, out_ref, rows_ref, buf, sem = refs
    device = place_ref[3]
    pieces = ((mine0, 0, 0), (other0, 1, 0), (mine1, 0, 1), (other1, 1, 1))
    entries, width = book_ref.shape
    owners, total, _ = mine0.shape
    count = DEAD // (4 * owners)
    start = total - count
    rows_ref[:, width:] = jnp.ones((DEAD, 128), F32)
    for n, piece in enumerate((mine0, mine1, other0, other1)):
        for j in range(owners):
            at = (n * owners + j) * count
            rows_ref[at : at + count, :width] = piece[j, start:, :].astype(F32)
    whole = mm(slots_ref[...], rows_ref[...].astype(BF), TN)
    codes = whole.shape[0]
    pick = lax.broadcasted_iota(jnp.int32, (entries, codes), 1) - device * entries
    pick = jnp.where(pick == lax.broadcasted_iota(jnp.int32, (entries, codes), 0), 1.0, 0.0).astype(BF)
    own = mm(pick, whole.astype(BF))
    out_ref[...] = jnp.where(own[:, width : width + 1] > 0.5, own[:, :width], book_ref[...])
    spread_all(place_ref, pieces, buf, sem, None, outs, start - buf.shape[1] * buf.shape[2])


def run_attention_finish(place, pieces, slots, book, ch):
    owners, total, half = pieces[0].shape
    rows = ch // (2 * owners)
    width = book.shape[1]
    return pl.pallas_call(
        attention_finish_body,
        name="attention_finish",
        in_specs=[SMEM] + [VMEM] * 6,
        out_specs=[HBM] * 4 + [VMEM],
        out_shape=[shape_of((ch, ch), F32)] * 4 + [shape_of(book.shape, F32)],
        scratch_shapes=[
            pltpu.VMEM((DEAD, width + 128), F32),
            pltpu.VMEM((4 * owners, 4, rows, half), F32),
            pltpu.SemaphoreType.DMA(()),
        ],
        cost_estimate=took(3),
        compiler_params=pltpu.CompilerParams(vmem_limit_bytes=12 << 20),
    )(place, *pieces, slots, book)


def conv_finish_body(place_ref, mine, other, *refs, far):
    out_ref, buf, sem = refs[-3:]
    spread_all(place_ref, ((mine, 0, far), (other, 1, far)), buf, sem, out_ref, ())


def run_conv_finish(place, mine, other, into, ch, name):
    owners, total, half = mine.shape
    rows = ch // (2 * owners)
    given = [] if into is None else [into]
    return pl.pallas_call(
        functools.partial(conv_finish_body, far=len(given)),
        name=name,
        in_specs=[SMEM] + [VMEM] * 2 + [HBM] * len(given),
        out_specs=HBM,
        out_shape=shape_of((9, ch, ch), F32),
        scratch_shapes=[pltpu.VMEM((2 * owners, 9, rows, half), F32), pltpu.SemaphoreType.DMA(())],
        input_output_aliases={3: 0} if given else {},
        cost_estimate=took(3.5),
        compiler_params=pltpu.CompilerParams(vmem_limit_bytes=12 << 20),
    )(place, mine, other, *given)


def together(*values):
    return lax.optimization_barrier(values)


def vectors_body(sums_ref, *outs):
    *vectors, usage_ref, perplexity_ref = outs
    for i, out in enumerate(vectors):
        out[...] = sums_ref[i : i + 1, :]
    codes = usage_ref.shape[1]
    width = sums_ref.shape[1]
    first = len(vectors)
    counts = jnp.concatenate([sums_ref[first + i : first + i + 1, :] for i in range(codes // width)], axis=1)
    usage_ref[...] = counts.astype(jnp.int32)
    share = counts / jnp.sum(counts, axis=1, keepdims=True)
    entropy = jnp.sum(share * jnp.log(share + 1e-10), axis=1, keepdims=True)
    perplexity_ref[...] = jnp.exp(-entropy)


def run_vectors(sums, vectors, codes):
    ch = sums.shape[1]
    return pl.pallas_call(
        vectors_body,
        name="vectors",
        in_specs=[VMEM],
        out_specs=[VMEM] * (vectors + 2),
        cost_estimate=took(1.4),
        out_shape=[shape_of((1, ch), F32)] * vectors + [shape_of((1, codes), jnp.int32), shape_of((1, 1), F32)],
    )(sums)


class Links:
    def __init__(self, chips):
        self.chips = chips
        bits = chips.bit_length() - 1
        self.low = 1 if bits < 6 else 2
        sizes = [self.low - 1, self.low, bits - 2 * self.low]
        shifts = [1, self.low, 2 * self.low]
        self.dims = [(shift, size) for shift, size in zip(shifts, sizes) if size > 0]
        self.rest = bits - 1

    def swapped(self, index):
        mask = (1 << self.low) - 1
        first, second = index & mask, (index >> self.low) & mask
        return ((index >> (2 * self.low)) << (2 * self.low)) | (first << self.low) | second

    def flat(self, index):
        total = index & 1
        for shift, size in self.dims:
            total = (total << size) | ((index >> shift) & ((1 << size) - 1))
        return total

    def key(self, key, core):
        return self.swapped(key) if core else key

    def send(self, value, key):
        pairs = [(g * 2 + c, (g ^ self.key(key, c)) * 2 + c) for g in range(self.chips) for c in range(2)]
        return lax.ppermute(value, AXES, pairs)

    def partner(self, value):
        pairs = [(g * 2 + c, g * 2 + 1 - c) for g in range(self.chips) for c in range(2)]
        return lax.ppermute(value, AXES, pairs)

    def far(self, value):
        pairs = [(g * 2 + c, (g ^ self.key(1, 1 - c)) * 2 + 1 - c) for g in range(self.chips) for c in range(2)]
        return lax.ppermute(value, AXES, pairs)

    def reduce(self, value, dim, keep=None):
        shift, size = self.dims[dim]
        got = [self.send(value[k], k << shift) for k in range(1, 1 << size)]
        total = (value if keep is None else keep)[0].astype(F32)
        for g in got:
            total = total + g.astype(F32)
        return total.astype(BF)

    def gather(self, value, dim):
        shift, size = self.dims[dim]
        return jnp.stack([value] + [self.send(value, k << shift) for k in range(1, 1 << size)])

    def lead(self):
        return tuple(1 << size for _, size in self.dims)

    def small_steps(self):
        steps = [lambda value: value + self.partner(value)]
        for bit in range(self.chips.bit_length() - 1):
            steps.append(lambda value, key=1 << bit: value + self.send(value, key))
        return steps


def local(
    image_rows, grad_out, code_ids, dead_flags, replace_ids, latents, codebook,
    norm1_gain, norm1_bias, conv1_kernel, conv1_bias, norm2_gain, norm2_bias, conv2_kernel, conv2_bias,
    norm3_gain, norm3_bias, query_weight, query_bias, key_weight, value_weight, value_bias, out_weight, out_bias,
    *, chips,
):
    links = Links(chips)
    owners = chips
    all_images, part_rows, side, ch = image_rows.shape
    images = all_images // 2
    px = grad_out.shape[1] * side
    part = part_rows * side
    core = lax.axis_index("row").astype(jnp.int32)
    chip = lax.axis_index("grp").astype(jnp.int32)
    device = chip * 2 + core
    as_first, as_second = links.flat(chip), links.flat(links.swapped(chip))
    mine_at = jnp.where(core == 0, as_first, as_second)
    other_at = jnp.where(core == 0, as_second, as_first)
    low = owners // 2
    place = jnp.stack([
        core, chip, device * latents.shape[0], device, mine_at, other_at,
        mine_at // low, other_at // low, mine_at % low,
    ])
    mine = image_rows.reshape(all_images, part, ch)
    other = links.partner(lax.dynamic_slice_in_dim(mine, (1 - core) * images, images))
    vectors = [
        norm1_gain, norm1_bias, conv1_bias, norm2_gain, norm2_bias, conv2_bias,
        norm3_gain, norm3_bias, query_bias, value_bias, out_bias,
    ]
    codes = dead_flags.shape[0]
    counts, slots, ckeep, csend, vec, w1 = run_prepare(
        place, code_ids.reshape(1, -1), dead_flags.reshape(1, -1), replace_ids.reshape(1, -1), latents,
        conv1_kernel.reshape(9 * ch, ch), vectors, owners,
    )
    own, to_chip, to_near, to_far, norm2, scale2, x, gy, w2, *weights = run_entry(
        place, mine, other, vec, w1, grad_out.reshape(images, px, ch), conv2_kernel.reshape(9 * ch, ch),
        (query_weight, key_weight, value_weight, out_weight), side,
    )
    acts = [own, links.partner(to_chip), links.send(to_near, 1), links.far(to_far)]
    out, dres, dkeep2, dsend2, stat_a, gkeep, gsend = run_attention(
        place, x, own, to_near, gy, ckeep, csend, vec, [w2] + weights, side
    )
    dres, dkeep2, dsend2, gsend, *acts[1:] = together(dres, dkeep2, dsend2, gsend, *acts[1:])
    grads2 = [dkeep2, links.partner(dsend2), links.send(dkeep2, 1), links.far(dsend2)]
    attn = (gkeep.astype(F32) + links.partner(gsend).astype(F32)).astype(BF)
    attn = attn.reshape((2, low) + attn.shape[1:])
    attn_keep, attn_send, dres = together(attn[0], attn[1], dres)
    attn_got = links.send(attn_send, 1)
    dkeep1, dsend1, dfull1, stat_b = run_back2(place, dres, norm2, scale2, vec, w2, side)
    grads2[0], stat_b = together(grads2[0], stat_b)
    grads1 = [dkeep1, links.partner(dsend1), links.send(dkeep1, 1), links.far(dsend1)]
    lead = links.lead()
    rest = range(1, len(lead))
    split = (lead[0], low // lead[0])

    def reduce(value, dims):
        for dim in dims:
            value = links.reduce(value, dim)
        return value

    def gather(value, dims):
        for dim in reversed(dims):
            value = links.gather(value, dim)
        return value

    def owned(value):
        return value.reshape((low,) + value.shape[-2:])

    sum2 = run_kernel_grad(place, 1, acts, grads2, split, side, "conv2_grad")
    sum2_keep, attn_got, grads1[0] = together(sum2, attn_got, grads1[0])
    sum1 = run_kernel_grad(place, 0, acts, grads1, split, side, "conv1_grad")
    attn = (attn_keep.astype(F32) + attn_got.astype(F32)).astype(BF)
    attn = attn.reshape(lead + attn.shape[1:])
    sum2 = sum2.reshape(lead + sum2.shape[2:])
    sum2_keep = sum2_keep.reshape(sum2.shape)
    sum1 = sum1.reshape(lead + sum1.shape[2:])
    attn = reduce(attn, [0])
    sum2 = links.reduce(sum2, 0, sum2_keep)
    attn, sum2, sum1, dfull1 = together(attn, sum2, sum1, dfull1)
    conv_rows = sum2.shape[-2]
    sum2 = reduce(jnp.concatenate([sum2, attn], axis=-2), rest)
    sum1 = reduce(sum1, [0])
    rows_out, in_send, stat_c = run_back1(place, dfull1, x, dres, vec, w1, side)
    sum2, sum1, in_send, stat_c = together(sum2, sum1, in_send, stat_c)
    vectors = jnp.concatenate([stat_c[:2], stat_b[2:3], stat_b[:2], stat_a[:6], counts[:1].reshape(-1, ch)])
    steps = links.small_steps()
    sum2 = gather(sum2, rest)
    in_got = links.partner(in_send)
    vectors = steps[0](vectors)
    sum2, sum1, in_got, vectors = together(sum2, sum1, in_got, vectors)
    sum2 = owned(gather(sum2, [0]))
    sum1 = reduce(sum1, rest)
    vectors = steps[1](vectors)
    input_grad, _ = run_place_rows(place, in_got, rows_out)
    sum2, sum1, vectors, input_grad = together(sum2, sum1, vectors, input_grad)
    far2 = links.send(sum2, 1)
    other2 = links.partner(sum2)
    sum1 = gather(sum1, rest)
    vectors = steps[2](vectors)
    grad2 = run_conv_finish(place, sum2, other2, None, ch, "conv2_finish")
    far2, sum1, vectors, grad2 = together(far2, sum1, vectors, grad2)
    sum1 = owned(gather(sum1, [0]))
    other_far2 = links.partner(far2)
    vectors = steps[3](vectors)
    sum1, vectors, other_far2 = together(sum1, vectors, other_far2)
    far1 = links.send(sum1, 1)
    other1 = links.partner(sum1)
    for step in steps[4:]:
        vectors = step(vectors)
    qg, kg, vg, og, new_codebook = run_attention_finish(
        place, (sum2, other2, far2, other_far2), slots, codebook, ch
    )
    grad2 = run_conv_finish(place, far2, other_far2, grad2, ch, "conv2_finish")
    grad1 = run_conv_finish(place, sum1, other1, None, ch, "conv1_finish")
    *vec_grads, usage, perplexity = run_vectors(vectors, 11, codes)
    (g1, b1, cb1, g2, b2, cb2, g3, b3, qb, vb, ob) = [v.reshape(ch) for v in vec_grads]
    far1, grad2, grad1, perplexity, new_codebook = together(far1, grad2, grad1, perplexity, new_codebook)
    grad1 = run_conv_finish(place, far1, links.partner(far1), grad1, ch, "conv1_finish")
    input_grad = input_grad.reshape(image_rows.shape)
    kernel_shape = (3, 3, ch, ch)
    return (
        out.reshape(grad_out.shape), input_grad,
        g1, b1, grad1.reshape(kernel_shape), cb1, g2, b2, grad2.reshape(kernel_shape), cb2, g3, b3,
        qg, qb, kg, vg, vb, og, ob,
        new_codebook, usage.reshape(codes), perplexity.reshape(()),
    )


def solution(mesh):
    both = ("grp", "row")
    in_specs = (
        P("grp", "row", None, None), P(both, None, None, None), P(both), P(), P(), P(both, None), P(both, None),
    ) + (P(),) * 17
    out_specs = (P(both, None, None, None), P("grp", "row", None, None)) + (P(),) * 17 + (P(both, None), P(), P())
    body = functools.partial(local, chips=mesh.shape["grp"])
    return jax.shard_map(body, mesh=mesh, in_specs=in_specs, out_specs=out_specs, check_vma=False)
```

```python
import functools

import jax
import jax.numpy as jnp
from jax import lax
from jax.experimental import pallas as pl
from jax.experimental.pallas import tpu as pltpu
from jax.sharding import PartitionSpec as P

EPS = 1e-06
GROUP = 16
LANES = 128
DEAD = 256
AXES = ("grp", "row")
F32 = jnp.float32
BF = jnp.bfloat16
NN = (((1,), (0,)), ((), ()))
NT = (((1,), (1,)), ((), ()))
TN = (((0,), (0,)), ((), ()))
VMEM = pl.BlockSpec(memory_space=pltpu.VMEM)
SMEM = pl.BlockSpec(memory_space=pltpu.SMEM)
HBM = pl.BlockSpec(memory_space=pltpu.HBM)
shape_of = jax.ShapeDtypeStruct


def took(us):
    return pl.CostEstimate(flops=int(us * 1.15e9), bytes_accessed=1 << 20, transcendentals=0)


def hbm(value):
    return pltpu.with_memory_space_constraint(value, pltpu.HBM)


def mm(a, b, dims=NN):
    return lax.dot_general(a, b, dims, preferred_element_type=F32)


def colsum(v):
    return jnp.sum(v, axis=0, keepdims=True)


def group_sums(rows):
    chunks = rows[0].shape[1] // LANES
    v = jnp.concatenate([r[:, c * LANES : (c + 1) * LANES] for r in rows for c in range(chunks)], axis=0)
    lane = lax.broadcasted_iota(jnp.int32, v.shape, 1)
    step = 1
    while step < GROUP:
        below = pltpu.roll(v, step, 1)
        above = pltpu.roll(v, LANES - step, 1)
        v = v + jnp.where((lane & step) != 0, below, above)
        step *= 2
    return [
        jnp.concatenate([v[k * chunks + c : k * chunks + c + 1] for c in range(chunks)], axis=1)
        for k in range(len(rows))
    ]


def normalized(images):
    count = images[0].shape[0] * GROUP
    middles = group_sums([colsum(v) for v in images])
    centered = [v - m / count for v, m in zip(images, middles)]
    spreads = group_sums([colsum(c * c) for c in centered])
    scales = [lax.rsqrt(v / count + EPS) for v in spreads]
    return [(c * r, r) for c, r in zip(centered, scales)]


def norm_back(images, gain):
    count = images[0][0].shape[0] * GROUP
    bias_grads = [colsum(dy) for _, _, dy in images]
    gain_grads = [colsum(dy * n) for n, _, dy in images]
    sums = group_sums([g * gain for g in bias_grads] + [g * gain for g in gain_grads])
    total = len(images)
    dxs = [
        r * (dy * gain - sums[i] / count - n * (sums[total + i] / count)) for i, (n, r, dy) in enumerate(images)
    ]
    return dxs, sum(gain_grads), sum(bias_grads)


def sigmoid(y):
    return 1.0 / (1.0 + jnp.exp(-y))


def shifted(v, side):
    px = v.shape[0]
    col = lax.broadcasted_iota(jnp.int32, v.shape, 0) % side
    left = jnp.where(col == 0, 0.0, pltpu.roll(v, 1, 0))
    right = jnp.where(col == side - 1, 0.0, pltpu.roll(v, px - 1, 0))
    return left, v, right


def put_shifts(s_ref, image, v, side):
    px, ch = v.shape
    for j, t in enumerate(shifted(v, side)):
        s_ref[image, side : px + side, j * ch : (j + 1) * ch] = t.astype(BF)


def clear_edges(s_ref, side):
    images, rows, width = s_ref.shape
    zero = jnp.zeros((side, width), BF)
    for i in range(images):
        s_ref[i, 0:side, :] = zero
        s_ref[i, rows - side : rows, :] = zero


def window(s_ref, first, px, cols):
    return jnp.concatenate([s_ref[i, first : first + px, cols] for i in range(s_ref.shape[0])], axis=0)


def conv(s_ref, w_ref, px, side, ch):
    acc = None
    for dh in range(3):
        part = mm(window(s_ref, dh * side, px, slice(None)), w_ref[dh * 3 * ch : (dh + 1) * 3 * ch, :])
        acc = part if acc is None else acc + part
    return acc


def conv_back(s_ref, w_ref, px, side, ch):
    acc = None
    for dh in range(3):
        for dw in range(3):
            tap = dh * 3 + dw
            cols = slice((2 - dw) * ch, (3 - dw) * ch)
            part = mm(window(s_ref, (2 - dh) * side, px, cols), w_ref[tap * ch : (tap + 1) * ch, :], NT)
            acc = part if acc is None else acc + part
    return acc


def split_cols(v, bit):
    half = v.shape[1] // 2
    low, high = v[:, :half], v[:, half:]
    return jnp.where(bit == 0, low, high), jnp.where(bit == 0, high, low)


def start_copies(pairs, sems):
    copies = [pltpu.make_async_copy(a, b, sems.at[i]) for i, (a, b) in enumerate(pairs)]
    for c in copies:
        c.start()
    return copies


def entry_body(
    place_ref, mine_hbm, other_ref, vec_ref, w1, gy_hbm, w2_hbm, wq_hbm, wk_hbm, wv_hbm, wo_hbm,
    own_ref, chip_ref, near_ref, far_ref, norm2_ref, scale2_ref, x_ref, gy_ref, w2, wq, wk, wv, wo, s_ref, sems, *, side,
):
    images, px, ch = x_ref.shape
    part = px // 2
    core = place_ref[0]
    bit, other_bit = place_ref[6], place_ref[7]
    here = pl.multiple_of(core * part, part)
    there = pl.multiple_of((1 - core) * part, part)
    copies = start_copies(
        [(mine_hbm.at[core * images + i], x_ref.at[i, pl.ds(here, part)]) for i in range(images)]
        + [(w2_hbm, w2), (gy_hbm, gy_ref), (wq_hbm, wq), (wk_hbm, wk), (wv_hbm, wv), (wo_hbm, wo)],
        sems,
    )

    def row(i):
        return vec_ref[i : i + 1, :]

    def give(which, a):
        for i in range(images):
            low = a[i].astype(BF)
            own_ref[which, i], near_ref[which, i] = split_cols(low, bit)
            chip_ref[which, i], far_ref[which, i] = split_cols(low, other_bit)

    clear_edges(s_ref, side)
    for i in range(images):
        x_ref[i, pl.ds(there, part), :] = other_ref[i]
    for c in copies[:images]:
        c.wait()
    active = []
    for i, (n, _) in enumerate(normalized([x_ref[i].astype(F32) for i in range(images)])):
        y = n * row(0) + row(1)
        active.append(y * sigmoid(y))
        put_shifts(s_ref, i, active[i], side)
    give(0, active)
    filtered = conv(s_ref, w1, px, side, ch) + row(2)
    active = []
    for i, (n, r) in enumerate(normalized([filtered[i * px : (i + 1) * px] for i in range(images)])):
        norm2_ref[i] = n
        scale2_ref[i : i + 1, :] = r
        y = n * row(3) + row(4)
        active.append(y * sigmoid(y))
    give(1, active)
    for c in copies[images:]:
        c.wait()


def run_entry(place, mine, other, vec, w1, gy, w2, weights, side):
    images, part, ch = other.shape
    px = 2 * part
    acts = shape_of((2, images, px, ch // 2), BF)
    whole = (images, px, ch)
    return pl.pallas_call(
        functools.partial(entry_body, side=side),
        name="entry",
        in_specs=[SMEM, HBM] + [VMEM] * 3 + [HBM] * 6,
        out_specs=[VMEM] * 13,
        out_shape=[acts] * 4
        + [shape_of(whole, F32), shape_of((images, ch), F32), shape_of(whole, BF), shape_of(whole, BF), shape_of(w2.shape, BF)]
        + [shape_of((ch, ch), BF)] * 4,
        scratch_shapes=[
            pltpu.VMEM((images, px + 2 * side, 3 * ch), BF),
            pltpu.SemaphoreType.DMA((images + 6,)),
        ],
        cost_estimate=took(8.5),
        compiler_params=pltpu.CompilerParams(vmem_limit_bytes=12 << 20),
    )(place, hbm(mine), other, vec, w1, *[hbm(v) for v in (gy, w2, *weights)])


def attention_body(
    place_ref, x_ref, own_ref, near_ref, gy_ref, ckeep_ref, csend_ref, vec_ref, w2, wq, wk, wv, wo,
    out_ref, dres_ref, dkeep_ref, dsend_ref, stat_ref, gkeep_ref, gsend_ref,
    s_ref, norm_ref, normed, qkv, mixed, *, side,
):
    images, px, ch = x_ref.shape
    core = place_ref[0]
    bit = place_ref[6]

    def row(i):
        return vec_ref[i : i + 1, :]

    every = range(images)
    clear_edges(s_ref, side)
    for i in every:
        mine, other = own_ref[1, i], near_ref[1, i]
        a = jnp.concatenate([jnp.where(bit == 0, mine, other), jnp.where(bit == 0, other, mine)], axis=1)
        put_shifts(s_ref, i, a.astype(F32), side)

    def flat(ref):
        return ref[...].reshape(images * px, ch)

    def spans(v):
        return [v[i * px : (i + 1) * px] for i in every]

    dm = mm(flat(gy_ref), wo[...], NT).astype(BF)
    branch = conv(s_ref, w2, px, side, ch) + row(5)
    res = [x_ref[i].astype(F32) + b for i, b in zip(every, spans(branch))]
    scales = []
    for i, (n, r) in enumerate(normalized(res)):
        dres_ref[i] = res[i]
        norm_ref[i] = n
        scales.append(r)
        normed[i] = (n * row(6) + row(7)).astype(BF)
    nb = flat(normed)
    queries = (mm(nb, wq[...]) + row(8)).astype(BF)
    keys = mm(nb, wk[...]).astype(BF)
    values = (mm(nb, wv[...]) + row(9)).astype(BF)
    scale = ch ** -0.5
    for i, qi, ki, vi, di in zip(every, spans(queries), spans(keys), spans(values), spans(dm)):
        scores = mm(qi, ki, NT) * scale
        dp = mm(di, vi, NT)
        peak = jnp.max(scores, axis=1, keepdims=True)
        lifted = jnp.exp(scores - peak)
        probs = lifted / jnp.sum(lifted, axis=1, keepdims=True)
        pb = probs.astype(BF)
        mixed[i] = mm(pb, vi).astype(BF)
        qkv[i, :, 2 * ch :] = mm(pb, di, TN).astype(BF)
        ds = (probs * (dp - jnp.sum(probs * dp, axis=1, keepdims=True))).astype(BF)
        qkv[i, :, :ch] = (mm(ds, ki) * scale).astype(BF)
        qkv[i, :, ch : 2 * ch] = (mm(ds, qi, TN) * scale).astype(BF)
    cotangents = qkv[...].reshape(images * px, 3 * ch)
    dq, dk, dv = [cotangents[:, j * ch : (j + 1) * ch] for j in range(3)]
    dn = mm(dq, wq[...], NT) + mm(dk, wk[...], NT) + mm(dv, wv[...], NT)
    projected = mm(flat(mixed), wo[...]) + row(10)
    for i, p in zip(every, spans(projected)):
        out_ref[i] = (dres_ref[i] + p).astype(BF)
    dxs, gain_grad, bias_grad = norm_back(
        [(norm_ref[i], r, d) for i, r, d in zip(every, scales, spans(dn))], row(6)
    )
    total = jnp.zeros((1, ch), F32)
    for i, dx in zip(every, dxs):
        dres = gy_ref[i].astype(F32) + dx
        dres_ref[i] = dres
        db = dres.astype(BF)
        dkeep_ref[i], dsend_ref[i] = split_cols(db, core)
        total = total + colsum(db.astype(F32))
    stat_ref[...] = jnp.zeros(stat_ref.shape, F32)
    stat_ref[0:1, :] = total
    stat_ref[1:2, :] = gain_grad
    stat_ref[2:3, :] = bias_grad
    stat_ref[3:4, :] = colsum(dq.astype(F32))
    stat_ref[4:5, :] = colsum(dv.astype(F32))
    stat_ref[5:6, :] = colsum(flat(gy_ref).astype(F32))
    owners = gkeep_ref.shape[0]
    rows = ch // owners
    mine_at, other_at = place_ref[4], place_ref[5]
    whole = mm(flat(normed), cotangents, TN)
    grads = [whole[:, j * ch : (j + 1) * ch] for j in range(3)] + [mm(flat(mixed), flat(gy_ref), TN)]
    for j, g in enumerate(grads):
        keep, send = split_cols(g.astype(BF), core)
        for o in range(owners):
            gkeep_ref[o ^ mine_at, j * rows : (j + 1) * rows] = keep[o * rows : (o + 1) * rows]
            gsend_ref[o ^ other_at, j * rows : (j + 1) * rows] = send[o * rows : (o + 1) * rows]
    for o in range(owners):
        gkeep_ref[o, 4 * rows :] = ckeep_ref[o]
        gsend_ref[o, 4 * rows :] = csend_ref[o]


def run_attention(place, x, own, near, gy, ckeep, csend, vec, weights, side):
    images, px, ch = gy.shape
    half = ch // 2
    owners, count, _ = ckeep.shape
    rows = 4 * (ch // owners) + count
    whole = (images, px, ch)
    return pl.pallas_call(
        functools.partial(attention_body, side=side),
        name="attention",
        in_specs=[SMEM] + [VMEM] * 12,
        out_specs=[VMEM] * 7,
        out_shape=[
            shape_of(whole, BF), shape_of(whole, F32),
            shape_of((images, px, half), BF), shape_of((images, px, half), BF),
            shape_of((8, ch), F32),
            shape_of((owners, rows, half), BF), shape_of((owners, rows, half), BF),
        ],
        scratch_shapes=[pltpu.VMEM((images, px + 2 * side, 3 * ch), BF), pltpu.VMEM(whole, F32)]
        + [pltpu.VMEM(whole, BF), pltpu.VMEM((images, px, 3 * ch), BF), pltpu.VMEM(whole, BF)],
        cost_estimate=took(13.5),
        compiler_params=pltpu.CompilerParams(vmem_limit_bytes=20 << 20),
    )(place, x, own, near, gy, ckeep, csend, vec, *weights)


def swish_back(da, ns, gain, bias):
    dys = []
    for d, n in zip(da, ns):
        y = n * gain + bias
        sig = sigmoid(y)
        dys.append(d * (sig * (1.0 + y * (1.0 - sig))))
    return dys


def back2_body(
    place_ref, dres_ref, norm2_ref, scale2_ref, vec_ref, w2,
    dkeep_ref, dsend_ref, dfull_ref, stat_ref, s_ref, *, side,
):
    images, px, ch = dres_ref.shape
    every = range(images)
    core = place_ref[0]
    clear_edges(s_ref, side)

    def row(i):
        return vec_ref[i : i + 1, :]

    for i in every:
        put_shifts(s_ref, i, dres_ref[i], side)
    da = conv_back(s_ref, w2, px, side, ch)
    ns = [norm2_ref[i] for i in every]
    dys = swish_back([da[i * px : (i + 1) * px] for i in every], ns, row(3), row(4))
    dxs, gain_grad, bias_grad = norm_back(
        [(n, scale2_ref[i : i + 1, :], dy) for i, n, dy in zip(every, ns, dys)], row(3)
    )
    total = jnp.zeros((1, ch), F32)
    for i, dx in zip(every, dxs):
        db = dx.astype(BF)
        dfull_ref[i] = db
        dkeep_ref[i], dsend_ref[i] = split_cols(db, core)
        total = total + colsum(db.astype(F32))
    stat_ref[...] = jnp.zeros(stat_ref.shape, F32)
    stat_ref[0:1, :] = gain_grad
    stat_ref[1:2, :] = bias_grad
    stat_ref[2:3, :] = total


def run_back2(place, dres, norm2, scale2, vec, w2, side):
    images, px, ch = dres.shape
    half = (images, px, ch // 2)
    return pl.pallas_call(
        functools.partial(back2_body, side=side),
        name="conv2_back",
        in_specs=[SMEM] + [VMEM] * 5,
        out_specs=[VMEM] * 4,
        out_shape=[shape_of(half, BF), shape_of(half, BF), shape_of((images, px, ch), BF), shape_of((8, ch), F32)],
        scratch_shapes=[pltpu.VMEM((images, px + 2 * side, 3 * ch), BF)],
        cost_estimate=took(5),
        compiler_params=pltpu.CompilerParams(vmem_limit_bytes=12 << 20),
    )(place, dres, norm2, scale2, vec, w2)


def back1_body(
    place_ref, dfull_ref, x_ref, dres_ref, vec_ref, w1,
    out_hbm, send_ref, stat_ref, s_ref, keep_ref, sem, *, side,
):
    images, px, ch = dres_ref.shape
    part = px // 2
    core = place_ref[0]
    every = range(images)
    clear_edges(s_ref, side)

    def row(i):
        return vec_ref[i : i + 1, :]

    for i in every:
        put_shifts(s_ref, i, dfull_ref[i].astype(F32), side)
    da = conv_back(s_ref, w1, px, side, ch)
    norms = normalized([x_ref[i].astype(F32) for i in every])
    ns = [n for n, _ in norms]
    dys = swish_back([da[i * px : (i + 1) * px] for i in every], ns, row(0), row(1))
    dxs, gain_grad, bias_grad = norm_back([(n, r, dy) for (n, r), dy in zip(norms, dys)], row(0))
    for i, dx in zip(every, dxs):
        total = (dres_ref[i] + dx).astype(BF)
        low, high = total[:part], total[part:]
        keep_ref[i] = jnp.where(core == 0, low, high)
        send_ref[i] = jnp.where(core == 0, high, low)
    stat_ref[...] = jnp.zeros(stat_ref.shape, F32)
    stat_ref[0:1, :] = gain_grad
    stat_ref[1:2, :] = bias_grad
    copy = pltpu.make_async_copy(keep_ref, out_hbm.at[pl.ds(core * images, images)], sem)
    copy.start()
    copy.wait()


def run_back1(place, dfull, x, dres, vec, w1, side):
    images, px, ch = dres.shape
    part = (images, px // 2, ch)
    return pl.pallas_call(
        functools.partial(back1_body, side=side),
        name="conv1_back",
        in_specs=[SMEM] + [VMEM] * 5,
        out_specs=[HBM, VMEM, VMEM],
        out_shape=[shape_of((2 * images, px // 2, ch), BF), shape_of(part, BF), shape_of((8, ch), F32)],
        scratch_shapes=[
            pltpu.VMEM((images, px + 2 * side, 3 * ch), BF),
            pltpu.VMEM(part, BF),
            pltpu.SemaphoreType.DMA(()),
        ],
        cost_estimate=took(0.1),
        compiler_params=pltpu.CompilerParams(vmem_limit_bytes=12 << 20),
    )(place, dfull, x, dres, vec, w1)


def place_rows_body(place_ref, got_ref, into_hbm, out_hbm, token_ref, sem):
    images = got_ref.shape[0]
    token_ref[...] = jnp.zeros(token_ref.shape, F32)
    copy = pltpu.make_async_copy(got_ref, out_hbm.at[pl.ds((1 - place_ref[0]) * images, images)], sem)
    copy.start()
    copy.wait()


def run_place_rows(place, got, into):
    return pl.pallas_call(
        place_rows_body,
        name="place_rows",
        in_specs=[SMEM, VMEM, HBM],
        out_specs=[HBM, VMEM],
        out_shape=[shape_of(into.shape, BF), shape_of((8, 128), F32)],
        scratch_shapes=[pltpu.SemaphoreType.DMA(())],
        input_output_aliases={2: 0},
        cost_estimate=took(1),
        compiler_params=pltpu.CompilerParams(vmem_limit_bytes=4 << 20),
    )(place, got, into)


def turn(a, i, s_ref, at, side):
    px, part = a.shape[-2:]
    for j, t in enumerate(shifted(a[i].astype(F32), side)):
        s_ref[j * part : (j + 1) * part, pl.ds(pl.multiple_of(at * px, px), px)] = t.astype(BF).T


def turn_body(*refs, side, which):
    *acts, s_ref = refs
    images = acts[0].shape[1]
    for n, a in enumerate(acts):

        def fill(i, carry, a=a, n=n):
            turn(a.at[which], i, s_ref, n * images + i, side)
            return carry

        lax.fori_loop(0, images, fill, 0)


def run_turn(which, acts, side):
    _, images, px, part = acts[0].shape
    return pl.pallas_call(
        functools.partial(turn_body, side=side, which=which),
        name="turn",
        in_specs=[VMEM] * 4,
        out_specs=VMEM,
        out_shape=shape_of((3 * part, 4 * images * px), BF),
        cost_estimate=took(2),
        compiler_params=pltpu.CompilerParams(vmem_limit_bytes=6 << 20),
    )(*acts)


def kernel_grad_body(place_ref, s_ref, *refs, side):
    *grads, out_ref, d_ref = refs
    images, px, half = grads[0].shape
    part = s_ref.shape[0] // 3
    bits = place_ref[8]
    first, second, _, _ = out_ref.shape
    owners = first * second
    rows = part // owners
    zero = jnp.zeros((side, half), BF)
    for n, d in enumerate(grads):
        for i in range(images):
            d_ref[n * images + i, 0:side, :] = zero
            d_ref[n * images + i, side : px + side, :] = d[i]
            d_ref[n * images + i, px + side :, :] = zero
    for dh in range(3):
        start = (2 - dh) * side
        d = jnp.concatenate([d_ref[n, start : start + px, :] for n in range(4 * images)], axis=0)
        g = mm(s_ref[...], d).astype(BF)
        for o in range(owners):
            at = o ^ bits
            for dw in range(3):
                tap = dh * 3 + dw
                begin = dw * part + o * rows
                out_ref[at // second, at % second, tap * rows : (tap + 1) * rows, :] = g[begin : begin + rows]


def run_kernel_grad(place, turned, grads, lead, side, us, name):
    images, px, half = grads[0].shape
    part = turned.shape[0] // 3
    rows = 9 * (part // (lead[0] * lead[1]))
    return pl.pallas_call(
        functools.partial(kernel_grad_body, side=side),
        name=name,
        in_specs=[SMEM] + [VMEM] * 5,
        out_specs=VMEM,
        out_shape=shape_of((lead[0], lead[1], rows, half), BF),
        scratch_shapes=[pltpu.VMEM((4 * images, px + 2 * side, half), BF)],
        cost_estimate=took(us),
        compiler_params=pltpu.CompilerParams(vmem_limit_bytes=10 << 20),
    )(place, turned, *grads)


def prepare_body(place_ref, ids_hbm, dead_hbm, replace_hbm, latents_hbm, w1_hbm, *refs):
    count_vectors = (len(refs) - 12) // 2
    vectors = refs[:count_vectors]
    counts_ref, slots_ref, keep_ref, send_ref, vec_ref, w1_ref = refs[count_vectors : count_vectors + 6]
    lines = refs[count_vectors + 6 : 2 * count_vectors + 6]
    ids_ref, dead_ref, replace_ref, latents_ref, sems, _ = refs[2 * count_vectors + 6 :]
    copies = start_copies(
        (
            (ids_hbm, ids_ref), (dead_hbm, dead_ref), (replace_hbm, replace_ref), (latents_hbm, latents_ref),
            *zip(vectors, lines), (w1_hbm, w1_ref),
        ),
        sems,
    )
    core = place_ref[0]
    offset = place_ref[2]
    for c in copies[:2]:
        c.wait()
    codes = dead_ref.shape[1]
    pixels, width = latents_ref.shape
    one = jnp.ones((), BF)
    none = jnp.zeros((), BF)
    code = lax.broadcasted_iota(jnp.int32, (codes, pixels), 0)
    hit = jnp.where(code == ids_ref[...], one, none)
    counts_ref[...] = mm(jnp.ones((8, pixels), BF), hit, NT)
    dead = dead_ref[...]
    ahead = lax.broadcasted_iota(jnp.int32, (codes, codes), 0) <= lax.broadcasted_iota(jnp.int32, (codes, codes), 1)
    rank = mm(jnp.broadcast_to(dead.astype(F32), (8, codes)).astype(BF), jnp.where(ahead, one, none))[0:1]
    rank = jnp.where(dead == 1, rank.astype(jnp.int32) - 1, -1)
    owners, count, _ = keep_ref.shape
    at = lax.broadcasted_iota(jnp.int32, (DEAD, codes), 0)
    beyond = at // (owners * count)
    owner = ((at % (owners * count)) // count) ^ jnp.where(beyond == 0, place_ref[4], place_ref[5])
    at = (beyond ^ core) * (owners * count) + owner * count + at % count
    slot = at == rank
    slots_ref[...] = jnp.where(slot, one, none)
    for c in copies[2:4]:
        c.wait()
    wanted = jnp.sum(jnp.where(slot, replace_ref[...], 0), axis=1, keepdims=True) - offset
    pixel = lax.broadcasted_iota(jnp.int32, (DEAD, pixels), 1)
    rows = mm(jnp.where(pixel == wanted, one, none), latents_ref[...]).astype(BF)
    for j in range(owners):
        keep_ref[j] = rows[j * count : (j + 1) * count]
        send_ref[j] = rows[DEAD // 2 + j * count : DEAD // 2 + (j + 1) * count]
    for c in copies[4:]:
        c.wait()
    for i, line in enumerate(lines):
        vec_ref[i : i + 1, :] = line[...].astype(F32).reshape(1, -1)


def run_prepare(place, ids, dead, replace, latents, w1, vectors, owners):
    codes = dead.shape[1]
    pixels, width = latents.shape
    ch = w1.shape[1]
    rows = shape_of((owners, DEAD // (2 * owners), width), BF)
    return pl.pallas_call(
        prepare_body,
        name="prepare",
        in_specs=[SMEM] + [HBM] * (5 + len(vectors)),
        out_specs=[VMEM] * 6,
        out_shape=[
            shape_of((8, codes), F32), shape_of((DEAD, codes), BF), rows, rows,
            shape_of((16, ch), F32), shape_of(w1.shape, BF),
        ],
        scratch_shapes=[pltpu.VMEM((ch,), BF)] * len(vectors)
        + [
            pltpu.VMEM((1, pixels), jnp.int32), pltpu.VMEM((1, codes), jnp.int32), pltpu.VMEM((1, codes), jnp.int32),
            pltpu.VMEM((pixels, width), BF), pltpu.SemaphoreType.DMA((5 + len(vectors),)), pltpu.SMEM((1,), jnp.int32),
        ],
        cost_estimate=took(2.2),
        compiler_params=pltpu.CompilerParams(vmem_limit_bytes=16 << 20),
    )(place, *[hbm(v) for v in (ids, dead, replace, latents, w1, *vectors)])


def spread_all(place_ref, pieces, buf, sem, taps_out, outs, start=0):
    core = place_ref[0]
    ats = (place_ref[4], place_ref[5])
    copies = []
    step = 0
    for piece, beyond, far in pieces:
        owners = piece.shape[0]
        _, groups, rows, cols = buf.shape
        high = core ^ beyond
        for j in range(owners):
            buf[step] = piece[j, start : start + groups * rows, :].astype(F32).reshape(groups, rows, cols)
            at = pl.ds(pl.multiple_of(((j + far * owners) ^ ats[beyond]) * rows, rows), rows)
            to = pl.ds(pl.multiple_of(high * cols, cols), cols)
            if taps_out is None:
                new = [pltpu.make_async_copy(buf.at[step, g], out.at[at, to], sem) for g, out in enumerate(outs)]
            else:
                new = [pltpu.make_async_copy(buf.at[step], taps_out.at[:, at, to], sem)]
            for c in new:
                c.start()
            copies += new
            step += 1
    for c in copies:
        c.wait()


def attention_finish_body(place_ref, mine0, other0, mine1, other1, slots_ref, book_ref, *refs):
    *outs, out_ref, rows_ref, buf, sem = refs
    device = place_ref[3]
    pieces = ((mine0, 0, 0), (other0, 1, 0), (mine1, 0, 1), (other1, 1, 1))
    entries, width = book_ref.shape
    owners, total, _ = mine0.shape
    count = DEAD // (4 * owners)
    start = total - count
    rows_ref[:, width:] = jnp.ones((DEAD, 128), F32)
    for n, piece in enumerate((mine0, mine1, other0, other1)):
        for j in range(owners):
            at = (n * owners + j) * count
            rows_ref[at : at + count, :width] = piece[j, start:, :].astype(F32)
    whole = mm(slots_ref[...], rows_ref[...].astype(BF), TN)
    codes = whole.shape[0]
    pick = lax.broadcasted_iota(jnp.int32, (entries, codes), 1) - device * entries
    pick = jnp.where(pick == lax.broadcasted_iota(jnp.int32, (entries, codes), 0), 1.0, 0.0).astype(BF)
    own = mm(pick, whole.astype(BF))
    out_ref[...] = jnp.where(own[:, width : width + 1] > 0.5, own[:, :width], book_ref[...])
    spread_all(place_ref, pieces, buf, sem, None, outs, start - buf.shape[1] * buf.shape[2])


def run_attention_finish(place, pieces, slots, book, ch):
    owners, total, half = pieces[0].shape
    rows = ch // (2 * owners)
    width = book.shape[1]
    return pl.pallas_call(
        attention_finish_body,
        name="attention_finish",
        in_specs=[SMEM] + [VMEM] * 6,
        out_specs=[HBM] * 4 + [VMEM],
        out_shape=[shape_of((ch, ch), F32)] * 4 + [shape_of(book.shape, F32)],
        scratch_shapes=[
            pltpu.VMEM((DEAD, width + 128), F32),
            pltpu.VMEM((4 * owners, 4, rows, half), F32),
            pltpu.SemaphoreType.DMA(()),
        ],
        cost_estimate=took(3),
        compiler_params=pltpu.CompilerParams(vmem_limit_bytes=12 << 20),
    )(place, *pieces, slots, book)


def conv_finish_body(place_ref, mine, other, *refs, far):
    out_ref, buf, sem = refs[-3:]
    spread_all(place_ref, ((mine, 0, far), (other, 1, far)), buf, sem, out_ref, ())


def run_conv_finish(place, mine, other, into, ch, name):
    owners, total, half = mine.shape
    rows = ch // (2 * owners)
    given = [] if into is None else [into]
    return pl.pallas_call(
        functools.partial(conv_finish_body, far=len(given)),
        name=name,
        in_specs=[SMEM] + [VMEM] * 2 + [HBM] * len(given),
        out_specs=HBM,
        out_shape=shape_of((9, ch, ch), F32),
        scratch_shapes=[pltpu.VMEM((2 * owners, 9, rows, half), F32), pltpu.SemaphoreType.DMA(())],
        input_output_aliases={3: 0} if given else {},
        cost_estimate=took(3.5),
        compiler_params=pltpu.CompilerParams(vmem_limit_bytes=12 << 20),
    )(place, mine, other, *given)


def together(*values):
    return lax.optimization_barrier(values)


def vectors_body(sums_ref, *outs):
    *vectors, usage_ref, perplexity_ref = outs
    for i, out in enumerate(vectors):
        out[...] = sums_ref[i : i + 1, :]
    codes = usage_ref.shape[1]
    width = sums_ref.shape[1]
    first = len(vectors)
    counts = jnp.concatenate([sums_ref[first + i : first + i + 1, :] for i in range(codes // width)], axis=1)
    usage_ref[...] = counts.astype(jnp.int32)
    share = counts / jnp.sum(counts, axis=1, keepdims=True)
    entropy = jnp.sum(share * jnp.log(share + 1e-10), axis=1, keepdims=True)
    perplexity_ref[...] = jnp.exp(-entropy)


def run_vectors(sums, vectors, codes):
    ch = sums.shape[1]
    return pl.pallas_call(
        vectors_body,
        name="vectors",
        in_specs=[VMEM],
        out_specs=[VMEM] * (vectors + 2),
        cost_estimate=took(1.4),
        out_shape=[shape_of((1, ch), F32)] * vectors + [shape_of((1, codes), jnp.int32), shape_of((1, 1), F32)],
    )(sums)


class Links:
    def __init__(self, chips):
        self.chips = chips
        bits = chips.bit_length() - 1
        self.low = 1 if bits < 6 else 2
        sizes = [self.low - 1, self.low, bits - 2 * self.low]
        shifts = [1, self.low, 2 * self.low]
        self.dims = [(shift, size) for shift, size in zip(shifts, sizes) if size > 0]
        self.rest = bits - 1

    def swapped(self, index):
        mask = (1 << self.low) - 1
        first, second = index & mask, (index >> self.low) & mask
        return ((index >> (2 * self.low)) << (2 * self.low)) | (first << self.low) | second

    def flat(self, index):
        total = index & 1
        for shift, size in self.dims:
            total = (total << size) | ((index >> shift) & ((1 << size) - 1))
        return total

    def key(self, key, core):
        return self.swapped(key) if core else key

    def send(self, value, key):
        pairs = [(g * 2 + c, (g ^ self.key(key, c)) * 2 + c) for g in range(self.chips) for c in range(2)]
        return lax.ppermute(value, AXES, pairs)

    def partner(self, value):
        pairs = [(g * 2 + c, g * 2 + 1 - c) for g in range(self.chips) for c in range(2)]
        return lax.ppermute(value, AXES, pairs)

    def far(self, value):
        pairs = [(g * 2 + c, (g ^ self.key(1, 1 - c)) * 2 + 1 - c) for g in range(self.chips) for c in range(2)]
        return lax.ppermute(value, AXES, pairs)

    def reduce(self, value, dim, keep=None):
        shift, size = self.dims[dim]
        got = [self.send(value[k], k << shift) for k in range(1, 1 << size)]
        total = (value if keep is None else keep)[0].astype(F32)
        for g in got:
            total = total + g.astype(F32)
        return total.astype(BF)

    def gather(self, value, dim):
        shift, size = self.dims[dim]
        return jnp.stack([value] + [self.send(value, k << shift) for k in range(1, 1 << size)])

    def lead(self):
        return tuple(1 << size for _, size in self.dims)

    def small_steps(self):
        steps = [lambda value: value + self.partner(value)]
        for bit in range(self.chips.bit_length() - 1):
            steps.append(lambda value, key=1 << bit: value + self.send(value, key))
        return steps


def local(
    image_rows, grad_out, code_ids, dead_flags, replace_ids, latents, codebook,
    norm1_gain, norm1_bias, conv1_kernel, conv1_bias, norm2_gain, norm2_bias, conv2_kernel, conv2_bias,
    norm3_gain, norm3_bias, query_weight, query_bias, key_weight, value_weight, value_bias, out_weight, out_bias,
    *, chips,
):
    links = Links(chips)
    owners = chips
    all_images, part_rows, side, ch = image_rows.shape
    images = all_images // 2
    px = grad_out.shape[1] * side
    part = part_rows * side
    core = lax.axis_index("row").astype(jnp.int32)
    chip = lax.axis_index("grp").astype(jnp.int32)
    device = chip * 2 + core
    as_first, as_second = links.flat(chip), links.flat(links.swapped(chip))
    mine_at = jnp.where(core == 0, as_first, as_second)
    other_at = jnp.where(core == 0, as_second, as_first)
    low = owners // 2
    place = jnp.stack([
        core, chip, device * latents.shape[0], device, mine_at, other_at,
        mine_at // low, other_at // low, mine_at % low,
    ])
    mine = image_rows.reshape(all_images, part, ch)
    other = links.partner(lax.dynamic_slice_in_dim(mine, (1 - core) * images, images))
    vectors = [
        norm1_gain, norm1_bias, conv1_bias, norm2_gain, norm2_bias, conv2_bias,
        norm3_gain, norm3_bias, query_bias, value_bias, out_bias,
    ]
    codes = dead_flags.shape[0]
    counts, slots, ckeep, csend, vec, w1 = run_prepare(
        place, code_ids.reshape(1, -1), dead_flags.reshape(1, -1), replace_ids.reshape(1, -1), latents,
        conv1_kernel.reshape(9 * ch, ch), vectors, owners,
    )
    own, to_chip, to_near, to_far, norm2, scale2, x, gy, w2, *weights = run_entry(
        place, mine, other, vec, w1, grad_out.reshape(images, px, ch), conv2_kernel.reshape(9 * ch, ch),
        (query_weight, key_weight, value_weight, out_weight), side,
    )
    acts = [own, links.partner(to_chip), links.send(to_near, 1), links.far(to_far)]
    out, dres, dkeep2, dsend2, stat_a, gkeep, gsend = run_attention(
        place, x, own, to_near, gy, ckeep, csend, vec, [w2] + weights, side
    )
    dres, dkeep2, dsend2, gsend, *acts[1:] = together(dres, dkeep2, dsend2, gsend, *acts[1:])
    grads2 = [dkeep2, links.partner(dsend2), links.send(dkeep2, 1), links.far(dsend2)]
    attn = (gkeep.astype(F32) + links.partner(gsend).astype(F32)).astype(BF)
    attn = attn.reshape((2, low) + attn.shape[1:])
    attn_got = links.send(attn[1], 1)
    lead = links.lead()
    rest = range(1, len(lead))
    split = (lead[0], low // lead[0])

    def reduce(value, dims):
        for dim in dims:
            value = links.reduce(value, dim)
        return value

    def gather(value, dims):
        for dim in reversed(dims):
            value = links.gather(value, dim)
        return value

    def owned(value):
        return value.reshape((low,) + value.shape[-2:])

    sum2 = run_kernel_grad(place, run_turn(1, acts, side), grads2, split, side, 3, "conv2_grad")
    sum2_keep, dres = together(sum2, dres)
    dkeep1, dsend1, dfull1, stat_b = run_back2(place, dres, norm2, scale2, vec, w2, side)
    attn = (attn[0].astype(F32) + attn_got.astype(F32)).astype(BF)
    attn = attn.reshape(lead + attn.shape[1:])
    sum2 = sum2.reshape(lead + sum2.shape[2:])
    attn = reduce(attn, [0])
    sum2 = links.reduce(sum2, 0, sum2_keep.reshape(sum2.shape))
    grads1 = [dkeep1, links.partner(dsend1), links.send(dkeep1, 1), links.far(dsend1)]
    attn, sum2, stat_b, dfull1, grads1[0], *acts = together(attn, sum2, stat_b, dfull1, dkeep1, *acts)
    sum2 = reduce(jnp.concatenate([sum2, attn], axis=-2), rest)
    sum1 = run_kernel_grad(place, run_turn(0, acts, side), grads1, split, side, 0.1, "conv1_grad")
    rows_out, in_send, stat_c = run_back1(place, dfull1, x, dres, vec, w1, side)
    sum2, sum1, in_send, stat_c = together(sum2, sum1, in_send, stat_c)
    vectors = jnp.concatenate([stat_c[:2], stat_b[2:3], stat_b[:2], stat_a[:6], counts[:1].reshape(-1, ch)])
    steps = links.small_steps()
    sum2 = gather(sum2, rest)
    sum1 = sum1.reshape(lead + sum1.shape[2:])
    sum1 = reduce(sum1, [0])
    in_got = links.partner(in_send)
    vectors = steps[0](vectors)
    sum2, sum1, in_got, vectors = together(sum2, sum1, in_got, vectors)
    sum2 = owned(gather(sum2, [0]))
    sum1 = reduce(sum1, rest)
    vectors = steps[1](vectors)
    sum2, sum1, vectors = together(sum2, sum1, vectors)
    far2 = links.send(sum2, 1)
    other2 = links.partner(sum2)
    sum1 = gather(sum1, rest)
    vectors = steps[2](vectors)
    input_grad, _ = run_place_rows(place, in_got, rows_out)
    sum1, vectors, other2, input_grad = together(sum1, vectors, other2, input_grad)
    sum1 = owned(gather(sum1, [0]))
    vectors = steps[3](vectors)
    grad2 = run_conv_finish(place, sum2, other2, None, ch, "conv2_finish")
    sum1, far2, vectors, grad2 = together(sum1, far2, vectors, grad2)
    far1 = links.send(sum1, 1)
    other1 = links.partner(sum1)
    other_far2 = links.partner(far2)
    for step in steps[4:]:
        vectors = step(vectors)
    qg, kg, vg, og, new_codebook = run_attention_finish(
        place, (sum2, other2, far2, other_far2), slots, codebook, ch
    )
    grad2 = run_conv_finish(place, far2, other_far2, grad2, ch, "conv2_finish")
    grad1 = run_conv_finish(place, sum1, other1, None, ch, "conv1_finish")
    far1, grad2, grad1, vectors, new_codebook = together(far1, grad2, grad1, vectors, new_codebook)
    *vec_grads, usage, perplexity = run_vectors(vectors, 11, codes)
    (g1, b1, cb1, g2, b2, cb2, g3, b3, qb, vb, ob) = [v.reshape(ch) for v in vec_grads]
    grad1 = run_conv_finish(place, far1, links.partner(far1), grad1, ch, "conv1_finish")
    input_grad = input_grad.reshape(image_rows.shape)
    kernel_shape = (3, 3, ch, ch)
    return (
        out.reshape(grad_out.shape), input_grad,
        g1, b1, grad1.reshape(kernel_shape), cb1, g2, b2, grad2.reshape(kernel_shape), cb2, g3, b3,
        qg, qb, kg, vg, vb, og, ob,
        new_codebook, usage.reshape(codes), perplexity.reshape(()),
    )


def solution(mesh):
    both = ("grp", "row")
    in_specs = (
        P("grp", "row", None, None), P(both, None, None, None), P(both), P(), P(), P(both, None), P(both, None),
    ) + (P(),) * 17
    out_specs = (P(both, None, None, None), P("grp", "row", None, None)) + (P(),) * 17 + (P(both, None), P(), P())
    body = functools.partial(local, chips=mesh.shape["grp"])
    return jax.shard_map(body, mesh=mesh, in_specs=in_specs, out_specs=out_specs, check_vma=False)
```

```python
import functools

import jax
import jax.numpy as jnp
from jax import lax
from jax.experimental import pallas as pl
from jax.experimental.pallas import tpu as pltpu
from jax.sharding import PartitionSpec as P

EPS = 1e-06
GROUP = 16
LANES = 128
DEAD = 256
AXES = ("grp", "row")
F32 = jnp.float32
BF = jnp.bfloat16
NN = (((1,), (0,)), ((), ()))
NT = (((1,), (1,)), ((), ()))
TN = (((0,), (0,)), ((), ()))
VMEM = pl.BlockSpec(memory_space=pltpu.VMEM)
SMEM = pl.BlockSpec(memory_space=pltpu.SMEM)
HBM = pl.BlockSpec(memory_space=pltpu.HBM)
shape_of = jax.ShapeDtypeStruct


def took(us):
    return pl.CostEstimate(flops=int(us * 1.15e9), bytes_accessed=1 << 20, transcendentals=0)


def hbm(value):
    return pltpu.with_memory_space_constraint(value, pltpu.HBM)


def mm(a, b, dims=NN):
    return lax.dot_general(a, b, dims, preferred_element_type=F32)


def colsum(v):
    return jnp.sum(v, axis=0, keepdims=True)


def group_sums(rows):
    chunks = rows[0].shape[1] // LANES
    v = jnp.concatenate([r[:, c * LANES : (c + 1) * LANES] for r in rows for c in range(chunks)], axis=0)
    lane = lax.broadcasted_iota(jnp.int32, v.shape, 1)
    step = 1
    while step < GROUP:
        below = pltpu.roll(v, step, 1)
        above = pltpu.roll(v, LANES - step, 1)
        v = v + jnp.where((lane & step) != 0, below, above)
        step *= 2
    return [
        jnp.concatenate([v[k * chunks + c : k * chunks + c + 1] for c in range(chunks)], axis=1)
        for k in range(len(rows))
    ]


def normalized(images):
    count = images[0].shape[0] * GROUP
    middles = group_sums([colsum(v) for v in images])
    centered = [v - m / count for v, m in zip(images, middles)]
    spreads = group_sums([colsum(c * c) for c in centered])
    scales = [lax.rsqrt(v / count + EPS) for v in spreads]
    return [(c * r, r) for c, r in zip(centered, scales)]


def norm_back(images, gain):
    count = images[0][0].shape[0] * GROUP
    bias_grads = [colsum(dy) for _, _, dy in images]
    gain_grads = [colsum(dy * n) for n, _, dy in images]
    sums = group_sums([g * gain for g in bias_grads] + [g * gain for g in gain_grads])
    total = len(images)
    dxs = [
        r * (dy * gain - sums[i] / count - n * (sums[total + i] / count)) for i, (n, r, dy) in enumerate(images)
    ]
    return dxs, sum(gain_grads), sum(bias_grads)


def sigmoid(y):
    return 1.0 / (1.0 + jnp.exp(-y))


def shifted(v, side):
    px = v.shape[0]
    col = lax.broadcasted_iota(jnp.int32, v.shape, 0) % side
    left = jnp.where(col == 0, 0.0, pltpu.roll(v, 1, 0))
    right = jnp.where(col == side - 1, 0.0, pltpu.roll(v, px - 1, 0))
    return left, v, right


def put_shifts(s_ref, image, v, side):
    px, ch = v.shape
    for j, t in enumerate(shifted(v, side)):
        s_ref[image, side : px + side, j * ch : (j + 1) * ch] = t.astype(BF)


def clear_edges(s_ref, side):
    images, rows, width = s_ref.shape
    zero = jnp.zeros((side, width), BF)
    for i in range(images):
        s_ref[i, 0:side, :] = zero
        s_ref[i, rows - side : rows, :] = zero


def window(s_ref, first, px, cols):
    return jnp.concatenate([s_ref[i, first : first + px, cols] for i in range(s_ref.shape[0])], axis=0)


def conv(s_ref, w_ref, px, side, ch):
    acc = None
    for dh in range(3):
        part = mm(window(s_ref, dh * side, px, slice(None)), w_ref[dh * 3 * ch : (dh + 1) * 3 * ch, :])
        acc = part if acc is None else acc + part
    return acc


def conv_back(s_ref, w_ref, px, side, ch):
    acc = None
    for dh in range(3):
        for dw in range(3):
            tap = dh * 3 + dw
            cols = slice((2 - dw) * ch, (3 - dw) * ch)
            part = mm(window(s_ref, (2 - dh) * side, px, cols), w_ref[tap * ch : (tap + 1) * ch, :], NT)
            acc = part if acc is None else acc + part
    return acc


def split_cols(v, bit):
    half = v.shape[1] // 2
    low, high = v[:, :half], v[:, half:]
    return jnp.where(bit == 0, low, high), jnp.where(bit == 0, high, low)


def start_copies(pairs, sems):
    copies = [pltpu.make_async_copy(a, b, sems.at[i]) for i, (a, b) in enumerate(pairs)]
    for c in copies:
        c.start()
    return copies


def entry_body(
    place_ref, mine_hbm, other_ref, vec_ref, w1_hbm, gy_hbm, w2_hbm, wq_hbm, wk_hbm, wv_hbm, wo_hbm,
    own_ref, chip_ref, near_ref, far_ref, norm2_ref, scale2_ref, x_ref, gy_ref, w2, wq, wk, wv, wo, w1, s_ref, sems,
    *, side,
):
    images, px, ch = x_ref.shape
    part = px // 2
    core = place_ref[0]
    bit, other_bit = place_ref[6], place_ref[7]
    here = pl.multiple_of(core * part, part)
    there = pl.multiple_of((1 - core) * part, part)
    copies = start_copies(
        [(mine_hbm.at[core * images + i], x_ref.at[i, pl.ds(here, part)]) for i in range(images)]
        + [(w1_hbm, w1), (w2_hbm, w2), (gy_hbm, gy_ref), (wq_hbm, wq), (wk_hbm, wk), (wv_hbm, wv), (wo_hbm, wo)],
        sems,
    )

    def row(i):
        return vec_ref[i : i + 1, :]

    def give(which, a):
        for i in range(images):
            low = a[i].astype(BF)
            own_ref[which, i], near_ref[which, i] = split_cols(low, bit)
            chip_ref[which, i], far_ref[which, i] = split_cols(low, other_bit)

    clear_edges(s_ref, side)
    for i in range(images):
        x_ref[i, pl.ds(there, part), :] = other_ref[core * images + i]
    for c in copies[:images]:
        c.wait()
    active = []
    for i, (n, _) in enumerate(normalized([x_ref[i].astype(F32) for i in range(images)])):
        y = n * row(0) + row(1)
        active.append(y * sigmoid(y))
        put_shifts(s_ref, i, active[i], side)
    give(0, active)
    copies[images].wait()
    filtered = conv(s_ref, w1, px, side, ch) + row(2)
    active = []
    for i, (n, r) in enumerate(normalized([filtered[i * px : (i + 1) * px] for i in range(images)])):
        norm2_ref[i] = n
        scale2_ref[i : i + 1, :] = r
        y = n * row(3) + row(4)
        active.append(y * sigmoid(y))
    give(1, active)
    for c in copies[images + 1 :]:
        c.wait()


def run_entry(place, mine, other, vec, w1, gy, w2, weights, side):
    images, px, ch = gy.shape
    acts = shape_of((2, images, px, ch // 2), BF)
    whole = (images, px, ch)
    return pl.pallas_call(
        functools.partial(entry_body, side=side),
        name="entry",
        in_specs=[SMEM, HBM] + [VMEM] * 2 + [HBM] * 7,
        out_specs=[VMEM] * 13,
        out_shape=[acts] * 4
        + [shape_of(whole, F32), shape_of((images, ch), F32), shape_of(whole, BF), shape_of(whole, BF), shape_of(w2.shape, BF)]
        + [shape_of((ch, ch), BF)] * 4,
        scratch_shapes=[
            pltpu.VMEM(w1.shape, BF),
            pltpu.VMEM((images, px + 2 * side, 3 * ch), BF),
            pltpu.SemaphoreType.DMA((images + 7,)),
        ],
        cost_estimate=took(8.5),
        compiler_params=pltpu.CompilerParams(vmem_limit_bytes=16 << 20),
    )(place, hbm(mine), other, vec, *[hbm(v) for v in (w1, gy, w2, *weights)])


def attention_body(
    place_ref, x_ref, own_ref, near_ref, gy_ref, ckeep_ref, csend_ref, vec_ref, w2, wq, wk, wv, wo,
    out_ref, dres_ref, dkeep_ref, dsend_ref, stat_ref, gkeep_ref, gsend_ref,
    s_ref, norm_ref, normed, qkv, mixed, *, side,
):
    images, px, ch = x_ref.shape
    core = place_ref[0]
    bit = place_ref[6]

    def row(i):
        return vec_ref[i : i + 1, :]

    every = range(images)
    clear_edges(s_ref, side)
    for i in every:
        mine, other = own_ref[1, i], near_ref[1, i]
        a = jnp.concatenate([jnp.where(bit == 0, mine, other), jnp.where(bit == 0, other, mine)], axis=1)
        put_shifts(s_ref, i, a.astype(F32), side)

    def flat(ref):
        return ref[...].reshape(images * px, ch)

    def spans(v):
        return [v[i * px : (i + 1) * px] for i in every]

    dm = mm(flat(gy_ref), wo[...], NT).astype(BF)
    branch = conv(s_ref, w2, px, side, ch) + row(5)
    res = [x_ref[i].astype(F32) + b for i, b in zip(every, spans(branch))]
    scales = []
    for i, (n, r) in enumerate(normalized(res)):
        dres_ref[i] = res[i]
        norm_ref[i] = n
        scales.append(r)
        normed[i] = (n * row(6) + row(7)).astype(BF)
    nb = flat(normed)
    queries = (mm(nb, wq[...]) + row(8)).astype(BF)
    keys = mm(nb, wk[...]).astype(BF)
    values = (mm(nb, wv[...]) + row(9)).astype(BF)
    scale = ch ** -0.5
    q, k, v, d = spans(queries), spans(keys), spans(values), spans(dm)
    scores = [mm(q[i], k[i], NT) * scale for i in every]
    dp = [mm(d[i], v[i], NT) for i in every]
    lifted = [jnp.exp(t - jnp.max(t, axis=1, keepdims=True)) for t in scores]
    probs = [t / jnp.sum(t, axis=1, keepdims=True) for t in lifted]
    low = [t.astype(BF) for t in probs]
    ds = [(p * (t - jnp.sum(p * t, axis=1, keepdims=True))).astype(BF) for p, t in zip(probs, dp)]
    for i in every:
        mixed[i] = mm(low[i], v[i]).astype(BF)
        qkv[i, :, 2 * ch :] = mm(low[i], d[i], TN).astype(BF)
        qkv[i, :, :ch] = (mm(ds[i], k[i]) * scale).astype(BF)
        qkv[i, :, ch : 2 * ch] = (mm(ds[i], q[i], TN) * scale).astype(BF)
    cotangents = qkv[...].reshape(images * px, 3 * ch)
    dq, dk, dv = [cotangents[:, j * ch : (j + 1) * ch] for j in range(3)]
    dn = mm(dq, wq[...], NT) + mm(dk, wk[...], NT) + mm(dv, wv[...], NT)
    projected = mm(flat(mixed), wo[...]) + row(10)
    for i, p in zip(every, spans(projected)):
        out_ref[i] = (dres_ref[i] + p).astype(BF)
    dxs, gain_grad, bias_grad = norm_back(
        [(norm_ref[i], r, d) for i, r, d in zip(every, scales, spans(dn))], row(6)
    )
    total = jnp.zeros((1, ch), F32)
    for i, dx in zip(every, dxs):
        dres = gy_ref[i].astype(F32) + dx
        dres_ref[i] = dres
        db = dres.astype(BF)
        dkeep_ref[i], dsend_ref[i] = split_cols(db, core)
        total = total + colsum(db.astype(F32))
    stat_ref[...] = jnp.zeros(stat_ref.shape, F32)
    stat_ref[0:1, :] = total
    stat_ref[1:2, :] = gain_grad
    stat_ref[2:3, :] = bias_grad
    stat_ref[3:4, :] = colsum(dq.astype(F32))
    stat_ref[4:5, :] = colsum(dv.astype(F32))
    stat_ref[5:6, :] = colsum(flat(gy_ref).astype(F32))
    owners = gkeep_ref.shape[0]
    rows = ch // owners
    mine_at, other_at = place_ref[4], place_ref[5]
    whole = mm(flat(normed), cotangents, TN)
    grads = [whole[:, j * ch : (j + 1) * ch] for j in range(3)] + [mm(flat(mixed), flat(gy_ref), TN)]
    for j, g in enumerate(grads):
        keep, send = split_cols(g.astype(BF), core)
        for o in range(owners):
            gkeep_ref[o ^ mine_at, j * rows : (j + 1) * rows] = keep[o * rows : (o + 1) * rows]
            gsend_ref[o ^ other_at, j * rows : (j + 1) * rows] = send[o * rows : (o + 1) * rows]
    for o in range(owners):
        gkeep_ref[o, 4 * rows :] = ckeep_ref[o]
        gsend_ref[o, 4 * rows :] = csend_ref[o]


def run_attention(place, x, own, near, gy, ckeep, csend, vec, weights, side):
    images, px, ch = gy.shape
    half = ch // 2
    owners, count, _ = ckeep.shape
    rows = 4 * (ch // owners) + count
    whole = (images, px, ch)
    return pl.pallas_call(
        functools.partial(attention_body, side=side),
        name="attention",
        in_specs=[SMEM] + [VMEM] * 12,
        out_specs=[VMEM] * 7,
        out_shape=[
            shape_of(whole, BF), shape_of(whole, F32),
            shape_of((images, px, half), BF), shape_of((images, px, half), BF),
            shape_of((8, ch), F32),
            shape_of((owners, rows, half), BF), shape_of((owners, rows, half), BF),
        ],
        scratch_shapes=[pltpu.VMEM((images, px + 2 * side, 3 * ch), BF), pltpu.VMEM(whole, F32)]
        + [pltpu.VMEM(whole, BF), pltpu.VMEM((images, px, 3 * ch), BF), pltpu.VMEM(whole, BF)],
        cost_estimate=took(13.5),
        compiler_params=pltpu.CompilerParams(vmem_limit_bytes=20 << 20),
    )(place, x, own, near, gy, ckeep, csend, vec, *weights)


def swish_back(da, ns, gain, bias):
    dys = []
    for d, n in zip(da, ns):
        y = n * gain + bias
        sig = sigmoid(y)
        dys.append(d * (sig * (1.0 + y * (1.0 - sig))))
    return dys


def back2_body(
    place_ref, dres_ref, norm2_ref, scale2_ref, vec_ref, w2,
    dkeep_ref, dsend_ref, dfull_ref, stat_ref, s_ref, *, side,
):
    images, px, ch = dres_ref.shape
    every = range(images)
    core = place_ref[0]
    clear_edges(s_ref, side)

    def row(i):
        return vec_ref[i : i + 1, :]

    for i in every:
        put_shifts(s_ref, i, dres_ref[i], side)
    da = conv_back(s_ref, w2, px, side, ch)
    ns = [norm2_ref[i] for i in every]
    dys = swish_back([da[i * px : (i + 1) * px] for i in every], ns, row(3), row(4))
    dxs, gain_grad, bias_grad = norm_back(
        [(n, scale2_ref[i : i + 1, :], dy) for i, n, dy in zip(every, ns, dys)], row(3)
    )
    total = jnp.zeros((1, ch), F32)
    for i, dx in zip(every, dxs):
        db = dx.astype(BF)
        dfull_ref[i] = db
        dkeep_ref[i], dsend_ref[i] = split_cols(db, core)
        total = total + colsum(db.astype(F32))
    stat_ref[...] = jnp.zeros(stat_ref.shape, F32)
    stat_ref[0:1, :] = gain_grad
    stat_ref[1:2, :] = bias_grad
    stat_ref[2:3, :] = total


def run_back2(place, dres, norm2, scale2, vec, w2, side):
    images, px, ch = dres.shape
    half = (images, px, ch // 2)
    return pl.pallas_call(
        functools.partial(back2_body, side=side),
        name="conv2_back",
        in_specs=[SMEM] + [VMEM] * 5,
        out_specs=[VMEM] * 4,
        out_shape=[shape_of(half, BF), shape_of(half, BF), shape_of((images, px, ch), BF), shape_of((8, ch), F32)],
        scratch_shapes=[pltpu.VMEM((images, px + 2 * side, 3 * ch), BF)],
        cost_estimate=took(5),
        compiler_params=pltpu.CompilerParams(vmem_limit_bytes=12 << 20),
    )(place, dres, norm2, scale2, vec, w2)


def back1_body(
    place_ref, dfull_ref, x_ref, dres_ref, vec_ref, w1_hbm,
    out_hbm, send_ref, stat_ref, w1, s_ref, keep_ref, sem, *, side,
):
    images, px, ch = dres_ref.shape
    part = px // 2
    core = place_ref[0]
    every = range(images)
    fetch = pltpu.make_async_copy(w1_hbm, w1, sem)
    fetch.start()
    clear_edges(s_ref, side)

    def row(i):
        return vec_ref[i : i + 1, :]

    for i in every:
        put_shifts(s_ref, i, dfull_ref[i].astype(F32), side)
    fetch.wait()
    da = conv_back(s_ref, w1, px, side, ch)
    norms = normalized([x_ref[i].astype(F32) for i in every])
    ns = [n for n, _ in norms]
    dys = swish_back([da[i * px : (i + 1) * px] for i in every], ns, row(0), row(1))
    dxs, gain_grad, bias_grad = norm_back([(n, r, dy) for (n, r), dy in zip(norms, dys)], row(0))
    for i, dx in zip(every, dxs):
        total = (dres_ref[i] + dx).astype(BF)
        low, high = total[:part], total[part:]
        keep_ref[i] = jnp.where(core == 0, low, high)
        send_ref[i] = jnp.where(core == 0, high, low)
    stat_ref[...] = jnp.zeros(stat_ref.shape, F32)
    stat_ref[0:1, :] = gain_grad
    stat_ref[1:2, :] = bias_grad
    copy = pltpu.make_async_copy(keep_ref, out_hbm.at[pl.ds(core * images, images)], sem)
    copy.start()
    copy.wait()


def run_back1(place, dfull, x, dres, vec, w1, side):
    images, px, ch = dres.shape
    part = (images, px // 2, ch)
    return pl.pallas_call(
        functools.partial(back1_body, side=side),
        name="conv1_back",
        in_specs=[SMEM] + [VMEM] * 4 + [HBM],
        out_specs=[HBM, VMEM, VMEM],
        out_shape=[shape_of((2 * images, px // 2, ch), BF), shape_of(part, BF), shape_of((8, ch), F32)],
        scratch_shapes=[
            pltpu.VMEM(w1.shape, BF),
            pltpu.VMEM((images, px + 2 * side, 3 * ch), BF),
            pltpu.VMEM(part, BF),
            pltpu.SemaphoreType.DMA(()),
        ],
        cost_estimate=took(0.1),
        compiler_params=pltpu.CompilerParams(vmem_limit_bytes=16 << 20),
    )(place, dfull, x, dres, vec, hbm(w1))


def place_rows_body(place_ref, got_ref, into_hbm, out_hbm, token_ref, sem):
    images = got_ref.shape[0]
    token_ref[...] = jnp.zeros(token_ref.shape, F32)
    copy = pltpu.make_async_copy(got_ref, out_hbm.at[pl.ds((1 - place_ref[0]) * images, images)], sem)
    copy.start()
    copy.wait()


def run_place_rows(place, got, into):
    return pl.pallas_call(
        place_rows_body,
        name="place_rows",
        in_specs=[SMEM, VMEM, HBM],
        out_specs=[HBM, VMEM],
        out_shape=[shape_of(into.shape, BF), shape_of((8, 128), F32)],
        scratch_shapes=[pltpu.SemaphoreType.DMA(())],
        input_output_aliases={2: 0},
        cost_estimate=took(1),
        compiler_params=pltpu.CompilerParams(vmem_limit_bytes=4 << 20),
    )(place, got, into)


def turn(a, i, s_ref, at, side):
    px, part = a.shape[-2:]
    for j, t in enumerate(shifted(a[i].astype(F32), side)):
        s_ref[j * part : (j + 1) * part, pl.ds(pl.multiple_of(at * px, px), px)] = t.astype(BF).T


def turn_body(*refs, side, which):
    *acts, s_ref = refs
    images = acts[0].shape[1]
    for n, a in enumerate(acts):

        def fill(i, carry, a=a, n=n):
            turn(a.at[which], i, s_ref, n * images + i, side)
            return carry

        lax.fori_loop(0, images, fill, 0)


def run_turn(which, acts, side, us):
    _, images, px, part = acts[0].shape
    return pl.pallas_call(
        functools.partial(turn_body, side=side, which=which),
        name="turn",
        in_specs=[VMEM] * 4,
        out_specs=VMEM,
        out_shape=shape_of((3 * part, 4 * images * px), BF),
        cost_estimate=took(us),
        compiler_params=pltpu.CompilerParams(vmem_limit_bytes=6 << 20),
    )(*acts)


def kernel_grad_body(place_ref, s_ref, *refs, side, other):
    *grads, out_ref, d_ref = refs
    images, px, half = grads[0].shape
    part = s_ref.shape[0] // 3
    owners = out_ref.shape[0]
    rows = part // (2 * owners)
    mine = place_ref[8] // owners
    bits = place_ref[8] % owners
    block = (1 - mine) if other else mine
    zero = jnp.zeros((side, half), BF)
    for n, d in enumerate(grads):
        for i in range(images):
            d_ref[n * images + i, 0:side, :] = zero
            d_ref[n * images + i, side : px + side, :] = d[i]
            d_ref[n * images + i, px + side :, :] = zero
    some = part // 2
    lhs = jnp.concatenate(
        [s_ref[pl.ds(pl.multiple_of(dw * part + block * some, some), some), :] for dw in range(3)], axis=0
    )
    for dh in range(3):
        start = (2 - dh) * side
        d = jnp.concatenate([d_ref[n, start : start + px, :] for n in range(4 * images)], axis=0)
        g = mm(lhs, d).astype(BF)
        for o in range(owners):
            for dw in range(3):
                tap = dh * 3 + dw
                begin = dw * some + o * rows
                out_ref[o ^ bits, tap * rows : (tap + 1) * rows, :] = g[begin : begin + rows]


def run_kernel_grad(place, turned, grads, owners, side, other, us, name):
    images, px, half = grads[0].shape
    part = turned.shape[0] // 3
    return pl.pallas_call(
        functools.partial(kernel_grad_body, side=side, other=other),
        name=name,
        in_specs=[SMEM] + [VMEM] * 5,
        out_specs=VMEM,
        out_shape=shape_of((owners, 9 * (part // (2 * owners)), half), BF),
        scratch_shapes=[pltpu.VMEM((4 * images, px + 2 * side, half), BF)],
        cost_estimate=took(us),
        compiler_params=pltpu.CompilerParams(vmem_limit_bytes=10 << 20),
    )(place, turned, *grads)


def prepare_body(place_ref, ids_hbm, dead_hbm, replace_hbm, latents_hbm, *refs):
    count_vectors = (len(refs) - 10) // 2
    vectors = refs[:count_vectors]
    counts_ref, slots_ref, keep_ref, send_ref, vec_ref = refs[count_vectors : count_vectors + 5]
    lines = refs[count_vectors + 5 : 2 * count_vectors + 5]
    ids_ref, dead_ref, replace_ref, latents_ref, sems = refs[2 * count_vectors + 5 :]
    copies = start_copies(
        (
            (ids_hbm, ids_ref), (dead_hbm, dead_ref), (replace_hbm, replace_ref), (latents_hbm, latents_ref),
            *zip(vectors, lines),
        ),
        sems,
    )
    core = place_ref[0]
    offset = place_ref[2]
    for c in copies[:2]:
        c.wait()
    codes = dead_ref.shape[1]
    pixels, width = latents_ref.shape
    one = jnp.ones((), BF)
    none = jnp.zeros((), BF)
    code = lax.broadcasted_iota(jnp.int32, (codes, pixels), 0)
    hit = jnp.where(code == ids_ref[...], one, none)
    counts_ref[...] = mm(jnp.ones((8, pixels), BF), hit, NT)
    dead = dead_ref[...]
    ahead = lax.broadcasted_iota(jnp.int32, (codes, codes), 0) <= lax.broadcasted_iota(jnp.int32, (codes, codes), 1)
    rank = mm(jnp.broadcast_to(dead.astype(F32), (8, codes)).astype(BF), jnp.where(ahead, one, none))[0:1]
    rank = jnp.where(dead == 1, rank.astype(jnp.int32) - 1, -1)
    owners, count, _ = keep_ref.shape
    at = lax.broadcasted_iota(jnp.int32, (DEAD, codes), 0)
    beyond = at // (owners * count)
    owner = ((at % (owners * count)) // count) ^ jnp.where(beyond == 0, place_ref[4], place_ref[5])
    at = (beyond ^ core) * (owners * count) + owner * count + at % count
    slot = at == rank
    slots_ref[...] = jnp.where(slot, one, none)
    for c in copies[2:4]:
        c.wait()
    wanted = jnp.sum(jnp.where(slot, replace_ref[...], 0), axis=1, keepdims=True) - offset
    pixel = lax.broadcasted_iota(jnp.int32, (DEAD, pixels), 1)
    rows = mm(jnp.where(pixel == wanted, one, none), latents_ref[...]).astype(BF)
    for j in range(owners):
        keep_ref[j] = rows[j * count : (j + 1) * count]
        send_ref[j] = rows[DEAD // 2 + j * count : DEAD // 2 + (j + 1) * count]
    for c in copies[4:]:
        c.wait()
    for i, line in enumerate(lines):
        vec_ref[i : i + 1, :] = line[...].astype(F32).reshape(1, -1)


def run_prepare(place, ids, dead, replace, latents, vectors, owners):
    codes = dead.shape[1]
    pixels, width = latents.shape
    ch = vectors[0].shape[0]
    rows = shape_of((owners, DEAD // (2 * owners), width), BF)
    return pl.pallas_call(
        prepare_body,
        name="prepare",
        in_specs=[SMEM] + [HBM] * (4 + len(vectors)),
        out_specs=[VMEM] * 5,
        out_shape=[
            shape_of((8, codes), F32), shape_of((DEAD, codes), BF), rows, rows,
            shape_of((16, ch), F32),
        ],
        scratch_shapes=[pltpu.VMEM((ch,), BF)] * len(vectors)
        + [
            pltpu.VMEM((1, pixels), jnp.int32), pltpu.VMEM((1, codes), jnp.int32), pltpu.VMEM((1, codes), jnp.int32),
            pltpu.VMEM((pixels, width), BF), pltpu.SemaphoreType.DMA((4 + len(vectors),)),
        ],
        cost_estimate=took(2.2),
        compiler_params=pltpu.CompilerParams(vmem_limit_bytes=16 << 20),
    )(place, *[hbm(v) for v in (ids, dead, replace, latents, *vectors)])


def spread_all(place_ref, pieces, buf, sem, taps_out, outs, start=0):
    core = place_ref[0]
    ats = (place_ref[4], place_ref[5])
    copies = []
    step = 0
    for piece, beyond, first in pieces:
        owners = piece.shape[0]
        _, groups, rows, cols = buf.shape
        high = core ^ beyond
        for j in range(owners):
            buf[step] = piece[j, start : start + groups * rows, :].astype(F32).reshape(groups, rows, cols)
            at = pl.ds(pl.multiple_of(((j + first) ^ ats[beyond]) * rows, rows), rows)
            to = pl.ds(pl.multiple_of(high * cols, cols), cols)
            if taps_out is None:
                new = [pltpu.make_async_copy(buf.at[step, g], out.at[at, to], sem) for g, out in enumerate(outs)]
            else:
                new = [pltpu.make_async_copy(buf.at[step], taps_out.at[:, at, to], sem)]
            for c in new:
                c.start()
            copies += new
            step += 1
    for c in copies:
        c.wait()


def attention_finish_body(place_ref, mine0, other0, mine1, other1, slots_ref, book_ref, *refs):
    *outs, out_ref, rows_ref, buf, sem = refs
    device = place_ref[3]
    entries, width = book_ref.shape
    owners, total, _ = mine0.shape
    pieces = ((mine0, 0, 0), (other0, 1, 0), (mine1, 0, owners), (other1, 1, owners))
    count = DEAD // (4 * owners)
    start = total - count
    rows_ref[:, width:] = jnp.ones((DEAD, 128), F32)
    for n, piece in enumerate((mine0, mine1, other0, other1)):
        for j in range(owners):
            at = (n * owners + j) * count
            rows_ref[at : at + count, :width] = piece[j, start:, :].astype(F32)
    whole = mm(slots_ref[...], rows_ref[...].astype(BF), TN)
    codes = whole.shape[0]
    pick = lax.broadcasted_iota(jnp.int32, (entries, codes), 1) - device * entries
    pick = jnp.where(pick == lax.broadcasted_iota(jnp.int32, (entries, codes), 0), 1.0, 0.0).astype(BF)
    own = mm(pick, whole.astype(BF))
    out_ref[...] = jnp.where(own[:, width : width + 1] > 0.5, own[:, :width], book_ref[...])
    spread_all(place_ref, pieces, buf, sem, None, outs, start - buf.shape[1] * buf.shape[2])


def run_attention_finish(place, pieces, slots, book, ch):
    owners, total, half = pieces[0].shape
    rows = ch // (2 * owners)
    width = book.shape[1]
    return pl.pallas_call(
        attention_finish_body,
        name="attention_finish",
        in_specs=[SMEM] + [VMEM] * 6,
        out_specs=[HBM] * 4 + [VMEM],
        out_shape=[shape_of((ch, ch), F32)] * 4 + [shape_of(book.shape, F32)],
        scratch_shapes=[
            pltpu.VMEM((DEAD, width + 128), F32),
            pltpu.VMEM((4 * owners, 4, rows, half), F32),
            pltpu.SemaphoreType.DMA(()),
        ],
        cost_estimate=took(3),
        compiler_params=pltpu.CompilerParams(vmem_limit_bytes=12 << 20),
    )(place, *pieces, slots, book)


def conv_finish_body(place_ref, *refs, firsts):
    out_ref, buf, sem = refs[-3:]
    pieces = [(refs[n], n % 2, firsts[n // 2]) for n in range(2 * len(firsts))]
    spread_all(place_ref, pieces, buf, sem, out_ref, ())


def run_conv_finish(place, pieces, into, ch, total, name):
    arrays = [a for mine, other, _ in pieces for a in (mine, other)]
    rows = ch // total
    half = arrays[0].shape[2]
    given = [] if into is None else [into]
    return pl.pallas_call(
        functools.partial(conv_finish_body, firsts=[first for _, _, first in pieces]),
        name=name,
        in_specs=[SMEM] + [VMEM] * len(arrays) + [HBM] * len(given),
        out_specs=HBM,
        out_shape=shape_of((9, ch, ch), F32),
        scratch_shapes=[
            pltpu.VMEM((sum(a.shape[0] for a in arrays), 9, rows, half), F32), pltpu.SemaphoreType.DMA(()),
        ],
        input_output_aliases={1 + len(arrays): 0} if given else {},
        cost_estimate=took(3),
        compiler_params=pltpu.CompilerParams(vmem_limit_bytes=12 << 20),
    )(place, *arrays, *given)


def together(*values):
    return lax.optimization_barrier(values)


def vectors_body(sums_ref, *outs):
    *vectors, usage_ref, perplexity_ref = outs
    for i, out in enumerate(vectors):
        out[...] = sums_ref[i : i + 1, :]
    codes = usage_ref.shape[1]
    width = sums_ref.shape[1]
    first = len(vectors)
    counts = jnp.concatenate([sums_ref[first + i : first + i + 1, :] for i in range(codes // width)], axis=1)
    usage_ref[...] = counts.astype(jnp.int32)
    share = counts / jnp.sum(counts, axis=1, keepdims=True)
    entropy = jnp.sum(share * jnp.log(share + 1e-10), axis=1, keepdims=True)
    perplexity_ref[...] = jnp.exp(-entropy)


def run_vectors(sums, vectors, codes):
    ch = sums.shape[1]
    return pl.pallas_call(
        vectors_body,
        name="vectors",
        in_specs=[VMEM],
        out_specs=[VMEM] * (vectors + 2),
        cost_estimate=took(1.4),
        out_shape=[shape_of((1, ch), F32)] * vectors + [shape_of((1, codes), jnp.int32), shape_of((1, 1), F32)],
    )(sums)


class Links:
    def __init__(self, chips):
        self.chips = chips
        bits = chips.bit_length() - 1
        self.low = 1 if bits < 6 else 2
        sizes = [self.low - 1, self.low, bits - 2 * self.low]
        shifts = [1, self.low, 2 * self.low]
        self.dims = [(shift, size) for shift, size in zip(shifts, sizes) if size > 0]
        self.rest = bits - 1

    def swapped(self, index):
        mask = (1 << self.low) - 1
        first, second = index & mask, (index >> self.low) & mask
        return ((index >> (2 * self.low)) << (2 * self.low)) | (first << self.low) | second

    def flat(self, index):
        total = index & 1
        for shift, size in self.dims:
            total = (total << size) | ((index >> shift) & ((1 << size) - 1))
        return total

    def key(self, key, core):
        return self.swapped(key) if core else key

    def send(self, value, key):
        pairs = [(g * 2 + c, (g ^ self.key(key, c)) * 2 + c) for g in range(self.chips) for c in range(2)]
        return lax.ppermute(value, AXES, pairs)

    def partner(self, value):
        pairs = [(g * 2 + c, g * 2 + 1 - c) for g in range(self.chips) for c in range(2)]
        return lax.ppermute(value, AXES, pairs)

    def far(self, value):
        pairs = [(g * 2 + c, (g ^ self.key(1, 1 - c)) * 2 + 1 - c) for g in range(self.chips) for c in range(2)]
        return lax.ppermute(value, AXES, pairs)

    def reduce(self, value, dim):
        shift, size = self.dims[dim]
        got = [self.send(value[k], k << shift) for k in range(1, 1 << size)]
        total = value[0].astype(F32)
        for g in got:
            total = total + g.astype(F32)
        return total.astype(BF)

    def gather(self, value, dim):
        shift, size = self.dims[dim]
        return jnp.stack([value] + [self.send(value, k << shift) for k in range(1, 1 << size)])

    def lead(self):
        return tuple(1 << size for _, size in self.dims)

    def small_steps(self):
        steps = [lambda value: value + self.partner(value)]
        for bit in range(self.chips.bit_length() - 1):
            steps.append(lambda value, key=1 << bit: value + self.send(value, key))
        return steps


def local(
    image_rows, grad_out, code_ids, dead_flags, replace_ids, latents, codebook,
    norm1_gain, norm1_bias, conv1_kernel, conv1_bias, norm2_gain, norm2_bias, conv2_kernel, conv2_bias,
    norm3_gain, norm3_bias, query_weight, query_bias, key_weight, value_weight, value_bias, out_weight, out_bias,
    *, chips,
):
    links = Links(chips)
    owners = chips
    all_images, part_rows, side, ch = image_rows.shape
    images = all_images // 2
    px = grad_out.shape[1] * side
    part = part_rows * side
    core = lax.axis_index("row").astype(jnp.int32)
    chip = lax.axis_index("grp").astype(jnp.int32)
    device = chip * 2 + core
    as_first, as_second = links.flat(chip), links.flat(links.swapped(chip))
    mine_at = jnp.where(core == 0, as_first, as_second)
    other_at = jnp.where(core == 0, as_second, as_first)
    low = owners // 2
    place = jnp.stack([
        core, chip, device * latents.shape[0], device, mine_at, other_at,
        mine_at // low, other_at // low, mine_at % low,
    ])
    mine = image_rows.reshape(all_images, part, ch)
    other = links.partner(mine)
    vectors = [
        norm1_gain, norm1_bias, conv1_bias, norm2_gain, norm2_bias, conv2_bias,
        norm3_gain, norm3_bias, query_bias, value_bias, out_bias,
    ]
    codes = dead_flags.shape[0]
    counts, slots, ckeep, csend, vec = run_prepare(
        place, code_ids.reshape(1, -1), dead_flags.reshape(1, -1), replace_ids.reshape(1, -1), latents, vectors, owners
    )
    w1 = conv1_kernel.reshape(9 * ch, ch)
    own, to_chip, to_near, to_far, norm2, scale2, x, gy, w2, *weights = run_entry(
        place, mine, other, vec, w1, grad_out.reshape(images, px, ch), conv2_kernel.reshape(9 * ch, ch),
        (query_weight, key_weight, value_weight, out_weight), side,
    )
    acts = [own, links.partner(to_chip), links.send(to_near, 1), links.far(to_far)]
    out, dres, dkeep2, dsend2, stat_a, gkeep, gsend = run_attention(
        place, x, own, to_near, gy, ckeep, csend, vec, [w2] + weights, side
    )
    dres, dkeep2, dsend2, gsend, *acts[1:] = together(dres, dkeep2, dsend2, gsend, *acts[1:])
    grads2 = [dkeep2, links.partner(dsend2), links.send(dkeep2, 1), links.far(dsend2)]
    attn = (gkeep.astype(F32) + links.partner(gsend).astype(F32)).astype(BF)
    attn = attn.reshape((2, low) + attn.shape[1:])
    attn_got = links.send(attn[1], 1)
    lead = links.lead()
    rest = range(1, len(lead))

    def reduce(value, dims):
        for dim in dims:
            value = links.reduce(value, dim)
        return value

    def gather(value, dims):
        for dim in reversed(dims):
            value = links.gather(value, dim)
        return value

    def owned(value):
        return value.reshape((low,) + value.shape[-2:])

    turned = run_turn(1, acts, side, 2)
    give2 = run_kernel_grad(place, turned, grads2, low // 2, side, True, 1.6, "conv2_grad_other")
    give2, dres, turned = together(give2, dres, turned)
    keep2 = run_kernel_grad(place, turned, grads2, low // 2, side, False, 1.6, "conv2_grad")
    attn_got, keep2, dres = together(attn_got, keep2, dres)
    dkeep1, dsend1, dfull1, stat_b = run_back2(place, dres, norm2, scale2, vec, w2, side)
    attn = (attn[0].astype(F32) + attn_got.astype(F32)).astype(BF)
    attn = attn.reshape(lead + attn.shape[1:])
    attn = reduce(attn, [0])
    first = 1 << links.dims[0][0]

    def paired(keep, give):
        total = (keep.astype(F32) + links.send(give, first).astype(F32)).astype(BF)
        return total.reshape(lead[1:] + total.shape[1:])

    sum2 = paired(keep2, give2)
    grads1 = [dkeep1, links.partner(dsend1), links.send(dkeep1, 1), links.far(dsend1)]
    attn, sum2, stat_b, dfull1, grads1[0], *acts = together(attn, sum2, stat_b, dfull1, dkeep1, *acts)
    sum2 = reduce(jnp.concatenate([sum2, attn], axis=-2), rest)
    turned = run_turn(0, acts, side, 0.1)
    give1 = run_kernel_grad(place, turned, grads1, low // 2, side, True, 0.1, "conv1_grad_other")
    keep1 = run_kernel_grad(place, turned, grads1, low // 2, side, False, 0.1, "conv1_grad")
    rows_out, in_send, stat_c = run_back1(place, dfull1, x, dres, vec, w1, side)
    sum2, keep1, give1, in_send, stat_c = together(sum2, keep1, give1, in_send, stat_c)
    vectors = jnp.concatenate([stat_c[:2], stat_b[2:3], stat_b[:2], stat_a[:6], counts[:1].reshape(-1, ch)])
    steps = links.small_steps()
    sum2 = gather(sum2, rest)
    sum1 = paired(keep1, give1)
    sum1, in_send = together(sum1, in_send)
    in_got = links.partner(in_send)
    vectors = steps[0](vectors)
    sum2, sum1, in_got, vectors = together(sum2, sum1, in_got, vectors)
    sum2 = owned(gather(sum2, [0]))
    sum1 = reduce(sum1, rest)
    vectors = steps[1](vectors)
    sum2, sum1, vectors = together(sum2, sum1, vectors)
    far2 = links.send(sum2, 1)
    other2 = links.partner(sum2)
    sum1 = gather(sum1, rest)
    vectors = steps[2](vectors)
    input_grad, _ = run_place_rows(place, in_got, rows_out)
    sum1, vectors, other2, input_grad = together(sum1, vectors, other2, input_grad)
    shift, size = links.dims[0]
    each = low >> size
    parts1 = [sum1.reshape((-1,) + sum1.shape[-2:])]
    parts1 += [links.send(parts1[0], k << shift) for k in range(1, 1 << size)]
    for step in steps[3:]:
        vectors = step(vectors)
    grad2 = run_conv_finish(place, [(sum2, other2, 0)], None, ch, owners, "conv2_finish")
    *parts1, far2, vectors, grad2 = together(*parts1, far2, vectors, grad2)
    far1 = [links.send(p, 1) for p in parts1]
    other1 = [links.partner(p) for p in parts1]
    other_far2 = links.partner(far2)
    near1 = [(m, o, n * each) for n, (m, o) in enumerate(zip(parts1, other1))]
    grad1 = run_conv_finish(place, near1, None, ch, owners, "conv1_finish")
    qg, kg, vg, og, new_codebook = run_attention_finish(
        place, (sum2, other2, far2, other_far2), slots, codebook, ch
    )
    grad2 = run_conv_finish(place, [(far2, other_far2, low)], grad2, ch, owners, "conv2_finish")
    *far1, grad2, grad1, vectors, new_codebook = together(*far1, grad2, grad1, vectors, new_codebook)
    *vec_grads, usage, perplexity = run_vectors(vectors, 11, codes)
    (g1, b1, cb1, g2, b2, cb2, g3, b3, qb, vb, ob) = [v.reshape(ch) for v in vec_grads]
    far1 = [(p, links.partner(p), low + n * each) for n, p in enumerate(far1)]
    grad1 = run_conv_finish(place, far1, grad1, ch, owners, "conv1_finish")
    input_grad = input_grad.reshape(image_rows.shape)
    kernel_shape = (3, 3, ch, ch)
    return (
        out.reshape(grad_out.shape), input_grad,
        g1, b1, grad1.reshape(kernel_shape), cb1, g2, b2, grad2.reshape(kernel_shape), cb2, g3, b3,
        qg, qb, kg, vg, vb, og, ob,
        new_codebook, usage.reshape(codes), perplexity.reshape(()),
    )


def solution(mesh):
    both = ("grp", "row")
    in_specs = (
        P("grp", "row", None, None), P(both, None, None, None), P(both), P(), P(), P(both, None), P(both, None),
    ) + (P(),) * 17
    out_specs = (P(both, None, None, None), P("grp", "row", None, None)) + (P(),) * 17 + (P(both, None), P(), P())
    body = functools.partial(local, chips=mesh.shape["grp"])
    return jax.shard_map(body, mesh=mesh, in_specs=in_specs, out_specs=out_specs, check_vma=False)
```

```python
import functools

import jax
import jax.numpy as jnp
from jax import lax
from jax.experimental import pallas as pl
from jax.experimental.pallas import tpu as pltpu
from jax.sharding import PartitionSpec as P

EPS = 1e-06
GROUP = 16
LANES = 128
DEAD = 256
AXES = ("grp", "row")
F32 = jnp.float32
BF = jnp.bfloat16
NN = (((1,), (0,)), ((), ()))
NT = (((1,), (1,)), ((), ()))
TN = (((0,), (0,)), ((), ()))
VMEM = pl.BlockSpec(memory_space=pltpu.VMEM)
SMEM = pl.BlockSpec(memory_space=pltpu.SMEM)
HBM = pl.BlockSpec(memory_space=pltpu.HBM)
shape_of = jax.ShapeDtypeStruct


def took(us):
    return pl.CostEstimate(flops=int(us * 1.15e9), bytes_accessed=1 << 20, transcendentals=0)


def hbm(value):
    return pltpu.with_memory_space_constraint(value, pltpu.HBM)


def mm(a, b, dims=NN):
    return lax.dot_general(a, b, dims, preferred_element_type=F32)


def colsum(v):
    return jnp.sum(v, axis=0, keepdims=True)


def group_sums(rows):
    chunks = rows[0].shape[1] // LANES
    v = jnp.concatenate([r[:, c * LANES : (c + 1) * LANES] for r in rows for c in range(chunks)], axis=0)
    lane = lax.broadcasted_iota(jnp.int32, v.shape, 1)
    step = 1
    while step < GROUP:
        below = pltpu.roll(v, step, 1)
        above = pltpu.roll(v, LANES - step, 1)
        v = v + jnp.where((lane & step) != 0, below, above)
        step *= 2
    return [
        jnp.concatenate([v[k * chunks + c : k * chunks + c + 1] for c in range(chunks)], axis=1)
        for k in range(len(rows))
    ]


def normalized(images):
    count = images[0].shape[0] * GROUP
    middles = group_sums([colsum(v) for v in images])
    centered = [v - m / count for v, m in zip(images, middles)]
    spreads = group_sums([colsum(c * c) for c in centered])
    scales = [lax.rsqrt(v / count + EPS) for v in spreads]
    return [(c * r, r) for c, r in zip(centered, scales)]


def norm_back(images, gain):
    count = images[0][0].shape[0] * GROUP
    bias_grads = [colsum(dy) for _, _, dy in images]
    gain_grads = [colsum(dy * n) for n, _, dy in images]
    sums = group_sums([g * gain for g in bias_grads] + [g * gain for g in gain_grads])
    total = len(images)
    dxs = [
        r * (dy * gain - sums[i] / count - n * (sums[total + i] / count)) for i, (n, r, dy) in enumerate(images)
    ]
    return dxs, sum(gain_grads), sum(bias_grads)


def sigmoid(y):
    return 1.0 / (1.0 + jnp.exp(-y))


def shifted(v, side):
    px = v.shape[0]
    col = lax.broadcasted_iota(jnp.int32, v.shape, 0) % side
    left = jnp.where(col == 0, 0.0, pltpu.roll(v, 1, 0))
    right = jnp.where(col == side - 1, 0.0, pltpu.roll(v, px - 1, 0))
    return left, v, right


def put_shifts(s_ref, image, v, side):
    px, ch = v.shape
    for j, t in enumerate(shifted(v, side)):
        s_ref[image, side : px + side, j * ch : (j + 1) * ch] = t.astype(BF)


def clear_edges(s_ref, side):
    images, rows, width = s_ref.shape
    zero = jnp.zeros((side, width), BF)
    for i in range(images):
        s_ref[i, 0:side, :] = zero
        s_ref[i, rows - side : rows, :] = zero


def window(s_ref, first, px, cols):
    return jnp.concatenate([s_ref[i, first : first + px, cols] for i in range(s_ref.shape[0])], axis=0)


def conv(s_ref, w_ref, px, side, ch):
    acc = None
    for dh in range(3):
        part = mm(window(s_ref, dh * side, px, slice(None)), w_ref[dh * 3 * ch : (dh + 1) * 3 * ch, :])
        acc = part if acc is None else acc + part
    return acc


def conv_back(s_ref, w_ref, px, side, ch):
    acc = None
    for dh in range(3):
        for dw in range(3):
            tap = dh * 3 + dw
            cols = slice((2 - dw) * ch, (3 - dw) * ch)
            part = mm(window(s_ref, (2 - dh) * side, px, cols), w_ref[tap * ch : (tap + 1) * ch, :], NT)
            acc = part if acc is None else acc + part
    return acc


def split_cols(v, bit):
    half = v.shape[1] // 2
    low, high = v[:, :half], v[:, half:]
    return jnp.where(bit == 0, low, high), jnp.where(bit == 0, high, low)


def start_copies(pairs, sems):
    copies = [pltpu.make_async_copy(a, b, sems.at[i]) for i, (a, b) in enumerate(pairs)]
    for c in copies:
        c.start()
    return copies


def entry_body(
    place_ref, mine_hbm, other_ref, vec_ref, w1_hbm, gy_hbm, w2_hbm, wq_hbm, wk_hbm, wv_hbm, wo_hbm,
    own_ref, chip_ref, near_ref, far_ref, norm2_ref, scale2_ref, x_ref, gy_ref, w2, wq, wk, wv, wo, w1, s_ref, sems,
    *, side,
):
    images, px, ch = x_ref.shape
    part = px // 2
    core = place_ref[0]
    bit, other_bit = place_ref[6], place_ref[7]
    here = pl.multiple_of(core * part, part)
    there = pl.multiple_of((1 - core) * part, part)
    copies = start_copies(
        [(mine_hbm.at[core * images + i], x_ref.at[i, pl.ds(here, part)]) for i in range(images)]
        + [(w1_hbm, w1), (w2_hbm, w2), (gy_hbm, gy_ref), (wq_hbm, wq), (wk_hbm, wk), (wv_hbm, wv), (wo_hbm, wo)],
        sems,
    )

    def row(i):
        return vec_ref[i : i + 1, :]

    def give(which, a):
        for i in range(images):
            low = a[i].astype(BF)
            own_ref[which, i], near_ref[which, i] = split_cols(low, bit)
            chip_ref[which, i], far_ref[which, i] = split_cols(low, other_bit)

    clear_edges(s_ref, side)
    for i in range(images):
        x_ref[i, pl.ds(there, part), :] = other_ref[core * images + i]
    for c in copies[:images]:
        c.wait()
    active = []
    for i, (n, _) in enumerate(normalized([x_ref[i].astype(F32) for i in range(images)])):
        y = n * row(0) + row(1)
        active.append(y * sigmoid(y))
        put_shifts(s_ref, i, active[i], side)
    give(0, active)
    copies[images].wait()
    filtered = conv(s_ref, w1, px, side, ch) + row(2)
    active = []
    for i, (n, r) in enumerate(normalized([filtered[i * px : (i + 1) * px] for i in range(images)])):
        norm2_ref[i] = n
        scale2_ref[i : i + 1, :] = r
        y = n * row(3) + row(4)
        active.append(y * sigmoid(y))
    give(1, active)
    for c in copies[images + 1 :]:
        c.wait()


def run_entry(place, mine, other, vec, w1, gy, w2, weights, side):
    images, px, ch = gy.shape
    acts = shape_of((2, images, px, ch // 2), BF)
    whole = (images, px, ch)
    return pl.pallas_call(
        functools.partial(entry_body, side=side),
        name="entry",
        in_specs=[SMEM, HBM] + [VMEM] * 2 + [HBM] * 7,
        out_specs=[VMEM] * 13,
        out_shape=[acts] * 4
        + [shape_of(whole, F32), shape_of((images, ch), F32), shape_of(whole, BF), shape_of(whole, BF), shape_of(w2.shape, BF)]
        + [shape_of((ch, ch), BF)] * 4,
        scratch_shapes=[
            pltpu.VMEM(w1.shape, BF),
            pltpu.VMEM((images, px + 2 * side, 3 * ch), BF),
            pltpu.SemaphoreType.DMA((images + 7,)),
        ],
        cost_estimate=took(8.5),
        compiler_params=pltpu.CompilerParams(vmem_limit_bytes=16 << 20),
    )(place, hbm(mine), other, vec, *[hbm(v) for v in (w1, gy, w2, *weights)])


def attention_body(
    place_ref, x_ref, own_ref, near_ref, gy_ref, ckeep_ref, csend_ref, vec_ref, w2, wq, wk, wv, wo,
    out_ref, dres_ref, dkeep_ref, dsend_ref, stat_ref, gkeep_ref, gsend_ref,
    s_ref, norm_ref, normed, qkv, mixed, *, side,
):
    images, px, ch = x_ref.shape
    core = place_ref[0]
    bit = place_ref[6]

    def row(i):
        return vec_ref[i : i + 1, :]

    every = range(images)
    clear_edges(s_ref, side)
    for i in every:
        mine, other = own_ref[1, i], near_ref[1, i]
        a = jnp.concatenate([jnp.where(bit == 0, mine, other), jnp.where(bit == 0, other, mine)], axis=1)
        put_shifts(s_ref, i, a.astype(F32), side)

    def flat(ref):
        return ref[...].reshape(images * px, ch)

    def spans(v):
        return [v[i * px : (i + 1) * px] for i in every]

    dm = mm(flat(gy_ref), wo[...], NT).astype(BF)
    branch = conv(s_ref, w2, px, side, ch) + row(5)
    res = [x_ref[i].astype(F32) + b for i, b in zip(every, spans(branch))]
    scales = []
    for i, (n, r) in enumerate(normalized(res)):
        dres_ref[i] = res[i]
        norm_ref[i] = n
        scales.append(r)
        normed[i] = (n * row(6) + row(7)).astype(BF)
    nb = flat(normed)
    queries = (mm(nb, wq[...]) + row(8)).astype(BF)
    keys = mm(nb, wk[...]).astype(BF)
    values = (mm(nb, wv[...]) + row(9)).astype(BF)
    scale = ch ** -0.5
    q, k, v, d = spans(queries), spans(keys), spans(values), spans(dm)
    scores = [mm(q[i], k[i], NT) * scale for i in every]
    dp = [mm(d[i], v[i], NT) for i in every]
    lifted = [jnp.exp(t - jnp.max(t, axis=1, keepdims=True)) for t in scores]
    probs = [t / jnp.sum(t, axis=1, keepdims=True) for t in lifted]
    low = [t.astype(BF) for t in probs]
    ds = [(p * (t - jnp.sum(p * t, axis=1, keepdims=True))).astype(BF) for p, t in zip(probs, dp)]
    for i in every:
        mixed[i] = mm(low[i], v[i]).astype(BF)
        qkv[i, :, 2 * ch :] = mm(low[i], d[i], TN).astype(BF)
        qkv[i, :, :ch] = (mm(ds[i], k[i]) * scale).astype(BF)
        qkv[i, :, ch : 2 * ch] = (mm(ds[i], q[i], TN) * scale).astype(BF)
    cotangents = qkv[...].reshape(images * px, 3 * ch)
    dq, dk, dv = [cotangents[:, j * ch : (j + 1) * ch] for j in range(3)]
    dn = mm(dq, wq[...], NT) + mm(dk, wk[...], NT) + mm(dv, wv[...], NT)
    projected = mm(flat(mixed), wo[...]) + row(10)
    for i, p in zip(every, spans(projected)):
        out_ref[i] = (dres_ref[i] + p).astype(BF)
    dxs, gain_grad, bias_grad = norm_back(
        [(norm_ref[i], r, d) for i, r, d in zip(every, scales, spans(dn))], row(6)
    )
    total = jnp.zeros((1, ch), F32)
    for i, dx in zip(every, dxs):
        dres = gy_ref[i].astype(F32) + dx
        dres_ref[i] = dres
        db = dres.astype(BF)
        dkeep_ref[i], dsend_ref[i] = split_cols(db, core)
        total = total + colsum(db.astype(F32))
    stat_ref[...] = jnp.zeros(stat_ref.shape, F32)
    stat_ref[0:1, :] = total
    stat_ref[1:2, :] = gain_grad
    stat_ref[2:3, :] = bias_grad
    stat_ref[3:4, :] = colsum(dq.astype(F32))
    stat_ref[4:5, :] = colsum(dv.astype(F32))
    stat_ref[5:6, :] = colsum(flat(gy_ref).astype(F32))
    owners = gkeep_ref.shape[0]
    rows = ch // owners
    mine_at, other_at = place_ref[4], place_ref[5]
    whole = mm(flat(normed), cotangents, TN)
    grads = [whole[:, j * ch : (j + 1) * ch] for j in range(3)] + [mm(flat(mixed), flat(gy_ref), TN)]
    for j, g in enumerate(grads):
        keep, send = split_cols(g.astype(BF), core)
        for o in range(owners):
            gkeep_ref[o ^ mine_at, j * rows : (j + 1) * rows] = keep[o * rows : (o + 1) * rows]
            gsend_ref[o ^ other_at, j * rows : (j + 1) * rows] = send[o * rows : (o + 1) * rows]
    for o in range(owners):
        gkeep_ref[o, 4 * rows :] = ckeep_ref[o]
        gsend_ref[o, 4 * rows :] = csend_ref[o]


def run_attention(place, x, own, near, gy, ckeep, csend, vec, weights, side):
    images, px, ch = gy.shape
    half = ch // 2
    owners, count, _ = ckeep.shape
    rows = 4 * (ch // owners) + count
    whole = (images, px, ch)
    return pl.pallas_call(
        functools.partial(attention_body, side=side),
        name="attention",
        in_specs=[SMEM] + [VMEM] * 12,
        out_specs=[VMEM] * 7,
        out_shape=[
            shape_of(whole, BF), shape_of(whole, F32),
            shape_of((images, px, half), BF), shape_of((images, px, half), BF),
            shape_of((8, ch), F32),
            shape_of((owners, rows, half), BF), shape_of((owners, rows, half), BF),
        ],
        scratch_shapes=[pltpu.VMEM((images, px + 2 * side, 3 * ch), BF), pltpu.VMEM(whole, F32)]
        + [pltpu.VMEM(whole, BF), pltpu.VMEM((images, px, 3 * ch), BF), pltpu.VMEM(whole, BF)],
        cost_estimate=took(13.5),
        compiler_params=pltpu.CompilerParams(vmem_limit_bytes=20 << 20),
    )(place, x, own, near, gy, ckeep, csend, vec, *weights)


def swish_back(da, ns, gain, bias):
    dys = []
    for d, n in zip(da, ns):
        y = n * gain + bias
        sig = sigmoid(y)
        dys.append(d * (sig * (1.0 + y * (1.0 - sig))))
    return dys


def back2_body(
    place_ref, dres_ref, norm2_ref, scale2_ref, vec_ref, w2,
    dkeep_ref, dsend_ref, dfull_ref, stat_ref, s_ref, *, side,
):
    images, px, ch = dres_ref.shape
    every = range(images)
    core = place_ref[0]
    clear_edges(s_ref, side)

    def row(i):
        return vec_ref[i : i + 1, :]

    for i in every:
        put_shifts(s_ref, i, dres_ref[i], side)
    da = conv_back(s_ref, w2, px, side, ch)
    ns = [norm2_ref[i] for i in every]
    dys = swish_back([da[i * px : (i + 1) * px] for i in every], ns, row(3), row(4))
    dxs, gain_grad, bias_grad = norm_back(
        [(n, scale2_ref[i : i + 1, :], dy) for i, n, dy in zip(every, ns, dys)], row(3)
    )
    total = jnp.zeros((1, ch), F32)
    for i, dx in zip(every, dxs):
        db = dx.astype(BF)
        dfull_ref[i] = db
        dkeep_ref[i], dsend_ref[i] = split_cols(db, core)
        total = total + colsum(db.astype(F32))
    stat_ref[...] = jnp.zeros(stat_ref.shape, F32)
    stat_ref[0:1, :] = gain_grad
    stat_ref[1:2, :] = bias_grad
    stat_ref[2:3, :] = total


def run_back2(place, dres, norm2, scale2, vec, w2, side):
    images, px, ch = dres.shape
    half = (images, px, ch // 2)
    return pl.pallas_call(
        functools.partial(back2_body, side=side),
        name="conv2_back",
        in_specs=[SMEM] + [VMEM] * 5,
        out_specs=[VMEM] * 4,
        out_shape=[shape_of(half, BF), shape_of(half, BF), shape_of((images, px, ch), BF), shape_of((8, ch), F32)],
        scratch_shapes=[pltpu.VMEM((images, px + 2 * side, 3 * ch), BF)],
        cost_estimate=took(5),
        compiler_params=pltpu.CompilerParams(vmem_limit_bytes=12 << 20),
    )(place, dres, norm2, scale2, vec, w2)


def back1_body(
    place_ref, dfull_ref, x_ref, dres_ref, vec_ref, w1_hbm,
    out_hbm, send_ref, stat_ref, w1, s_ref, keep_ref, sem, *, side,
):
    images, px, ch = dres_ref.shape
    part = px // 2
    core = place_ref[0]
    every = range(images)
    fetch = pltpu.make_async_copy(w1_hbm, w1, sem)
    fetch.start()
    clear_edges(s_ref, side)

    def row(i):
        return vec_ref[i : i + 1, :]

    for i in every:
        put_shifts(s_ref, i, dfull_ref[i].astype(F32), side)
    fetch.wait()
    da = conv_back(s_ref, w1, px, side, ch)
    norms = normalized([x_ref[i].astype(F32) for i in every])
    ns = [n for n, _ in norms]
    dys = swish_back([da[i * px : (i + 1) * px] for i in every], ns, row(0), row(1))
    dxs, gain_grad, bias_grad = norm_back([(n, r, dy) for (n, r), dy in zip(norms, dys)], row(0))
    for i, dx in zip(every, dxs):
        total = (dres_ref[i] + dx).astype(BF)
        low, high = total[:part], total[part:]
        keep_ref[i] = jnp.where(core == 0, low, high)
        send_ref[i] = jnp.where(core == 0, high, low)
    stat_ref[...] = jnp.zeros(stat_ref.shape, F32)
    stat_ref[0:1, :] = gain_grad
    stat_ref[1:2, :] = bias_grad
    copy = pltpu.make_async_copy(keep_ref, out_hbm.at[pl.ds(core * images, images)], sem)
    copy.start()
    copy.wait()


def run_back1(place, dfull, x, dres, vec, w1, side):
    images, px, ch = dres.shape
    part = (images, px // 2, ch)
    return pl.pallas_call(
        functools.partial(back1_body, side=side),
        name="conv1_back",
        in_specs=[SMEM] + [VMEM] * 4 + [HBM],
        out_specs=[HBM, VMEM, VMEM],
        out_shape=[shape_of((2 * images, px // 2, ch), BF), shape_of(part, BF), shape_of((8, ch), F32)],
        scratch_shapes=[
            pltpu.VMEM(w1.shape, BF),
            pltpu.VMEM((images, px + 2 * side, 3 * ch), BF),
            pltpu.VMEM(part, BF),
            pltpu.SemaphoreType.DMA(()),
        ],
        cost_estimate=took(0.1),
        compiler_params=pltpu.CompilerParams(vmem_limit_bytes=16 << 20),
    )(place, dfull, x, dres, vec, hbm(w1))


def place_rows_body(place_ref, got_ref, into_hbm, out_hbm, token_ref, sem):
    images = got_ref.shape[0]
    token_ref[...] = jnp.zeros(token_ref.shape, F32)
    copy = pltpu.make_async_copy(got_ref, out_hbm.at[pl.ds((1 - place_ref[0]) * images, images)], sem)
    copy.start()
    copy.wait()


def run_place_rows(place, got, into):
    return pl.pallas_call(
        place_rows_body,
        name="place_rows",
        in_specs=[SMEM, VMEM, HBM],
        out_specs=[HBM, VMEM],
        out_shape=[shape_of(into.shape, BF), shape_of((8, 128), F32)],
        scratch_shapes=[pltpu.SemaphoreType.DMA(())],
        input_output_aliases={2: 0},
        cost_estimate=took(1),
        compiler_params=pltpu.CompilerParams(vmem_limit_bytes=4 << 20),
    )(place, got, into)


def turn(a, i, s_ref, at, side):
    px, part = a.shape[-2:]
    for j, t in enumerate(shifted(a[i].astype(F32), side)):
        s_ref[j * part : (j + 1) * part, pl.ds(pl.multiple_of(at * px, px), px)] = t.astype(BF).T


def turn_body(*refs, side, which):
    *acts, s_ref = refs
    images = acts[0].shape[1]
    for n, a in enumerate(acts):

        def fill(i, carry, a=a, n=n):
            turn(a.at[which], i, s_ref, n * images + i, side)
            return carry

        lax.fori_loop(0, images, fill, 0)


def run_turn(which, acts, side, us):
    _, images, px, part = acts[0].shape
    return pl.pallas_call(
        functools.partial(turn_body, side=side, which=which),
        name="turn",
        in_specs=[VMEM] * 4,
        out_specs=VMEM,
        out_shape=shape_of((3 * part, 4 * images * px), BF),
        cost_estimate=took(us),
        compiler_params=pltpu.CompilerParams(vmem_limit_bytes=6 << 20),
    )(*acts)


def kernel_grad_body(place_ref, s_ref, *refs, side, other):
    *grads, out_ref, d_ref = refs
    images, px, half = grads[0].shape
    part = s_ref.shape[0] // 3
    owners = out_ref.shape[0]
    rows = part // (2 * owners)
    mine = place_ref[8] // owners
    bits = place_ref[8] % owners
    block = (1 - mine) if other else mine
    zero = jnp.zeros((side, half), BF)
    for n, d in enumerate(grads):
        for i in range(images):
            d_ref[n * images + i, 0:side, :] = zero
            d_ref[n * images + i, side : px + side, :] = d[i]
            d_ref[n * images + i, px + side :, :] = zero
    some = part // 2
    lhs = jnp.concatenate(
        [s_ref[pl.ds(pl.multiple_of(dw * part + block * some, some), some), :] for dw in range(3)], axis=0
    )
    for dh in range(3):
        start = (2 - dh) * side
        d = jnp.concatenate([d_ref[n, start : start + px, :] for n in range(4 * images)], axis=0)
        g = mm(lhs, d).astype(BF)
        for o in range(owners):
            for dw in range(3):
                tap = dh * 3 + dw
                begin = dw * some + o * rows
                out_ref[o ^ bits, tap * rows : (tap + 1) * rows, :] = g[begin : begin + rows]


def run_kernel_grad(place, turned, grads, owners, side, other, us, name):
    images, px, half = grads[0].shape
    part = turned.shape[0] // 3
    return pl.pallas_call(
        functools.partial(kernel_grad_body, side=side, other=other),
        name=name,
        in_specs=[SMEM] + [VMEM] * 5,
        out_specs=VMEM,
        out_shape=shape_of((owners, 9 * (part // (2 * owners)), half), BF),
        scratch_shapes=[pltpu.VMEM((4 * images, px + 2 * side, half), BF)],
        cost_estimate=took(us),
        compiler_params=pltpu.CompilerParams(vmem_limit_bytes=10 << 20),
    )(place, turned, *grads)


def prepare_body(place_ref, ids_hbm, dead_hbm, replace_hbm, latents_hbm, *refs):
    count_vectors = (len(refs) - 10) // 2
    vectors = refs[:count_vectors]
    counts_ref, slots_ref, keep_ref, send_ref, vec_ref = refs[count_vectors : count_vectors + 5]
    lines = refs[count_vectors + 5 : 2 * count_vectors + 5]
    ids_ref, dead_ref, replace_ref, latents_ref, sems = refs[2 * count_vectors + 5 :]
    copies = start_copies(
        (
            (ids_hbm, ids_ref), (dead_hbm, dead_ref), (replace_hbm, replace_ref), (latents_hbm, latents_ref),
            *zip(vectors, lines),
        ),
        sems,
    )
    core = place_ref[0]
    offset = place_ref[2]
    for c in copies[:2]:
        c.wait()
    codes = dead_ref.shape[1]
    pixels, width = latents_ref.shape
    one = jnp.ones((), BF)
    none = jnp.zeros((), BF)
    code = lax.broadcasted_iota(jnp.int32, (codes, pixels), 0)
    hit = jnp.where(code == ids_ref[...], one, none)
    counts_ref[...] = mm(jnp.ones((8, pixels), BF), hit, NT)
    dead = dead_ref[...]
    ahead = lax.broadcasted_iota(jnp.int32, (codes, codes), 0) <= lax.broadcasted_iota(jnp.int32, (codes, codes), 1)
    rank = mm(jnp.broadcast_to(dead.astype(F32), (8, codes)).astype(BF), jnp.where(ahead, one, none))[0:1]
    rank = jnp.where(dead == 1, rank.astype(jnp.int32) - 1, -1)
    owners, count, _ = keep_ref.shape
    at = lax.broadcasted_iota(jnp.int32, (DEAD, codes), 0)
    beyond = at // (owners * count)
    owner = ((at % (owners * count)) // count) ^ jnp.where(beyond == 0, place_ref[4], place_ref[5])
    at = (beyond ^ core) * (owners * count) + owner * count + at % count
    slot = at == rank
    slots_ref[...] = jnp.where(slot, one, none)
    for c in copies[2:4]:
        c.wait()
    wanted = jnp.sum(jnp.where(slot, replace_ref[...], 0), axis=1, keepdims=True) - offset
    pixel = lax.broadcasted_iota(jnp.int32, (DEAD, pixels), 1)
    rows = mm(jnp.where(pixel == wanted, one, none), latents_ref[...]).astype(BF)
    for j in range(owners):
        keep_ref[j] = rows[j * count : (j + 1) * count]
        send_ref[j] = rows[DEAD // 2 + j * count : DEAD // 2 + (j + 1) * count]
    for c in copies[4:]:
        c.wait()
    for i, line in enumerate(lines):
        vec_ref[i : i + 1, :] = line[...].astype(F32).reshape(1, -1)


def run_prepare(place, ids, dead, replace, latents, vectors, owners):
    codes = dead.shape[1]
    pixels, width = latents.shape
    ch = vectors[0].shape[0]
    rows = shape_of((owners, DEAD // (2 * owners), width), BF)
    return pl.pallas_call(
        prepare_body,
        name="prepare",
        in_specs=[SMEM] + [HBM] * (4 + len(vectors)),
        out_specs=[VMEM] * 5,
        out_shape=[
            shape_of((8, codes), F32), shape_of((DEAD, codes), BF), rows, rows,
            shape_of((16, ch), F32),
        ],
        scratch_shapes=[pltpu.VMEM((ch,), BF)] * len(vectors)
        + [
            pltpu.VMEM((1, pixels), jnp.int32), pltpu.VMEM((1, codes), jnp.int32), pltpu.VMEM((1, codes), jnp.int32),
            pltpu.VMEM((pixels, width), BF), pltpu.SemaphoreType.DMA((4 + len(vectors),)),
        ],
        cost_estimate=took(2.2),
        compiler_params=pltpu.CompilerParams(vmem_limit_bytes=16 << 20),
    )(place, *[hbm(v) for v in (ids, dead, replace, latents, *vectors)])


def spread_all(place_ref, pieces, buf, sem, taps_out, outs, start=0):
    core = place_ref[0]
    ats = (place_ref[4], place_ref[5])
    copies = []
    step = 0
    for piece, beyond, first in pieces:
        owners = piece.shape[0]
        _, groups, rows, cols = buf.shape
        high = core ^ beyond
        for j in range(owners):
            buf[step] = piece[j, start : start + groups * rows, :].astype(F32).reshape(groups, rows, cols)
            at = pl.ds(pl.multiple_of(((j + first) ^ ats[beyond]) * rows, rows), rows)
            to = pl.ds(pl.multiple_of(high * cols, cols), cols)
            if taps_out is None:
                new = [pltpu.make_async_copy(buf.at[step, g], out.at[at, to], sem) for g, out in enumerate(outs)]
            else:
                new = [pltpu.make_async_copy(buf.at[step], taps_out.at[:, at, to], sem)]
            for c in new:
                c.start()
            copies += new
            step += 1
    for c in copies:
        c.wait()


def attention_finish_body(place_ref, mine0, other0, mine1, other1, slots_ref, book_ref, *refs):
    *outs, out_ref, rows_ref, buf, sem = refs
    device = place_ref[3]
    entries, width = book_ref.shape
    owners, total, _ = mine0.shape
    pieces = ((mine0, 0, 0), (other0, 1, 0), (mine1, 0, owners), (other1, 1, owners))
    count = DEAD // (4 * owners)
    start = total - count
    rows_ref[:, width:] = jnp.ones((DEAD, 128), F32)
    for n, piece in enumerate((mine0, mine1, other0, other1)):
        for j in range(owners):
            at = (n * owners + j) * count
            rows_ref[at : at + count, :width] = piece[j, start:, :].astype(F32)
    whole = mm(slots_ref[...], rows_ref[...].astype(BF), TN)
    codes = whole.shape[0]
    pick = lax.broadcasted_iota(jnp.int32, (entries, codes), 1) - device * entries
    pick = jnp.where(pick == lax.broadcasted_iota(jnp.int32, (entries, codes), 0), 1.0, 0.0).astype(BF)
    own = mm(pick, whole.astype(BF))
    out_ref[...] = jnp.where(own[:, width : width + 1] > 0.5, own[:, :width], book_ref[...])
    spread_all(place_ref, pieces, buf, sem, None, outs, start - buf.shape[1] * buf.shape[2])


def run_attention_finish(place, pieces, slots, book, ch):
    owners, total, half = pieces[0].shape
    rows = ch // (2 * owners)
    width = book.shape[1]
    return pl.pallas_call(
        attention_finish_body,
        name="attention_finish",
        in_specs=[SMEM] + [VMEM] * 6,
        out_specs=[HBM] * 4 + [VMEM],
        out_shape=[shape_of((ch, ch), F32)] * 4 + [shape_of(book.shape, F32)],
        scratch_shapes=[
            pltpu.VMEM((DEAD, width + 128), F32),
            pltpu.VMEM((4 * owners, 4, rows, half), F32),
            pltpu.SemaphoreType.DMA(()),
        ],
        cost_estimate=took(3),
        compiler_params=pltpu.CompilerParams(vmem_limit_bytes=12 << 20),
    )(place, *pieces, slots, book)


def conv_finish_body(place_ref, *refs, firsts):
    out_ref, buf, sem = refs[-3:]
    pieces = [(refs[n], n % 2, firsts[n // 2]) for n in range(2 * len(firsts))]
    spread_all(place_ref, pieces, buf, sem, out_ref, ())


def run_conv_finish(place, pieces, into, ch, total, name):
    arrays = [a for mine, other, _ in pieces for a in (mine, other)]
    rows = ch // total
    half = arrays[0].shape[2]
    given = [] if into is None else [into]
    return pl.pallas_call(
        functools.partial(conv_finish_body, firsts=[first for _, _, first in pieces]),
        name=name,
        in_specs=[SMEM] + [VMEM] * len(arrays) + [HBM] * len(given),
        out_specs=HBM,
        out_shape=shape_of((9, ch, ch), F32),
        scratch_shapes=[
            pltpu.VMEM((sum(a.shape[0] for a in arrays), 9, rows, half), F32), pltpu.SemaphoreType.DMA(()),
        ],
        input_output_aliases={1 + len(arrays): 0} if given else {},
        cost_estimate=took(3),
        compiler_params=pltpu.CompilerParams(vmem_limit_bytes=12 << 20),
    )(place, *arrays, *given)


def together(*values):
    return lax.optimization_barrier(values)


def vectors_body(sums_ref, *outs):
    *vectors, usage_ref, perplexity_ref = outs
    for i, out in enumerate(vectors):
        out[...] = sums_ref[i : i + 1, :]
    codes = usage_ref.shape[1]
    width = sums_ref.shape[1]
    first = len(vectors)
    counts = jnp.concatenate([sums_ref[first + i : first + i + 1, :] for i in range(codes // width)], axis=1)
    usage_ref[...] = counts.astype(jnp.int32)
    share = counts / jnp.sum(counts, axis=1, keepdims=True)
    entropy = jnp.sum(share * jnp.log(share + 1e-10), axis=1, keepdims=True)
    perplexity_ref[...] = jnp.exp(-entropy)


def run_vectors(sums, vectors, codes):
    ch = sums.shape[1]
    return pl.pallas_call(
        vectors_body,
        name="vectors",
        in_specs=[VMEM],
        out_specs=[VMEM] * (vectors + 2),
        cost_estimate=took(1.4),
        out_shape=[shape_of((1, ch), F32)] * vectors + [shape_of((1, codes), jnp.int32), shape_of((1, 1), F32)],
    )(sums)


class Links:
    def __init__(self, chips):
        self.chips = chips
        bits = chips.bit_length() - 1
        self.low = 1 if bits < 6 else 2
        sizes = [self.low - 1, self.low, bits - 2 * self.low]
        shifts = [1, self.low, 2 * self.low]
        self.dims = [(shift, size) for shift, size in zip(shifts, sizes) if size > 0]
        self.rest = bits - 1

    def swapped(self, index):
        mask = (1 << self.low) - 1
        first, second = index & mask, (index >> self.low) & mask
        return ((index >> (2 * self.low)) << (2 * self.low)) | (first << self.low) | second

    def flat(self, index):
        total = index & 1
        for shift, size in self.dims:
            total = (total << size) | ((index >> shift) & ((1 << size) - 1))
        return total

    def key(self, key, core):
        return self.swapped(key) if core else key

    def send(self, value, key):
        pairs = [(g * 2 + c, (g ^ self.key(key, c)) * 2 + c) for g in range(self.chips) for c in range(2)]
        return lax.ppermute(value, AXES, pairs)

    def partner(self, value):
        pairs = [(g * 2 + c, g * 2 + 1 - c) for g in range(self.chips) for c in range(2)]
        return lax.ppermute(value, AXES, pairs)

    def far(self, value):
        pairs = [(g * 2 + c, (g ^ self.key(1, 1 - c)) * 2 + 1 - c) for g in range(self.chips) for c in range(2)]
        return lax.ppermute(value, AXES, pairs)

    def reduce(self, value, dim):
        shift, size = self.dims[dim]
        got = [self.send(value[k], k << shift) for k in range(1, 1 << size)]
        total = value[0].astype(F32)
        for g in got:
            total = total + g.astype(F32)
        return total.astype(BF)

    def gather(self, value, dim):
        shift, size = self.dims[dim]
        return jnp.stack([value] + [self.send(value, k << shift) for k in range(1, 1 << size)])

    def lead(self):
        return tuple(1 << size for _, size in self.dims)

    def small_steps(self):
        steps = [lambda value: value + self.partner(value)]
        for bit in range(self.chips.bit_length() - 1):
            steps.append(lambda value, key=1 << bit: value + self.send(value, key))
        return steps


def local(
    image_rows, grad_out, code_ids, dead_flags, replace_ids, latents, codebook,
    norm1_gain, norm1_bias, conv1_kernel, conv1_bias, norm2_gain, norm2_bias, conv2_kernel, conv2_bias,
    norm3_gain, norm3_bias, query_weight, query_bias, key_weight, value_weight, value_bias, out_weight, out_bias,
    *, chips,
):
    links = Links(chips)
    owners = chips
    all_images, part_rows, side, ch = image_rows.shape
    images = all_images // 2
    px = grad_out.shape[1] * side
    part = part_rows * side
    core = lax.axis_index("row").astype(jnp.int32)
    chip = lax.axis_index("grp").astype(jnp.int32)
    device = chip * 2 + core
    as_first, as_second = links.flat(chip), links.flat(links.swapped(chip))
    mine_at = jnp.where(core == 0, as_first, as_second)
    other_at = jnp.where(core == 0, as_second, as_first)
    low = owners // 2
    place = jnp.stack([
        core, chip, device * latents.shape[0], device, mine_at, other_at,
        mine_at // low, other_at // low, mine_at % low,
    ])
    mine = image_rows.reshape(all_images, part, ch)
    other = links.partner(mine)
    vectors = [
        norm1_gain, norm1_bias, conv1_bias, norm2_gain, norm2_bias, conv2_bias,
        norm3_gain, norm3_bias, query_bias, value_bias, out_bias,
    ]
    codes = dead_flags.shape[0]
    counts, slots, ckeep, csend, vec = run_prepare(
        place, code_ids.reshape(1, -1), dead_flags.reshape(1, -1), replace_ids.reshape(1, -1), latents, vectors, owners
    )
    w1 = conv1_kernel.reshape(9 * ch, ch)
    own, to_chip, to_near, to_far, norm2, scale2, x, gy, w2, *weights = run_entry(
        place, mine, other, vec, w1, grad_out.reshape(images, px, ch), conv2_kernel.reshape(9 * ch, ch),
        (query_weight, key_weight, value_weight, out_weight), side,
    )
    acts = [own, links.partner(to_chip), links.send(to_near, 1), links.far(to_far)]
    out, dres, dkeep2, dsend2, stat_a, gkeep, gsend = run_attention(
        place, x, own, to_near, gy, ckeep, csend, vec, [w2] + weights, side
    )
    dres, dkeep2, dsend2, gsend, *acts[1:] = together(dres, dkeep2, dsend2, gsend, *acts[1:])
    grads2 = [dkeep2, links.partner(dsend2), links.send(dkeep2, 1), links.far(dsend2)]
    attn = (gkeep.astype(F32) + links.partner(gsend).astype(F32)).astype(BF)
    attn = attn.reshape((2, low) + attn.shape[1:])
    attn_got = links.send(attn[1], 1)
    lead = links.lead()
    rest = range(1, len(lead))

    def reduce(value, dims):
        for dim in dims:
            value = links.reduce(value, dim)
        return value

    def gather(value, dims):
        for dim in reversed(dims):
            value = links.gather(value, dim)
        return value

    def owned(value):
        return value.reshape((low,) + value.shape[-2:])

    turned = run_turn(1, acts, side, 2)
    give2 = run_kernel_grad(place, turned, grads2, low // 2, side, True, 1.6, "conv2_grad_other")
    give2, dres, turned = together(give2, dres, turned)
    keep2 = run_kernel_grad(place, turned, grads2, low // 2, side, False, 1.6, "conv2_grad")
    attn_got, keep2, dres = together(attn_got, keep2, dres)
    dkeep1, dsend1, dfull1, stat_b = run_back2(place, dres, norm2, scale2, vec, w2, side)
    attn = (attn[0].astype(F32) + attn_got.astype(F32)).astype(BF)
    attn = attn.reshape(lead + attn.shape[1:])
    attn = reduce(attn, [0])
    first = 1 << links.dims[0][0]

    def paired(keep, give):
        total = (keep.astype(F32) + links.send(give, first).astype(F32)).astype(BF)
        return total.reshape(lead[1:] + total.shape[1:])

    sum2 = paired(keep2, give2)
    grads1 = [dkeep1, links.partner(dsend1), links.send(dkeep1, 1), links.far(dsend1)]
    attn, sum2, stat_b, dfull1, grads1[0], *acts = together(attn, sum2, stat_b, dfull1, dkeep1, *acts)
    sum2 = reduce(jnp.concatenate([sum2, attn], axis=-2), rest)
    turned = run_turn(0, acts, side, 0.1)
    give1 = run_kernel_grad(place, turned, grads1, low // 2, side, True, 0.1, "conv1_grad_other")
    keep1 = run_kernel_grad(place, turned, grads1, low // 2, side, False, 0.1, "conv1_grad")
    rows_out, in_send, stat_c = run_back1(place, dfull1, x, dres, vec, w1, side)
    sum2, keep1, give1, in_send, stat_c = together(sum2, keep1, give1, in_send, stat_c)
    vectors = jnp.concatenate([stat_c[:2], stat_b[2:3], stat_b[:2], stat_a[:6], counts[:1].reshape(-1, ch)])
    steps = links.small_steps()
    sum2 = gather(sum2, rest)
    got1 = [links.send(give1[k], first) for k in range(give1.shape[0])]
    sum1 = jnp.stack([(keep1[k].astype(F32) + g.astype(F32)).astype(BF) for k, g in enumerate(got1)])
    sum1 = sum1.reshape(lead[1:] + sum1.shape[1:])
    sum1, in_send = together(sum1, in_send)
    in_got = links.partner(in_send)
    vectors = steps[0](vectors)
    sum2, sum1, in_got, vectors = together(sum2, sum1, in_got, vectors)
    sum2 = owned(gather(sum2, [0]))
    sum1 = reduce(sum1, rest)
    vectors = steps[1](vectors)
    sum2, sum1, vectors = together(sum2, sum1, vectors)
    far2 = links.send(sum2, 1)
    other2 = links.partner(sum2)
    sum1 = gather(sum1, rest)
    vectors = steps[2](vectors)
    input_grad, _ = run_place_rows(place, in_got, rows_out)
    sum1, vectors, other2, input_grad = together(sum1, vectors, other2, input_grad)
    shift, size = links.dims[0]
    each = low >> size
    parts1 = [sum1.reshape((-1,) + sum1.shape[-2:])]
    parts1 += [links.send(parts1[0], k << shift) for k in range(1, 1 << size)]
    for step in steps[3:]:
        vectors = step(vectors)
    grad2 = run_conv_finish(place, [(sum2, other2, 0)], None, ch, owners, "conv2_finish")
    *parts1, far2, vectors, grad2 = together(*parts1, far2, vectors, grad2)
    far1 = [links.send(p, 1) for p in parts1]
    other1 = [links.partner(p) for p in parts1]
    other_far2 = links.partner(far2)
    near1 = [(m, o, n * each) for n, (m, o) in enumerate(zip(parts1, other1))]
    grad1 = run_conv_finish(place, near1, None, ch, owners, "conv1_finish")
    qg, kg, vg, og, new_codebook = run_attention_finish(
        place, (sum2, other2, far2, other_far2), slots, codebook, ch
    )
    grad2 = run_conv_finish(place, [(far2, other_far2, low)], grad2, ch, owners, "conv2_finish")
    *far1, grad2, grad1, vectors, new_codebook = together(*far1, grad2, grad1, vectors, new_codebook)
    *vec_grads, usage, perplexity = run_vectors(vectors, 11, codes)
    (g1, b1, cb1, g2, b2, cb2, g3, b3, qb, vb, ob) = [v.reshape(ch) for v in vec_grads]
    far1 = [(p, links.partner(p), low + n * each) for n, p in enumerate(far1)]
    grad1 = run_conv_finish(place, far1, grad1, ch, owners, "conv1_finish")
    input_grad = input_grad.reshape(image_rows.shape)
    kernel_shape = (3, 3, ch, ch)
    return (
        out.reshape(grad_out.shape), input_grad,
        g1, b1, grad1.reshape(kernel_shape), cb1, g2, b2, grad2.reshape(kernel_shape), cb2, g3, b3,
        qg, qb, kg, vg, vb, og, ob,
        new_codebook, usage.reshape(codes), perplexity.reshape(()),
    )


def solution(mesh):
    both = ("grp", "row")
    in_specs = (
        P("grp", "row", None, None), P(both, None, None, None), P(both), P(), P(), P(both, None), P(both, None),
    ) + (P(),) * 17
    out_specs = (P(both, None, None, None), P("grp", "row", None, None)) + (P(),) * 17 + (P(both, None), P(), P())
    body = functools.partial(local, chips=mesh.shape["grp"])
    return jax.shard_map(body, mesh=mesh, in_specs=in_specs, out_specs=out_specs, check_vma=False)
```
